128 devices in a mesh: dom: 2 (over core), gx: 8 (over z, y_hi), yz: 8 (over y_lo, x).
Axes of the slice: x: 4, y: 4 (y_hi: 2, y_lo: 2; y = y_hi * 2 + y_lo), z: 4, core: 2. Of those that a mesh axis runs over, the one named last changes fastest.
Arguments:
- field_state: float32 [2, 8, 128, 128, 128], P('dom', None, 'gx', 'yz'), as said below
- shell_owner: int32 [8, 8, 8], P('gx'), may hold values from 0 to 7, as said below
- block_sources: int32 [8, 8, 4, 4], P('gx', 'yz'), may hold values from -1 to 15, as said below
- block_targets: int32 [8, 8, 4], P('gx', 'yz'), may hold values from -1 to 63, as said below
- interp_weights: bfloat16 [8, 8, 4, 4, 512, 512], P('gx', 'yz'), as said below
Outputs:
- new_state: float32 [2, 8, 128, 128, 128], P('dom', None, 'gx', 'yz')
The draws below stay inside these ranges and needn't reach their ends.
Inputs may be any that keep to these rules, and one draw needn't show every extreme that they name: `shell_owner`: entry [g, t, b] is the yz index of the heliosphere device, at the same gx index g, that owns shell block b of the corona device (g, t). No corona device gives more than 2 of its blocks to one owner, and in every gx index some owner receives exactly 2 blocks from each corona device of that gx index. `block_sources`: the live entries of device (g, y) come first in slot order and are the positions 0 to R - 1 of its owned list, each exactly once, R being the number of shell blocks it owns; the rest are -1. `block_targets`: live slots of one device name distinct local blocks; a slot is -1 exactly when all its sources are -1. `field_state`: each cell holds conserved variables of a state with positive density and pressure. `interp_weights`: for every target cell the entries over all 4 source blocks and their cells sum to less than one.
All inputs are finite; a program needn't handle non-finite values.
Results may differ from the reference program's by a relative error of at most 0.002.
Values may be sent and summed in bfloat16 or wider, within the bound.
A program may use at most 64 MiB of HBM per device.

```python
import jax
import jax.numpy as jnp
from jax import lax

NCOMP = 8
BLK = 8
LX = 16
LY = 16
LZ = 128
SR = 2
CAP = 2
K = 4
SB = 8
BC = 512
NBD = 4
NX = 128
NY = 128
NS = 512
N_GX = 8
N_YZ = 8


HEAT_RATIO = 5.0 / 3.0


def routing(key):
    base_key = jax.random.fold_in(key, 11)
    hot_key = jax.random.fold_in(base_key, 1)
    pick_key = jax.random.fold_in(base_key, 2)
    order_key = jax.random.fold_in(base_key, 3)
    rank_key = jax.random.fold_in(base_key, 4)
    place_key = jax.random.fold_in(base_key, 5)
    hot_owner = jax.random.randint(hot_key, (N_GX,), 0, N_YZ).astype(jnp.int32)
    pool_size = (N_YZ - 1) * CAP

    def sender_row(sender_index):
        hot_one = hot_owner[sender_index // N_YZ]
        owner_pool = (hot_one + 1 + jnp.arange(pool_size, dtype=jnp.int32) // CAP) % N_YZ
        chosen = jax.random.permutation(jax.random.fold_in(pick_key, sender_index), owner_pool)[:SB - CAP]
        entries = jnp.concatenate([jnp.full((CAP,), hot_one, jnp.int32), chosen.astype(jnp.int32)])
        return jax.random.permutation(jax.random.fold_in(order_key, sender_index), entries).astype(jnp.int32)
    owner_table = jax.vmap(sender_row)(jnp.arange(N_GX * N_YZ, dtype=jnp.int32)).reshape(N_GX, N_YZ, SB)
    slot_total = NBD * K
    block_total = LX // BLK * (LY // BLK) * (LZ // BLK)

    def receiver_row(device_index):
        column_owners = owner_table[device_index // N_YZ].reshape(-1)
        yz_index = device_index % N_YZ
        owned_count = jnp.sum((column_owners == yz_index).astype(jnp.int32))
        scores = jax.random.permutation(jax.random.fold_in(rank_key, device_index), slot_total).astype(jnp.int32)
        positions = jnp.arange(slot_total, dtype=jnp.int32)
        live_entry = positions < owned_count
        sort_order = jnp.argsort(jnp.where(live_entry, scores, slot_total + positions), stable=True).astype(jnp.int32)
        sources = jnp.where(live_entry, sort_order, -1).astype(jnp.int32).reshape(NBD, K)
        block_perm = jax.random.permutation(jax.random.fold_in(place_key, device_index), block_total)[:NBD].astype(jnp.int32)
        block_perm = jnp.where(block_perm == block_total - 1, block_perm[0], block_perm)
        block_perm = block_perm.at[0].set(block_total - 1)
        live_slot = jnp.arange(NBD, dtype=jnp.int32) * K < owned_count
        targets = jnp.where(live_slot, block_perm, -1).astype(jnp.int32)
        return (sources, targets)
    sources, targets = jax.vmap(receiver_row)(jnp.arange(N_GX * N_YZ, dtype=jnp.int32))
    return (owner_table, sources.reshape(N_GX, N_YZ, NBD, K), targets.reshape(N_GX, N_YZ, NBD))


def draw_shell_owner(key, part):
    return routing(key)[0]


def draw_block_sources(key, part):
    return routing(key)[1]


def draw_block_targets(key, part):
    return routing(key)[2]


def draw_interp_weights(key, part):
    perm_key = jax.random.fold_in(key, 31)
    share_key = jax.random.fold_in(key, 32)
    rest_key = jax.random.fold_in(key, 33)
    share_low = 0.5
    share_high = 1.5
    share_unit = 0.13
    rest_total = 0.17
    block_count = N_GX * N_YZ * NBD * K

    def one_block(block_index):
        target_source = jax.random.permutation(jax.random.fold_in(perm_key, block_index), BC).astype(jnp.int32)
        share = jax.random.uniform(jax.random.fold_in(share_key, block_index), (BC,), jnp.float32, share_low, share_high) * share_unit
        spread = jax.random.uniform(jax.random.fold_in(rest_key, block_index), (BC, BC), jnp.float32, 0.0, 2.0 * rest_total / (K * BC))
        source_spots = jnp.arange(BC, dtype=jnp.int32)
        leading = jnp.where(source_spots[:, None] == target_source[None, :], share[None, :], 0.0)
        return (spread + leading).astype(jnp.bfloat16)
    blocks = lax.map(one_block, jnp.arange(block_count, dtype=jnp.int32))
    return blocks.reshape(N_GX, N_YZ, NBD, K, BC, BC)


def draw_field_state(key, part):
    grid_shape = (2, NX, NY, LZ)
    density_key = jax.random.fold_in(key, 21)
    velocity_key = jax.random.fold_in(key, 22)
    magnetic_key = jax.random.fold_in(key, 23)
    pressure_key = jax.random.fold_in(key, 24)
    density = jnp.exp(jax.random.uniform(density_key, grid_shape, jnp.float32, jnp.log(0.5), jnp.log(2.0)))
    velocity = jax.random.uniform(velocity_key, (3,) + grid_shape, jnp.float32, -1.0, 1.0)
    magnetic = jax.random.uniform(magnetic_key, (3,) + grid_shape, jnp.float32, -1.0, 1.0)
    pressure = jnp.exp(jax.random.uniform(pressure_key, grid_shape, jnp.float32, jnp.log(0.5), jnp.log(2.0)))
    energy = pressure / (HEAT_RATIO - 1.0) + 0.5 * density * jnp.sum(velocity * velocity, axis=0)
    energy = energy + 0.5 * jnp.sum(magnetic * magnetic, axis=0)
    parts_list = [density, density * velocity[0], density * velocity[1], density * velocity[2], magnetic[0], magnetic[1], magnetic[2], energy]
    return jnp.stack(parts_list, axis=1).astype(jnp.float32)


def setup_inputs(seed: int = 0) -> dict:
    streams_of = jax.random.split(jax.random.key(seed), 6)
    field_state = draw_field_state(jax.random.fold_in(streams_of[5], 71), 0)
    shell_owner = draw_shell_owner(jax.random.fold_in(streams_of[5], 71), 0)
    block_sources = draw_block_sources(jax.random.fold_in(streams_of[5], 71), 0)
    block_targets = draw_block_targets(jax.random.fold_in(streams_of[5], 71), 0)
    interp_weights = draw_interp_weights(jax.random.fold_in(streams_of[5], 71), 0)
    return dict(field_state=field_state, shell_owner=shell_owner, block_sources=block_sources, block_targets=block_targets, interp_weights=interp_weights)


HEAT_RATIO = 5.0 / 3.0
CORONA_RATIO = 0.04
HELIO_RATIO = 0.03

def direction_flux(grid_cells, direction):
    density = grid_cells[0]
    momentum = grid_cells[1:4]
    magnetic = grid_cells[4:7]
    energy = grid_cells[7]
    velocity = momentum / density
    field_sq = lax.optimization_barrier(jnp.sum(magnetic * magnetic, axis=0))
    pressure = (HEAT_RATIO - 1.0) * (energy - 0.5 * lax.optimization_barrier(jnp.sum(momentum * velocity, axis=0)) - 0.5 * field_sq)
    total_pressure = pressure + 0.5 * field_sq
    normal_speed = velocity[direction]
    normal_field = magnetic[direction]
    velocity_dot = lax.optimization_barrier(jnp.sum(velocity * magnetic, axis=0))
    flux_list = [momentum[direction]]
    for other in range(3):
        term = momentum[other] * normal_speed - magnetic[other] * normal_field
        if other == direction:
            term = term + total_pressure
        flux_list.append(term)
    for other in range(3):
        flux_list.append(normal_speed * magnetic[other] - normal_field * velocity[other])
    flux_list.append((energy + total_pressure) * normal_speed - normal_field * velocity_dot)
    wave_speed = jnp.abs(normal_speed) + jnp.sqrt((HEAT_RATIO * pressure + field_sq) / density)
    return (jnp.stack(flux_list), wave_speed)

def interface_change(padded_line, direction):
    phys_flux, wave_speed = direction_flux(padded_line, direction)
    array_dim = direction + 1
    cell_count = padded_line.shape[array_dim]
    low_cells = lax.slice_in_dim(padded_line, 0, cell_count - 1, axis=array_dim)
    high_cells = lax.slice_in_dim(padded_line, 1, cell_count, axis=array_dim)
    low_flux = lax.slice_in_dim(phys_flux, 0, cell_count - 1, axis=array_dim)
    high_flux = lax.slice_in_dim(phys_flux, 1, cell_count, axis=array_dim)
    low_speed = lax.slice_in_dim(wave_speed, 0, cell_count - 1, axis=direction)
    high_speed = lax.slice_in_dim(wave_speed, 1, cell_count, axis=direction)
    fastest = jnp.maximum(low_speed, high_speed)
    face_flux = 0.5 * (low_flux + high_flux) - 0.5 * fastest[None] * (high_cells - low_cells)
    upper_face = lax.slice_in_dim(face_flux, 1, cell_count - 1, axis=array_dim)
    lower_face = lax.slice_in_dim(face_flux, 0, cell_count - 2, axis=array_dim)
    return upper_face - lower_face

def advance(line_set, inner_cells, step_ratio):
    change = interface_change(line_set[0], 0) + interface_change(line_set[1], 1)
    change = change + interface_change(line_set[2], 2)
    return inner_cells - step_ratio * change

def evolve(domain_grid, wrap_x, step_ratio):
    if wrap_x:
        padded = jnp.pad(domain_grid, ((0, 0), (1, 1), (0, 0), (0, 0)), mode='wrap')
    else:
        padded = jnp.pad(domain_grid, ((0, 0), (1, 1), (0, 0), (0, 0)), mode='edge')
    padded = jnp.pad(padded, ((0, 0), (0, 0), (1, 1), (1, 1)), mode='edge')

    def slab_update(slab_index):
        slab_cells = lax.dynamic_slice_in_dim(padded, slab_index * LX, LX + 2, 1)
        line_set = (slab_cells[:, :, 1:-1, 1:-1], slab_cells[:, 1:-1, :, 1:-1], slab_cells[:, 1:-1, 1:-1, :])
        return advance(line_set, slab_cells[:, 1:-1, 1:-1, 1:-1], step_ratio)
    slab_stack = lax.map(slab_update, jnp.arange(N_GX, dtype=jnp.int32))
    return jnp.transpose(slab_stack, (1, 0, 2, 3, 4)).reshape(NCOMP, NX, NY, LZ)

def reference(field_state, shell_owner, block_sources, block_targets, interp_weights):
    corona = field_state[0]
    helio_grid = field_state[1]
    per_x = LX // BLK
    per_y = LY // BLK
    per_z = LZ // BLK
    shell_cells = corona[:, :, :, LZ - SR * BLK:]
    shell_cells = shell_cells.reshape(NCOMP, N_GX, per_x, BLK, N_YZ, per_y, BLK, SR, BLK)
    shell_cells = shell_cells.transpose(1, 4, 2, 5, 7, 0, 3, 6, 8).reshape(NS, NCOMP, BC).astype(jnp.bfloat16)

    def owned_list(device_index):
        column_owners = shell_owner[device_index // N_YZ].reshape(-1)
        yz_index = device_index % N_YZ
        all_spots = jnp.arange(N_YZ * SB, dtype=jnp.int32)
        sort_keys = jnp.where(column_owners == yz_index, all_spots, N_YZ * SB + all_spots)
        sort_order = jnp.argsort(sort_keys, stable=True).astype(jnp.int32)
        return device_index // N_YZ * (N_YZ * SB) + sort_order
    owned_ids = jax.vmap(owned_list)(jnp.arange(N_GX * N_YZ, dtype=jnp.int32))
    raw_sources = block_sources.reshape(N_GX * N_YZ, NBD * K)
    global_ids = jnp.take_along_axis(owned_ids, jnp.maximum(raw_sources, 0), axis=1)
    global_ids = jnp.where(raw_sources >= 0, global_ids, -1).reshape(-1, K)
    flat_weights = interp_weights.reshape(-1, K, BC, BC)

    def one_slot(slot_item):
        slot_sources, slot_weights = slot_item
        picked = shell_cells[jnp.maximum(slot_sources, 0)]
        picked = jnp.where((slot_sources >= 0)[:, None, None], picked, jnp.zeros_like(picked))
        return jnp.einsum('kcs,kst->ct', picked.astype(jnp.float32), slot_weights.astype(jnp.float32), precision=lax.Precision.HIGHEST)
    boundary_blocks = lax.map(one_slot, (global_ids, flat_weights))
    slot_index = jnp.arange(N_GX * N_YZ * NBD, dtype=jnp.int32)
    device_index = slot_index // NBD
    target_block = block_targets.reshape(-1).astype(jnp.int32)
    block_spot = jnp.maximum(target_block, 0)
    base_x = device_index // N_YZ * LX + block_spot // (per_y * per_z) * BLK
    base_y = device_index % N_YZ * LY + block_spot // per_z % per_y * BLK
    base_z = block_spot % per_z * BLK
    offsets = jnp.arange(BC, dtype=jnp.int32)
    cell_x = base_x[:, None] + offsets[None, :] // (BLK * BLK)
    cell_y = base_y[:, None] + offsets[None, :] // BLK % BLK
    cell_z = base_z[:, None] + offsets[None, :] % BLK
    cell_x = jnp.where(target_block[:, None] >= 0, cell_x, NX)
    helio_grid = helio_grid.at[:, cell_x, cell_y, cell_z].set(jnp.transpose(boundary_blocks, (1, 0, 2)), mode='drop')
    new_corona = evolve(corona, True, CORONA_RATIO)
    new_helio = evolve(helio_grid, False, HELIO_RATIO)
    return jnp.stack([new_corona, new_helio])
```

```python
import jax
import jax.numpy as jnp
from jax import lax
from jax.sharding import PartitionSpec as P

BLK = 8
SR = 2
CAP = 2


HEAT_RATIO = 5.0 / 3.0
CORONA_RATIO = 0.04
HELIO_RATIO = 0.03


def direction_flux(grid_cells, direction):
    density = grid_cells[0]
    momentum = grid_cells[1:4]
    magnetic = grid_cells[4:7]
    energy = grid_cells[7]
    velocity = momentum / density
    field_sq = jnp.sum(magnetic * magnetic, axis=0)
    pressure = (HEAT_RATIO - 1.0) * (
        energy - 0.5 * jnp.sum(momentum * velocity, axis=0) - 0.5 * field_sq
    )
    total_pressure = pressure + 0.5 * field_sq
    normal_speed = velocity[direction]
    normal_field = magnetic[direction]
    velocity_dot = jnp.sum(velocity * magnetic, axis=0)
    flux_list = [momentum[direction]]
    for other in range(3):
        term = momentum[other] * normal_speed - magnetic[other] * normal_field
        if other == direction:
            term = term + total_pressure
        flux_list.append(term)
    for other in range(3):
        flux_list.append(normal_speed * magnetic[other] - normal_field * velocity[other])
    flux_list.append((energy + total_pressure) * normal_speed - normal_field * velocity_dot)
    wave_speed = jnp.abs(normal_speed) + jnp.sqrt((HEAT_RATIO * pressure + field_sq) / density)
    return (jnp.stack(flux_list), wave_speed)


def interface_change(padded_line, direction):
    phys_flux, wave_speed = direction_flux(padded_line, direction)
    array_dim = direction + 1
    cell_count = padded_line.shape[array_dim]
    low_cells = lax.slice_in_dim(padded_line, 0, cell_count - 1, axis=array_dim)
    high_cells = lax.slice_in_dim(padded_line, 1, cell_count, axis=array_dim)
    low_flux = lax.slice_in_dim(phys_flux, 0, cell_count - 1, axis=array_dim)
    high_flux = lax.slice_in_dim(phys_flux, 1, cell_count, axis=array_dim)
    low_speed = lax.slice_in_dim(wave_speed, 0, cell_count - 1, axis=direction)
    high_speed = lax.slice_in_dim(wave_speed, 1, cell_count, axis=direction)
    fastest = jnp.maximum(low_speed, high_speed)
    face_flux = 0.5 * (low_flux + high_flux) - 0.5 * fastest[None] * (high_cells - low_cells)
    upper_face = lax.slice_in_dim(face_flux, 1, cell_count - 1, axis=array_dim)
    lower_face = lax.slice_in_dim(face_flux, 0, cell_count - 2, axis=array_dim)
    return upper_face - lower_face


def advance(line_set, inner_cells, step_ratio):
    change = interface_change(line_set[0], 0) + interface_change(line_set[1], 1)
    change = change + interface_change(line_set[2], 2)
    return inner_cells - step_ratio * change


def ghost_pair(cells, axis, dim, wrap, fix_low, fix_high):
    count = lax.axis_size(axis)
    size = cells.shape[dim]
    head = lax.slice_in_dim(cells, 0, 1, axis=dim)
    tail = lax.slice_in_dim(cells, size - 1, size, axis=dim)
    up = [(i, i + 1) for i in range(count - 1)]
    down = [(i + 1, i) for i in range(count - 1)]
    if wrap:
        up.append((count - 1, 0))
        down.append((0, count - 1))
    from_low = lax.ppermute(tail, axis, up)
    from_high = lax.ppermute(head, axis, down)
    low = jnp.where(fix_low, head, from_low)
    high = jnp.where(fix_high, tail, from_high)
    return jnp.concatenate([low, cells, high], axis=dim)


def local(field_state, shell_owner, block_sources, block_targets, interp_weights):
    grid_cells = field_state[0]
    ncomp, len_x, len_y, len_z = grid_cells.shape
    domain = lax.axis_index("dom")
    column = lax.axis_index("gx")
    yz_index = lax.axis_index("yz")
    gx_count = lax.axis_size("gx")
    yz_count = lax.axis_size("yz")
    per_y = len_y // BLK
    per_z = len_z // BLK
    volume = BLK * BLK * BLK
    shell_cells = grid_cells[:, :, :, len_z - SR * BLK :]
    shell_cells = shell_cells.reshape(ncomp, len_x // BLK, BLK, per_y, BLK, SR, BLK)
    shell_cells = (
        shell_cells.transpose(1, 3, 5, 0, 2, 4, 6).reshape(-1, ncomp * volume).astype(jnp.bfloat16)
    )
    count_here = shell_cells.shape[0]
    owner_table = shell_owner[0]
    own_owner = lax.dynamic_index_in_dim(owner_table, yz_index, 0, keepdims=False)
    index_here = jnp.arange(count_here, dtype=jnp.int32)
    local_same = own_owner[None, :] == own_owner[:, None]
    rank_local = jnp.sum(
        (local_same & (index_here[None, :] < index_here[:, None])).astype(jnp.int32), axis=1
    )
    slot_of = own_owner * CAP + rank_local
    slot_count = yz_count * CAP
    select = jnp.arange(slot_count, dtype=jnp.int32)[:, None] == slot_of[None, :]
    send_cells = jnp.dot(
        select.astype(jnp.bfloat16), shell_cells, preferred_element_type=jnp.float32
    )
    send_cells = send_cells.astype(jnp.bfloat16).reshape(yz_count, CAP, ncomp * volume)
    moved = lax.ppermute(send_cells, "dom", [(0, 1)])
    got_cells = lax.all_to_all(moved, "yz", split_axis=0, concat_axis=0, tiled=True)
    got_cells = got_cells.reshape(slot_count, ncomp * volume)
    mine = (owner_table == yz_index).astype(jnp.int32)
    per_sender = jnp.sum(mine, axis=1)
    before = jnp.cumsum(per_sender) - per_sender
    rank_slot = jnp.arange(CAP, dtype=jnp.int32)
    got_tags = jnp.where(
        rank_slot[None, :] < per_sender[:, None], before[:, None] + rank_slot[None, :], -1
    ).reshape(slot_count)
    wanted = block_sources[0, 0].reshape(-1)
    match_table = (wanted[:, None] == got_tags[None, :]) & (wanted[:, None] >= 0)
    picked = jnp.dot(
        match_table.astype(jnp.bfloat16), got_cells, preferred_element_type=jnp.float32
    )
    slots_here = block_targets.shape[2]
    picked = picked.astype(jnp.bfloat16).reshape(slots_here, -1, ncomp, volume)
    interp_blocks = jnp.einsum(
        "jkcs,jkst->jct", picked, interp_weights[0, 0], preferred_element_type=jnp.float32
    )

    for slot_number in range(slots_here):
        target_block = block_targets[0, 0, slot_number]
        live_slot = (target_block >= 0) & (domain == 1)
        block_spot = jnp.maximum(target_block, 0)
        block_x = block_spot // (per_y * per_z)
        block_y = block_spot // per_z % per_y
        block_z = block_spot % per_z
        corner_start = (jnp.int32(0), block_x * BLK, block_y * BLK, block_z * BLK)
        old_block = lax.dynamic_slice(grid_cells, corner_start, (ncomp, BLK, BLK, BLK))
        new_block = interp_blocks[slot_number].reshape(ncomp, BLK, BLK, BLK)
        grid_cells = lax.dynamic_update_slice(
            grid_cells, jnp.where(live_slot, new_block, old_block), corner_start
        )

    helio_side = domain == 1
    low_x = helio_side & (column == 0)
    high_x = helio_side & (column == gx_count - 1)
    low_y = yz_index == 0
    high_y = yz_index == yz_count - 1
    line_x = ghost_pair(grid_cells, "gx", 1, True, low_x, high_x)
    line_y = ghost_pair(grid_cells, "yz", 2, False, low_y, high_y)
    line_z = jnp.pad(grid_cells, ((0, 0), (0, 0), (0, 0), (1, 1)), mode="edge")
    step_ratio = jnp.where(domain == 0, CORONA_RATIO, HELIO_RATIO).astype(jnp.float32)
    updated = advance((line_x, line_y, line_z), grid_cells, step_ratio)
    return updated[None]


def solution(mesh):
    placed = (
        P("dom", None, "gx", "yz", None),
        P("gx", None, None),
        P("gx", "yz", None, None),
        P("gx", "yz", None),
        P("gx", "yz", None, None, None, None),
    )
    return jax.shard_map(
        local,
        mesh=mesh,
        in_specs=placed,
        out_specs=P("dom", None, "gx", "yz", None),
        check_vma=False,
    )
```

```python
import jax
import jax.numpy as jnp
from jax import lax
from jax.sharding import PartitionSpec as P

BLK = 8
SR = 2
CAP = 2


HEAT_RATIO = 5.0 / 3.0
CORONA_RATIO = 0.04
HELIO_RATIO = 0.03


def direction_flux(grid_cells, direction):
    density = grid_cells[0]
    momentum = grid_cells[1:4]
    magnetic = grid_cells[4:7]
    energy = grid_cells[7]
    velocity = momentum / density
    field_sq = jnp.sum(magnetic * magnetic, axis=0)
    pressure = (HEAT_RATIO - 1.0) * (
        energy - 0.5 * jnp.sum(momentum * velocity, axis=0) - 0.5 * field_sq
    )
    total_pressure = pressure + 0.5 * field_sq
    normal_speed = velocity[direction]
    normal_field = magnetic[direction]
    velocity_dot = jnp.sum(velocity * magnetic, axis=0)
    flux_list = [momentum[direction]]
    for other in range(3):
        term = momentum[other] * normal_speed - magnetic[other] * normal_field
        if other == direction:
            term = term + total_pressure
        flux_list.append(term)
    for other in range(3):
        flux_list.append(normal_speed * magnetic[other] - normal_field * velocity[other])
    flux_list.append((energy + total_pressure) * normal_speed - normal_field * velocity_dot)
    wave_speed = jnp.abs(normal_speed) + jnp.sqrt((HEAT_RATIO * pressure + field_sq) / density)
    return (jnp.stack(flux_list), wave_speed)


def interface_change(padded_line, direction):
    phys_flux, wave_speed = direction_flux(padded_line, direction)
    array_dim = direction + 1
    cell_count = padded_line.shape[array_dim]
    low_cells = lax.slice_in_dim(padded_line, 0, cell_count - 1, axis=array_dim)
    high_cells = lax.slice_in_dim(padded_line, 1, cell_count, axis=array_dim)
    low_flux = lax.slice_in_dim(phys_flux, 0, cell_count - 1, axis=array_dim)
    high_flux = lax.slice_in_dim(phys_flux, 1, cell_count, axis=array_dim)
    low_speed = lax.slice_in_dim(wave_speed, 0, cell_count - 1, axis=direction)
    high_speed = lax.slice_in_dim(wave_speed, 1, cell_count, axis=direction)
    fastest = jnp.maximum(low_speed, high_speed)
    face_flux = 0.5 * (low_flux + high_flux) - 0.5 * fastest[None] * (high_cells - low_cells)
    upper_face = lax.slice_in_dim(face_flux, 1, cell_count - 1, axis=array_dim)
    lower_face = lax.slice_in_dim(face_flux, 0, cell_count - 2, axis=array_dim)
    return upper_face - lower_face


def advance(line_set, inner_cells, step_ratio):
    change = interface_change(line_set[0], 0) + interface_change(line_set[1], 1)
    change = change + interface_change(line_set[2], 2)
    return inner_cells - step_ratio * change


def ghost_pair(cells, axis, dim, wrap, fix_low, fix_high):
    count = lax.axis_size(axis)
    size = cells.shape[dim]
    head = lax.slice_in_dim(cells, 0, 1, axis=dim)
    tail = lax.slice_in_dim(cells, size - 1, size, axis=dim)
    up = [(i, i + 1) for i in range(count - 1)]
    down = [(i + 1, i) for i in range(count - 1)]
    if wrap:
        up.append((count - 1, 0))
        down.append((0, count - 1))
    from_low = lax.ppermute(tail, axis, up)
    from_high = lax.ppermute(head, axis, down)
    low = jnp.where(fix_low, head, from_low)
    high = jnp.where(fix_high, tail, from_high)
    return jnp.concatenate([low, cells, high], axis=dim)


def local(field_state, shell_owner, block_sources, block_targets, interp_weights):
    grid_cells = field_state[0]
    ncomp, len_x, len_y, len_z = grid_cells.shape
    domain = lax.axis_index("dom")
    column = lax.axis_index("gx")
    yz_index = lax.axis_index("yz")
    gx_count = lax.axis_size("gx")
    yz_count = lax.axis_size("yz")
    per_y = len_y // BLK
    per_z = len_z // BLK
    volume = BLK * BLK * BLK
    shell_cells = grid_cells[:, :, :, len_z - SR * BLK :]
    shell_cells = shell_cells.reshape(ncomp, len_x // BLK, BLK, per_y, BLK, SR, BLK)
    shell_cells = (
        shell_cells.transpose(1, 3, 5, 0, 2, 4, 6).reshape(-1, ncomp * volume).astype(jnp.bfloat16)
    )
    count_here = shell_cells.shape[0]
    owner_table = shell_owner[0]
    own_owner = lax.dynamic_index_in_dim(owner_table, yz_index, 0, keepdims=False)
    index_here = jnp.arange(count_here, dtype=jnp.int32)
    local_same = own_owner[None, :] == own_owner[:, None]
    rank_local = jnp.sum(
        (local_same & (index_here[None, :] < index_here[:, None])).astype(jnp.int32), axis=1
    )
    slot_of = own_owner * CAP + rank_local
    slot_count = yz_count * CAP
    select = jnp.arange(slot_count, dtype=jnp.int32)[:, None] == slot_of[None, :]
    send_cells = jnp.dot(
        select.astype(jnp.bfloat16), shell_cells, preferred_element_type=jnp.float32
    )
    send_cells = send_cells.astype(jnp.bfloat16).reshape(yz_count, CAP, ncomp * volume)
    moved = lax.ppermute(send_cells, "dom", [(0, 1)])
    got_cells = lax.all_to_all(moved, "yz", split_axis=0, concat_axis=0, tiled=True)
    got_cells = got_cells.reshape(slot_count, ncomp * volume)
    mine = (owner_table == yz_index).astype(jnp.int32)
    per_sender = jnp.sum(mine, axis=1)
    before = jnp.cumsum(per_sender) - per_sender
    rank_slot = jnp.arange(CAP, dtype=jnp.int32)
    got_tags = jnp.where(
        rank_slot[None, :] < per_sender[:, None], before[:, None] + rank_slot[None, :], -1
    ).reshape(slot_count)
    wanted = block_sources[0, 0].reshape(-1)
    match_table = (wanted[:, None] == got_tags[None, :]) & (wanted[:, None] >= 0)
    picked = jnp.dot(
        match_table.astype(jnp.bfloat16), got_cells, preferred_element_type=jnp.float32
    )
    slots_here = block_targets.shape[2]
    picked = picked.astype(jnp.bfloat16).reshape(slots_here, -1, ncomp, volume)
    interp_blocks = jnp.einsum(
        "jkcs,jkst->jct", picked, interp_weights[0, 0], preferred_element_type=jnp.float32
    )

    block_of = (
        (lax.broadcasted_iota(jnp.int32, (len_x, len_y, len_z), 0) // BLK * per_y
         + lax.broadcasted_iota(jnp.int32, (len_x, len_y, len_z), 1) // BLK) * per_z
        + lax.broadcasted_iota(jnp.int32, (len_x, len_y, len_z), 2) // BLK
    )
    reps = (1, len_x // BLK, len_y // BLK, len_z // BLK)
    for slot_number in range(slots_here):
        target_block = block_targets[0, 0, slot_number]
        target_block = jnp.where(domain == 1, target_block, -1)
        new_block = interp_blocks[slot_number].reshape(ncomp, BLK, BLK, BLK)
        grid_cells = jnp.where(
            (block_of == target_block)[None], jnp.tile(new_block, reps), grid_cells
        )

    helio_side = domain == 1
    low_x = helio_side & (column == 0)
    high_x = helio_side & (column == gx_count - 1)
    low_y = yz_index == 0
    high_y = yz_index == yz_count - 1
    line_x = ghost_pair(grid_cells, "gx", 1, True, low_x, high_x)
    line_y = ghost_pair(grid_cells, "yz", 2, False, low_y, high_y)
    line_z = jnp.pad(grid_cells, ((0, 0), (0, 0), (0, 0), (1, 1)), mode="edge")
    step_ratio = jnp.where(domain == 0, CORONA_RATIO, HELIO_RATIO).astype(jnp.float32)
    updated = advance((line_x, line_y, line_z), grid_cells, step_ratio)
    return updated[None]


def solution(mesh):
    placed = (
        P("dom", None, "gx", "yz", None),
        P("gx", None, None),
        P("gx", "yz", None, None),
        P("gx", "yz", None),
        P("gx", "yz", None, None, None, None),
    )
    return jax.shard_map(
        local,
        mesh=mesh,
        in_specs=placed,
        out_specs=P("dom", None, "gx", "yz", None),
        check_vma=False,
    )
```

```python
import jax
import jax.numpy as jnp
from jax import lax
from jax.sharding import PartitionSpec as P

BLK = 8
SR = 2
CAP = 2


HEAT_RATIO = 5.0 / 3.0
CORONA_RATIO = 0.04
HELIO_RATIO = 0.03


def direction_flux(grid_cells, direction):
    density = grid_cells[0]
    momentum = grid_cells[1:4]
    magnetic = grid_cells[4:7]
    energy = grid_cells[7]
    velocity = momentum / density
    field_sq = jnp.sum(magnetic * magnetic, axis=0)
    pressure = (HEAT_RATIO - 1.0) * (
        energy - 0.5 * jnp.sum(momentum * velocity, axis=0) - 0.5 * field_sq
    )
    total_pressure = pressure + 0.5 * field_sq
    normal_speed = velocity[direction]
    normal_field = magnetic[direction]
    velocity_dot = jnp.sum(velocity * magnetic, axis=0)
    flux_list = [momentum[direction]]
    for other in range(3):
        term = momentum[other] * normal_speed - magnetic[other] * normal_field
        if other == direction:
            term = term + total_pressure
        flux_list.append(term)
    for other in range(3):
        flux_list.append(normal_speed * magnetic[other] - normal_field * velocity[other])
    flux_list.append((energy + total_pressure) * normal_speed - normal_field * velocity_dot)
    wave_speed = jnp.abs(normal_speed) + jnp.sqrt((HEAT_RATIO * pressure + field_sq) / density)
    return (jnp.stack(flux_list), wave_speed)


def interface_change(padded_line, direction):
    phys_flux, wave_speed = direction_flux(padded_line, direction)
    array_dim = direction + 1
    cell_count = padded_line.shape[array_dim]
    low_cells = lax.slice_in_dim(padded_line, 0, cell_count - 1, axis=array_dim)
    high_cells = lax.slice_in_dim(padded_line, 1, cell_count, axis=array_dim)
    low_flux = lax.slice_in_dim(phys_flux, 0, cell_count - 1, axis=array_dim)
    high_flux = lax.slice_in_dim(phys_flux, 1, cell_count, axis=array_dim)
    low_speed = lax.slice_in_dim(wave_speed, 0, cell_count - 1, axis=direction)
    high_speed = lax.slice_in_dim(wave_speed, 1, cell_count, axis=direction)
    fastest = jnp.maximum(low_speed, high_speed)
    face_flux = 0.5 * (low_flux + high_flux) - 0.5 * fastest[None] * (high_cells - low_cells)
    upper_face = lax.slice_in_dim(face_flux, 1, cell_count - 1, axis=array_dim)
    lower_face = lax.slice_in_dim(face_flux, 0, cell_count - 2, axis=array_dim)
    return upper_face - lower_face


def advance(line_set, inner_cells, step_ratio):
    change = interface_change(line_set[0], 0) + interface_change(line_set[1], 1)
    change = change + interface_change(line_set[2], 2)
    return inner_cells - step_ratio * change


def ghost_pair(cells, axis, dim, wrap, fix_low, fix_high):
    count = lax.axis_size(axis)
    size = cells.shape[dim]
    head = lax.slice_in_dim(cells, 0, 1, axis=dim)
    tail = lax.slice_in_dim(cells, size - 1, size, axis=dim)
    up = [(i, i + 1) for i in range(count - 1)]
    down = [(i + 1, i) for i in range(count - 1)]
    if wrap:
        up.append((count - 1, 0))
        down.append((0, count - 1))
    from_low = lax.ppermute(tail, axis, up)
    from_high = lax.ppermute(head, axis, down)
    low = jnp.where(fix_low, head, from_low)
    high = jnp.where(fix_high, tail, from_high)
    return jnp.concatenate([low, cells, high], axis=dim)


def local(field_state, shell_owner, block_sources, block_targets, interp_weights):
    grid_cells = field_state[0]
    ncomp, len_x, len_y, len_z = grid_cells.shape
    domain = lax.axis_index("dom")
    column = lax.axis_index("gx")
    yz_index = lax.axis_index("yz")
    gx_count = lax.axis_size("gx")
    yz_count = lax.axis_size("yz")
    per_y = len_y // BLK
    per_z = len_z // BLK
    volume = BLK * BLK * BLK
    shell_cells = grid_cells[:, :, :, len_z - SR * BLK :]
    shell_cells = shell_cells.reshape(ncomp, len_x // BLK, BLK, per_y, BLK, SR, BLK)
    shell_cells = (
        shell_cells.transpose(1, 3, 5, 0, 2, 4, 6).reshape(-1, ncomp * volume).astype(jnp.bfloat16)
    )
    count_here = shell_cells.shape[0]
    owner_table = shell_owner[0]
    own_owner = lax.dynamic_index_in_dim(owner_table, yz_index, 0, keepdims=False)
    index_here = jnp.arange(count_here, dtype=jnp.int32)
    local_same = own_owner[None, :] == own_owner[:, None]
    rank_local = jnp.sum(
        (local_same & (index_here[None, :] < index_here[:, None])).astype(jnp.int32), axis=1
    )
    slot_of = own_owner * CAP + rank_local
    slot_count = yz_count * CAP
    select = jnp.arange(slot_count, dtype=jnp.int32)[:, None] == slot_of[None, :]
    send_cells = jnp.dot(
        select.astype(jnp.bfloat16), shell_cells, preferred_element_type=jnp.float32
    )
    send_cells = send_cells.astype(jnp.bfloat16).reshape(yz_count, CAP, ncomp * volume)
    moved = lax.ppermute(send_cells, "dom", [(0, 1)])
    got_cells = lax.all_to_all(moved, "yz", split_axis=0, concat_axis=0, tiled=True)
    got_cells = got_cells.reshape(slot_count, ncomp * volume)
    mine = (owner_table == yz_index).astype(jnp.int32)
    per_sender = jnp.sum(mine, axis=1)
    before = jnp.cumsum(per_sender) - per_sender
    rank_slot = jnp.arange(CAP, dtype=jnp.int32)
    got_tags = jnp.where(
        rank_slot[None, :] < per_sender[:, None], before[:, None] + rank_slot[None, :], -1
    ).reshape(slot_count)
    wanted = block_sources[0, 0].reshape(-1)
    match_table = (wanted[:, None] == got_tags[None, :]) & (wanted[:, None] >= 0)
    picked = jnp.dot(
        match_table.astype(jnp.bfloat16), got_cells, preferred_element_type=jnp.float32
    )
    slots_here = block_targets.shape[2]
    picked = picked.astype(jnp.bfloat16).reshape(slots_here, -1, ncomp, volume)
    interp_blocks = jnp.einsum(
        "jkcs,jkst->jct", picked, interp_weights[0, 0], preferred_element_type=jnp.float32
    )

    rows = lax.broadcasted_iota(jnp.int32, (len_x, len_y, len_z), 0) // BLK
    cols = lax.broadcasted_iota(jnp.int32, (len_x, len_y, len_z), 1) // BLK
    lanes = lax.broadcasted_iota(jnp.int32, (len_x, len_y, len_z), 2)
    spread_of = lax.broadcasted_iota(jnp.int32, (BLK, len_z), 1) % BLK
    offset_of = lax.broadcasted_iota(jnp.int32, (BLK, len_z), 0)
    spread = (spread_of == offset_of).astype(jnp.float32)
    stacked = interp_blocks.reshape(slots_here * ncomp * BLK * BLK, BLK)
    stacked = jnp.dot(stacked, spread, precision=lax.Precision.HIGHEST)
    stacked = stacked.reshape(slots_here, ncomp, BLK, BLK, len_z)
    for slot_number in range(slots_here):
        target_block = block_targets[0, 0, slot_number]
        target_block = jnp.where(domain == 1, target_block, -1)
        block_spot = jnp.maximum(target_block, 0)
        hit = (
            (rows == block_spot // (per_y * per_z))
            & (cols == block_spot // per_z % per_y)
            & (lanes // BLK == block_spot % per_z)
            & (target_block >= 0)
        )
        placed = jnp.tile(stacked[slot_number], (1, len_x // BLK, len_y // BLK, 1))
        grid_cells = jnp.where(hit[None], placed, grid_cells)

    helio_side = domain == 1
    low_x = helio_side & (column == 0)
    high_x = helio_side & (column == gx_count - 1)
    low_y = yz_index == 0
    high_y = yz_index == yz_count - 1
    line_x = ghost_pair(grid_cells, "gx", 1, True, low_x, high_x)
    line_y = ghost_pair(grid_cells, "yz", 2, False, low_y, high_y)
    line_z = jnp.pad(grid_cells, ((0, 0), (0, 0), (0, 0), (1, 1)), mode="edge")
    step_ratio = jnp.where(domain == 0, CORONA_RATIO, HELIO_RATIO).astype(jnp.float32)
    updated = advance((line_x, line_y, line_z), grid_cells, step_ratio)
    return updated[None]


def solution(mesh):
    placed = (
        P("dom", None, "gx", "yz", None),
        P("gx", None, None),
        P("gx", "yz", None, None),
        P("gx", "yz", None),
        P("gx", "yz", None, None, None, None),
    )
    return jax.shard_map(
        local,
        mesh=mesh,
        in_specs=placed,
        out_specs=P("dom", None, "gx", "yz", None),
        check_vma=False,
    )
```

```python
import jax
import jax.numpy as jnp
from jax import lax
from jax.experimental import pallas as pl
from jax.experimental.pallas import tpu as pltpu
from jax.sharding import PartitionSpec as P

MESH = pl.DeviceIdType.MESH

BLK = 8
SR = 2
CAP = 2


HEAT_RATIO = 5.0 / 3.0
CORONA_RATIO = 0.04
HELIO_RATIO = 0.03


def direction_flux(grid_cells, direction):
    density = grid_cells[0]
    momentum = grid_cells[1:4]
    magnetic = grid_cells[4:7]
    energy = grid_cells[7]
    velocity = momentum / density
    field_sq = jnp.sum(magnetic * magnetic, axis=0)
    pressure = (HEAT_RATIO - 1.0) * (
        energy - 0.5 * jnp.sum(momentum * velocity, axis=0) - 0.5 * field_sq
    )
    total_pressure = pressure + 0.5 * field_sq
    normal_speed = velocity[direction]
    normal_field = magnetic[direction]
    velocity_dot = jnp.sum(velocity * magnetic, axis=0)
    flux_list = [momentum[direction]]
    for other in range(3):
        term = momentum[other] * normal_speed - magnetic[other] * normal_field
        if other == direction:
            term = term + total_pressure
        flux_list.append(term)
    for other in range(3):
        flux_list.append(normal_speed * magnetic[other] - normal_field * velocity[other])
    flux_list.append((energy + total_pressure) * normal_speed - normal_field * velocity_dot)
    wave_speed = jnp.abs(normal_speed) + jnp.sqrt((HEAT_RATIO * pressure + field_sq) / density)
    return (jnp.stack(flux_list), wave_speed)


def interface_change(padded_line, direction):
    phys_flux, wave_speed = direction_flux(padded_line, direction)
    array_dim = direction + 1
    cell_count = padded_line.shape[array_dim]
    low_cells = lax.slice_in_dim(padded_line, 0, cell_count - 1, axis=array_dim)
    high_cells = lax.slice_in_dim(padded_line, 1, cell_count, axis=array_dim)
    low_flux = lax.slice_in_dim(phys_flux, 0, cell_count - 1, axis=array_dim)
    high_flux = lax.slice_in_dim(phys_flux, 1, cell_count, axis=array_dim)
    low_speed = lax.slice_in_dim(wave_speed, 0, cell_count - 1, axis=direction)
    high_speed = lax.slice_in_dim(wave_speed, 1, cell_count, axis=direction)
    fastest = jnp.maximum(low_speed, high_speed)
    face_flux = 0.5 * (low_flux + high_flux) - 0.5 * fastest[None] * (high_cells - low_cells)
    upper_face = lax.slice_in_dim(face_flux, 1, cell_count - 1, axis=array_dim)
    lower_face = lax.slice_in_dim(face_flux, 0, cell_count - 2, axis=array_dim)
    return upper_face - lower_face


def advance(line_set, inner_cells, step_ratio):
    change = interface_change(line_set[0], 0) + interface_change(line_set[1], 1)
    change = change + interface_change(line_set[2], 2)
    return inner_cells - step_ratio * change


def ghost_pair(cells, axis, dim, wrap, fix_low, fix_high):
    count = lax.axis_size(axis)
    size = cells.shape[dim]
    head = lax.slice_in_dim(cells, 0, 1, axis=dim)
    tail = lax.slice_in_dim(cells, size - 1, size, axis=dim)
    up = [(i, i + 1) for i in range(count - 1)]
    down = [(i + 1, i) for i in range(count - 1)]
    if wrap:
        up.append((count - 1, 0))
        down.append((0, count - 1))
    from_low = lax.ppermute(tail, axis, up)
    from_high = lax.ppermute(head, axis, down)
    low = jnp.where(fix_low, head, from_low)
    high = jnp.where(fix_high, tail, from_high)
    return jnp.concatenate([low, cells, high], axis=dim)


def route_kernel(send_ref, out_ref, landed, send_sem, recv_sem):
    domain = lax.axis_index("dom")
    here = lax.axis_index("yz")
    count = send_ref.shape[0]
    barrier = pltpu.get_barrier_semaphore()
    for partner in range(count):
        pl.semaphore_signal(
            barrier, inc=1, device_id={"dom": 1 - domain, "yz": partner}, device_id_type=MESH
        )
    pl.semaphore_wait(barrier, count)

    @pl.when(domain == 0)
    def _():
        copies = []
        for owner in range(count):
            copy = pltpu.make_async_remote_copy(
                src_ref=send_ref.at[owner],
                dst_ref=landed.at[here],
                send_sem=send_sem.at[owner],
                recv_sem=recv_sem.at[here],
                device_id={"dom": 1, "yz": owner},
                device_id_type=MESH,
            )
            copy.start()
            copies.append(copy)
        for copy in copies:
            copy.wait_send()
        out_ref[...] = jnp.zeros_like(out_ref)

    @pl.when(domain == 1)
    def _():
        for sender in range(count):
            pltpu.make_async_remote_copy(
                src_ref=send_ref.at[sender],
                dst_ref=landed.at[sender],
                send_sem=send_sem.at[sender],
                recv_sem=recv_sem.at[sender],
                device_id={"dom": 0, "yz": sender},
                device_id_type=MESH,
            ).wait_recv()
        out_ref[...] = landed[...]


def route_blocks(send_cells):
    count = send_cells.shape[0]
    return pl.pallas_call(
        route_kernel,
        out_shape=jax.ShapeDtypeStruct(send_cells.shape, send_cells.dtype),
        in_specs=[pl.BlockSpec(memory_space=pltpu.VMEM)],
        out_specs=pl.BlockSpec(memory_space=pltpu.VMEM),
        scratch_shapes=[
            pltpu.VMEM(send_cells.shape, send_cells.dtype),
            pltpu.SemaphoreType.DMA((count,)),
            pltpu.SemaphoreType.DMA((count,)),
        ],
        compiler_params=pltpu.CompilerParams(collective_id=0, has_side_effects=True),
    )(send_cells)


def local(field_state, shell_owner, block_sources, block_targets, interp_weights):
    grid_cells = field_state[0]
    ncomp, len_x, len_y, len_z = grid_cells.shape
    domain = lax.axis_index("dom")
    column = lax.axis_index("gx")
    yz_index = lax.axis_index("yz")
    gx_count = lax.axis_size("gx")
    yz_count = lax.axis_size("yz")
    per_y = len_y // BLK
    per_z = len_z // BLK
    volume = BLK * BLK * BLK
    shell_cells = grid_cells[:, :, :, len_z - SR * BLK :]
    shell_cells = shell_cells.reshape(ncomp, len_x // BLK, BLK, per_y, BLK, SR, BLK)
    shell_cells = (
        shell_cells.transpose(1, 3, 5, 0, 2, 4, 6).reshape(-1, ncomp * volume).astype(jnp.bfloat16)
    )
    count_here = shell_cells.shape[0]
    owner_table = shell_owner[0]
    own_owner = lax.dynamic_index_in_dim(owner_table, yz_index, 0, keepdims=False)
    index_here = jnp.arange(count_here, dtype=jnp.int32)
    local_same = own_owner[None, :] == own_owner[:, None]
    rank_local = jnp.sum(
        (local_same & (index_here[None, :] < index_here[:, None])).astype(jnp.int32), axis=1
    )
    slot_of = own_owner * CAP + rank_local
    slot_count = yz_count * CAP
    select = jnp.arange(slot_count, dtype=jnp.int32)[:, None] == slot_of[None, :]
    send_cells = jnp.dot(
        select.astype(jnp.bfloat16), shell_cells, preferred_element_type=jnp.float32
    )
    send_cells = send_cells.astype(jnp.bfloat16).reshape(yz_count, CAP * ncomp, volume)
    got_cells = route_blocks(send_cells).reshape(slot_count, ncomp * volume)
    mine = (owner_table == yz_index).astype(jnp.int32)
    per_sender = jnp.sum(mine, axis=1)
    before = jnp.cumsum(per_sender) - per_sender
    rank_slot = jnp.arange(CAP, dtype=jnp.int32)
    got_tags = jnp.where(
        rank_slot[None, :] < per_sender[:, None], before[:, None] + rank_slot[None, :], -1
    ).reshape(slot_count)
    wanted = block_sources[0, 0].reshape(-1)
    match_table = (wanted[:, None] == got_tags[None, :]) & (wanted[:, None] >= 0)
    picked = jnp.dot(
        match_table.astype(jnp.bfloat16), got_cells, preferred_element_type=jnp.float32
    )
    slots_here = block_targets.shape[2]
    picked = picked.astype(jnp.bfloat16).reshape(slots_here, -1, ncomp, volume)
    interp_blocks = jnp.einsum(
        "jkcs,jkst->jct", picked, interp_weights[0, 0], preferred_element_type=jnp.float32
    )

    rows = lax.broadcasted_iota(jnp.int32, (len_x, len_y, len_z), 0) // BLK
    cols = lax.broadcasted_iota(jnp.int32, (len_x, len_y, len_z), 1) // BLK
    lanes = lax.broadcasted_iota(jnp.int32, (len_x, len_y, len_z), 2)
    spread_of = lax.broadcasted_iota(jnp.int32, (BLK, len_z), 1) % BLK
    offset_of = lax.broadcasted_iota(jnp.int32, (BLK, len_z), 0)
    spread = (spread_of == offset_of).astype(jnp.float32)
    stacked = interp_blocks.reshape(slots_here * ncomp * BLK * BLK, BLK)
    stacked = jnp.dot(stacked, spread, precision=lax.Precision.HIGHEST)
    stacked = stacked.reshape(slots_here, ncomp, BLK, BLK, len_z)
    for slot_number in range(slots_here):
        target_block = block_targets[0, 0, slot_number]
        target_block = jnp.where(domain == 1, target_block, -1)
        block_spot = jnp.maximum(target_block, 0)
        hit = (
            (rows == block_spot // (per_y * per_z))
            & (cols == block_spot // per_z % per_y)
            & (lanes // BLK == block_spot % per_z)
            & (target_block >= 0)
        )
        placed = jnp.tile(stacked[slot_number], (1, len_x // BLK, len_y // BLK, 1))
        grid_cells = jnp.where(hit[None], placed, grid_cells)

    helio_side = domain == 1
    low_x = helio_side & (column == 0)
    high_x = helio_side & (column == gx_count - 1)
    low_y = yz_index == 0
    high_y = yz_index == yz_count - 1
    line_x = ghost_pair(grid_cells, "gx", 1, True, low_x, high_x)
    line_y = ghost_pair(grid_cells, "yz", 2, False, low_y, high_y)
    line_z = jnp.pad(grid_cells, ((0, 0), (0, 0), (0, 0), (1, 1)), mode="edge")
    step_ratio = jnp.where(domain == 0, CORONA_RATIO, HELIO_RATIO).astype(jnp.float32)
    updated = advance((line_x, line_y, line_z), grid_cells, step_ratio)
    return updated[None]


def solution(mesh):
    placed = (
        P("dom", None, "gx", "yz", None),
        P("gx", None, None),
        P("gx", "yz", None, None),
        P("gx", "yz", None),
        P("gx", "yz", None, None, None, None),
    )
    return jax.shard_map(
        local,
        mesh=mesh,
        in_specs=placed,
        out_specs=P("dom", None, "gx", "yz", None),
        check_vma=False,
    )
```

```python
import jax
import jax.numpy as jnp
from jax import lax
from jax.experimental import pallas as pl
from jax.experimental.pallas import tpu as pltpu
from jax.sharding import PartitionSpec as P

MESH = pl.DeviceIdType.MESH

BLK = 8
SR = 2
CAP = 2


HEAT_RATIO = 5.0 / 3.0
CORONA_RATIO = 0.04
HELIO_RATIO = 0.03


def direction_flux(grid_cells, direction):
    density = grid_cells[0]
    momentum = grid_cells[1:4]
    magnetic = grid_cells[4:7]
    energy = grid_cells[7]
    velocity = momentum / density
    field_sq = jnp.sum(magnetic * magnetic, axis=0)
    pressure = (HEAT_RATIO - 1.0) * (
        energy - 0.5 * jnp.sum(momentum * velocity, axis=0) - 0.5 * field_sq
    )
    total_pressure = pressure + 0.5 * field_sq
    normal_speed = velocity[direction]
    normal_field = magnetic[direction]
    velocity_dot = jnp.sum(velocity * magnetic, axis=0)
    flux_list = [momentum[direction]]
    for other in range(3):
        term = momentum[other] * normal_speed - magnetic[other] * normal_field
        if other == direction:
            term = term + total_pressure
        flux_list.append(term)
    for other in range(3):
        flux_list.append(normal_speed * magnetic[other] - normal_field * velocity[other])
    flux_list.append((energy + total_pressure) * normal_speed - normal_field * velocity_dot)
    wave_speed = jnp.abs(normal_speed) + jnp.sqrt((HEAT_RATIO * pressure + field_sq) / density)
    return (jnp.stack(flux_list), wave_speed)


def interface_change(padded_line, direction):
    phys_flux, wave_speed = direction_flux(padded_line, direction)
    array_dim = direction + 1
    cell_count = padded_line.shape[array_dim]
    low_cells = lax.slice_in_dim(padded_line, 0, cell_count - 1, axis=array_dim)
    high_cells = lax.slice_in_dim(padded_line, 1, cell_count, axis=array_dim)
    low_flux = lax.slice_in_dim(phys_flux, 0, cell_count - 1, axis=array_dim)
    high_flux = lax.slice_in_dim(phys_flux, 1, cell_count, axis=array_dim)
    low_speed = lax.slice_in_dim(wave_speed, 0, cell_count - 1, axis=direction)
    high_speed = lax.slice_in_dim(wave_speed, 1, cell_count, axis=direction)
    fastest = jnp.maximum(low_speed, high_speed)
    face_flux = 0.5 * (low_flux + high_flux) - 0.5 * fastest[None] * (high_cells - low_cells)
    upper_face = lax.slice_in_dim(face_flux, 1, cell_count - 1, axis=array_dim)
    lower_face = lax.slice_in_dim(face_flux, 0, cell_count - 2, axis=array_dim)
    return upper_face - lower_face


def advance(line_set, inner_cells, step_ratio):
    change = interface_change(line_set[0], 0) + interface_change(line_set[1], 1)
    change = change + interface_change(line_set[2], 2)
    return inner_cells - step_ratio * change


def route_kernel(send_ref, out_ref, landed, send_sem, recv_sem):
    domain = lax.axis_index("dom")
    here = lax.axis_index("yz")
    count = send_ref.shape[0]
    barrier = pltpu.get_barrier_semaphore()
    for partner in range(count):
        pl.semaphore_signal(
            barrier, inc=1, device_id={"dom": 1 - domain, "yz": partner}, device_id_type=MESH
        )
    pl.semaphore_wait(barrier, count)

    @pl.when(domain == 0)
    def _():
        copies = []
        for owner in range(count):
            copy = pltpu.make_async_remote_copy(
                src_ref=send_ref.at[owner],
                dst_ref=landed.at[here],
                send_sem=send_sem.at[owner],
                recv_sem=recv_sem.at[here],
                device_id={"dom": 1, "yz": owner},
                device_id_type=MESH,
            )
            copy.start()
            copies.append(copy)
        for copy in copies:
            copy.wait_send()
        out_ref[...] = jnp.zeros_like(out_ref)

    @pl.when(domain == 1)
    def _():
        for sender in range(count):
            pltpu.make_async_remote_copy(
                src_ref=send_ref.at[sender],
                dst_ref=landed.at[sender],
                send_sem=send_sem.at[sender],
                recv_sem=recv_sem.at[sender],
                device_id={"dom": 0, "yz": sender},
                device_id_type=MESH,
            ).wait_recv()
        out_ref[...] = landed[...]


def route_blocks(send_cells):
    count = send_cells.shape[0]
    return pl.pallas_call(
        route_kernel,
        out_shape=jax.ShapeDtypeStruct(send_cells.shape, send_cells.dtype),
        in_specs=[pl.BlockSpec(memory_space=pltpu.VMEM)],
        out_specs=pl.BlockSpec(memory_space=pltpu.VMEM),
        scratch_shapes=[
            pltpu.VMEM(send_cells.shape, send_cells.dtype),
            pltpu.SemaphoreType.DMA((count,)),
            pltpu.SemaphoreType.DMA((count,)),
        ],
        compiler_params=pltpu.CompilerParams(collective_id=0, has_side_effects=True),
    )(send_cells)


def halo_kernel(grid_ref, out_ref, landed, send_sem, recv_sem):
    column = lax.axis_index("gx")
    row = lax.axis_index("yz")
    gx_count = lax.axis_size("gx")
    yz_count = lax.axis_size("yz")
    len_x, len_y = grid_ref.shape[1], grid_ref.shape[2]
    up_x = {"gx": lax.rem(column + 1, gx_count)}
    down_x = {"gx": lax.rem(column + gx_count - 1, gx_count)}
    up_y = {"yz": lax.rem(row + 1, yz_count)}
    down_y = {"yz": lax.rem(row + yz_count - 1, yz_count)}
    barrier = pltpu.get_barrier_semaphore()
    for partner in (up_x, down_x, up_y, down_y):
        pl.semaphore_signal(barrier, inc=1, device_id=partner, device_id_type=MESH)
    pl.semaphore_wait(barrier, 4)
    sends = (
        (grid_ref.at[:, len_x - 1], up_x),
        (grid_ref.at[:, 0], down_x),
        (grid_ref.at[:, :, len_y - 1], up_y),
        (grid_ref.at[:, :, 0], down_y),
    )
    copies = []
    for slot, (source, partner) in enumerate(sends):
        copy = pltpu.make_async_remote_copy(
            src_ref=source,
            dst_ref=landed.at[slot],
            send_sem=send_sem.at[slot],
            recv_sem=recv_sem.at[slot],
            device_id=partner,
            device_id_type=MESH,
        )
        copy.start()
        copies.append(copy)
    for copy in copies:
        copy.wait()
    out_ref[...] = landed[...]


def exchange_faces(grid_cells):
    ncomp, len_x, len_y, len_z = grid_cells.shape
    face = (4, ncomp, len_x, len_z)
    return pl.pallas_call(
        halo_kernel,
        out_shape=jax.ShapeDtypeStruct(face, grid_cells.dtype),
        in_specs=[pl.BlockSpec(memory_space=pl.ANY)],
        out_specs=pl.BlockSpec(memory_space=pltpu.VMEM),
        scratch_shapes=[
            pltpu.VMEM(face, grid_cells.dtype),
            pltpu.SemaphoreType.DMA((4,)),
            pltpu.SemaphoreType.DMA((4,)),
        ],
        compiler_params=pltpu.CompilerParams(collective_id=1, has_side_effects=True),
    )(grid_cells)


def local(field_state, shell_owner, block_sources, block_targets, interp_weights):
    grid_cells = field_state[0]
    ncomp, len_x, len_y, len_z = grid_cells.shape
    domain = lax.axis_index("dom")
    column = lax.axis_index("gx")
    yz_index = lax.axis_index("yz")
    gx_count = lax.axis_size("gx")
    yz_count = lax.axis_size("yz")
    per_y = len_y // BLK
    per_z = len_z // BLK
    volume = BLK * BLK * BLK
    shell_cells = grid_cells[:, :, :, len_z - SR * BLK :]
    shell_cells = shell_cells.reshape(ncomp, len_x // BLK, BLK, per_y, BLK, SR, BLK)
    shell_cells = (
        shell_cells.transpose(1, 3, 5, 0, 2, 4, 6).reshape(-1, ncomp * volume).astype(jnp.bfloat16)
    )
    count_here = shell_cells.shape[0]
    owner_table = shell_owner[0]
    own_owner = lax.dynamic_index_in_dim(owner_table, yz_index, 0, keepdims=False)
    index_here = jnp.arange(count_here, dtype=jnp.int32)
    local_same = own_owner[None, :] == own_owner[:, None]
    rank_local = jnp.sum(
        (local_same & (index_here[None, :] < index_here[:, None])).astype(jnp.int32), axis=1
    )
    slot_of = own_owner * CAP + rank_local
    slot_count = yz_count * CAP
    select = jnp.arange(slot_count, dtype=jnp.int32)[:, None] == slot_of[None, :]
    send_cells = jnp.dot(
        select.astype(jnp.bfloat16), shell_cells, preferred_element_type=jnp.float32
    )
    send_cells = send_cells.astype(jnp.bfloat16).reshape(yz_count, CAP * ncomp, volume)
    got_cells = route_blocks(send_cells).reshape(slot_count, ncomp * volume)
    mine = (owner_table == yz_index).astype(jnp.int32)
    per_sender = jnp.sum(mine, axis=1)
    before = jnp.cumsum(per_sender) - per_sender
    rank_slot = jnp.arange(CAP, dtype=jnp.int32)
    got_tags = jnp.where(
        rank_slot[None, :] < per_sender[:, None], before[:, None] + rank_slot[None, :], -1
    ).reshape(slot_count)
    wanted = block_sources[0, 0].reshape(-1)
    match_table = (wanted[:, None] == got_tags[None, :]) & (wanted[:, None] >= 0)
    picked = jnp.dot(
        match_table.astype(jnp.bfloat16), got_cells, preferred_element_type=jnp.float32
    )
    slots_here = block_targets.shape[2]
    picked = picked.astype(jnp.bfloat16).reshape(slots_here, -1, ncomp, volume)
    interp_blocks = jnp.einsum(
        "jkcs,jkst->jct", picked, interp_weights[0, 0], preferred_element_type=jnp.float32
    )

    rows = lax.broadcasted_iota(jnp.int32, (len_x, len_y, len_z), 0) // BLK
    cols = lax.broadcasted_iota(jnp.int32, (len_x, len_y, len_z), 1) // BLK
    lanes = lax.broadcasted_iota(jnp.int32, (len_x, len_y, len_z), 2)
    spread_of = lax.broadcasted_iota(jnp.int32, (BLK, len_z), 1) % BLK
    offset_of = lax.broadcasted_iota(jnp.int32, (BLK, len_z), 0)
    spread = (spread_of == offset_of).astype(jnp.float32)
    stacked = interp_blocks.reshape(slots_here * ncomp * BLK * BLK, BLK)
    stacked = jnp.dot(stacked, spread, precision=lax.Precision.HIGHEST)
    stacked = stacked.reshape(slots_here, ncomp, BLK, BLK, len_z)
    targets = jnp.where(domain == 1, block_targets[0, 0], -1)
    spots = jnp.maximum(targets, 0)
    hit = (
        (rows[None] == (spots // (per_y * per_z))[:, None, None, None])
        & (cols[None] == (spots // per_z % per_y)[:, None, None, None])
        & (lanes[None] // BLK == (spots % per_z)[:, None, None, None])
        & (targets >= 0)[:, None, None, None]
    )
    for slot_number in range(slots_here):
        placed = jnp.tile(stacked[slot_number], (1, len_x // BLK, len_y // BLK, 1))
        grid_cells = jnp.where(hit[slot_number][None], placed, grid_cells)

    helio_side = domain == 1
    low_x = helio_side & (column == 0)
    high_x = helio_side & (column == gx_count - 1)
    low_y = yz_index == 0
    high_y = yz_index == yz_count - 1
    ghosts = exchange_faces(grid_cells)
    from_low_x, from_high_x, from_low_y, from_high_y = (
        lax.expand_dims(ghosts[0], (1,)),
        lax.expand_dims(ghosts[1], (1,)),
        lax.expand_dims(ghosts[2], (2,)),
        lax.expand_dims(ghosts[3], (2,)),
    )
    head_x, tail_x = grid_cells[:, :1], grid_cells[:, -1:]
    head_y, tail_y = grid_cells[:, :, :1], grid_cells[:, :, -1:]
    line_x = jnp.concatenate(
        [jnp.where(low_x, head_x, from_low_x), grid_cells, jnp.where(high_x, tail_x, from_high_x)],
        axis=1,
    )
    line_y = jnp.concatenate(
        [jnp.where(low_y, head_y, from_low_y), grid_cells, jnp.where(high_y, tail_y, from_high_y)],
        axis=2,
    )
    line_z = jnp.pad(grid_cells, ((0, 0), (0, 0), (0, 0), (1, 1)), mode="edge")
    step_ratio = jnp.where(domain == 0, CORONA_RATIO, HELIO_RATIO).astype(jnp.float32)
    updated = advance((line_x, line_y, line_z), grid_cells, step_ratio)
    return updated[None]


def solution(mesh):
    placed = (
        P("dom", None, "gx", "yz", None),
        P("gx", None, None),
        P("gx", "yz", None, None),
        P("gx", "yz", None),
        P("gx", "yz", None, None, None, None),
    )
    return jax.shard_map(
        local,
        mesh=mesh,
        in_specs=placed,
        out_specs=P("dom", None, "gx", "yz", None),
        check_vma=False,
    )
```

```python
import jax
import jax.numpy as jnp
from jax import lax
from jax.experimental import pallas as pl
from jax.experimental.pallas import tpu as pltpu
from jax.sharding import PartitionSpec as P

MESH = pl.DeviceIdType.MESH

BLK = 8
SR = 2
CAP = 2


HEAT_RATIO = 5.0 / 3.0
CORONA_RATIO = 0.04
HELIO_RATIO = 0.03


def direction_flux(grid_cells, direction):
    density = grid_cells[0]
    momentum = grid_cells[1:4]
    magnetic = grid_cells[4:7]
    energy = grid_cells[7]
    velocity = momentum / density
    field_sq = jnp.sum(magnetic * magnetic, axis=0)
    pressure = (HEAT_RATIO - 1.0) * (
        energy - 0.5 * jnp.sum(momentum * velocity, axis=0) - 0.5 * field_sq
    )
    total_pressure = pressure + 0.5 * field_sq
    normal_speed = velocity[direction]
    normal_field = magnetic[direction]
    velocity_dot = jnp.sum(velocity * magnetic, axis=0)
    flux_list = [momentum[direction]]
    for other in range(3):
        term = momentum[other] * normal_speed - magnetic[other] * normal_field
        if other == direction:
            term = term + total_pressure
        flux_list.append(term)
    for other in range(3):
        flux_list.append(normal_speed * magnetic[other] - normal_field * velocity[other])
    flux_list.append((energy + total_pressure) * normal_speed - normal_field * velocity_dot)
    wave_speed = jnp.abs(normal_speed) + jnp.sqrt((HEAT_RATIO * pressure + field_sq) / density)
    return (jnp.stack(flux_list), wave_speed)


def interface_change(padded_line, direction):
    phys_flux, wave_speed = direction_flux(padded_line, direction)
    array_dim = direction + 1
    cell_count = padded_line.shape[array_dim]
    low_cells = lax.slice_in_dim(padded_line, 0, cell_count - 1, axis=array_dim)
    high_cells = lax.slice_in_dim(padded_line, 1, cell_count, axis=array_dim)
    low_flux = lax.slice_in_dim(phys_flux, 0, cell_count - 1, axis=array_dim)
    high_flux = lax.slice_in_dim(phys_flux, 1, cell_count, axis=array_dim)
    low_speed = lax.slice_in_dim(wave_speed, 0, cell_count - 1, axis=direction)
    high_speed = lax.slice_in_dim(wave_speed, 1, cell_count, axis=direction)
    fastest = jnp.maximum(low_speed, high_speed)
    face_flux = 0.5 * (low_flux + high_flux) - 0.5 * fastest[None] * (high_cells - low_cells)
    upper_face = lax.slice_in_dim(face_flux, 1, cell_count - 1, axis=array_dim)
    lower_face = lax.slice_in_dim(face_flux, 0, cell_count - 2, axis=array_dim)
    return upper_face - lower_face


def advance(line_set, inner_cells, step_ratio):
    change = interface_change(line_set[0], 0) + interface_change(line_set[1], 1)
    change = change + interface_change(line_set[2], 2)
    return inner_cells - step_ratio * change


def route_kernel(send_ref, out_ref, landed, send_sem, recv_sem):
    domain = lax.axis_index("dom")
    here = lax.axis_index("yz")
    count = send_ref.shape[0]
    barrier = pltpu.get_barrier_semaphore()
    for partner in range(count):
        pl.semaphore_signal(
            barrier, inc=1, device_id={"dom": 1 - domain, "yz": partner}, device_id_type=MESH
        )
    pl.semaphore_wait(barrier, count)

    @pl.when(domain == 0)
    def _():
        copies = []
        for owner in range(count):
            copy = pltpu.make_async_remote_copy(
                src_ref=send_ref.at[owner],
                dst_ref=landed.at[here],
                send_sem=send_sem.at[owner],
                recv_sem=recv_sem.at[here],
                device_id={"dom": 1, "yz": owner},
                device_id_type=MESH,
            )
            copy.start()
            copies.append(copy)
        for copy in copies:
            copy.wait_send()
        out_ref[...] = jnp.zeros_like(out_ref)

    @pl.when(domain == 1)
    def _():
        for sender in range(count):
            pltpu.make_async_remote_copy(
                src_ref=send_ref.at[sender],
                dst_ref=landed.at[sender],
                send_sem=send_sem.at[sender],
                recv_sem=recv_sem.at[sender],
                device_id={"dom": 0, "yz": sender},
                device_id_type=MESH,
            ).wait_recv()
        out_ref[...] = landed[...]


def route_blocks(send_cells):
    count = send_cells.shape[0]
    return pl.pallas_call(
        route_kernel,
        out_shape=jax.ShapeDtypeStruct(send_cells.shape, send_cells.dtype),
        in_specs=[pl.BlockSpec(memory_space=pltpu.VMEM)],
        out_specs=pl.BlockSpec(memory_space=pltpu.VMEM),
        scratch_shapes=[
            pltpu.VMEM(send_cells.shape, send_cells.dtype),
            pltpu.SemaphoreType.DMA((count,)),
            pltpu.SemaphoreType.DMA((count,)),
        ],
        compiler_params=pltpu.CompilerParams(collective_id=0, has_side_effects=True),
    )(send_cells)


def halo_kernel(grid_ref, out_ref, landed, send_sem, recv_sem):
    column = lax.axis_index("gx")
    row = lax.axis_index("yz")
    gx_count = lax.axis_size("gx")
    yz_count = lax.axis_size("yz")
    len_x, len_y = grid_ref.shape[1], grid_ref.shape[2]
    up_x = {"gx": lax.rem(column + 1, gx_count)}
    down_x = {"gx": lax.rem(column + gx_count - 1, gx_count)}
    up_y = {"yz": lax.rem(row + 1, yz_count)}
    down_y = {"yz": lax.rem(row + yz_count - 1, yz_count)}
    barrier = pltpu.get_barrier_semaphore()
    for partner in (up_x, down_x, up_y, down_y):
        pl.semaphore_signal(barrier, inc=1, device_id=partner, device_id_type=MESH)
    pl.semaphore_wait(barrier, 4)
    sends = (
        (grid_ref.at[:, len_x - 1], up_x),
        (grid_ref.at[:, 0], down_x),
        (grid_ref.at[:, :, len_y - 1], up_y),
        (grid_ref.at[:, :, 0], down_y),
    )
    copies = []
    for slot, (source, partner) in enumerate(sends):
        copy = pltpu.make_async_remote_copy(
            src_ref=source,
            dst_ref=landed.at[slot],
            send_sem=send_sem.at[slot],
            recv_sem=recv_sem.at[slot],
            device_id=partner,
            device_id_type=MESH,
        )
        copy.start()
        copies.append(copy)
    for copy in copies:
        copy.wait()
    out_ref[...] = landed[...]


def exchange_faces(grid_cells):
    ncomp, len_x, len_y, len_z = grid_cells.shape
    face = (4, ncomp, len_x, len_z)
    return pl.pallas_call(
        halo_kernel,
        out_shape=jax.ShapeDtypeStruct(face, grid_cells.dtype),
        in_specs=[pl.BlockSpec(memory_space=pltpu.VMEM)],
        out_specs=pl.BlockSpec(memory_space=pltpu.VMEM),
        scratch_shapes=[
            pltpu.VMEM(face, grid_cells.dtype),
            pltpu.SemaphoreType.DMA((4,)),
            pltpu.SemaphoreType.DMA((4,)),
        ],
        compiler_params=pltpu.CompilerParams(collective_id=1, has_side_effects=True),
    )(grid_cells)


def local(field_state, shell_owner, block_sources, block_targets, interp_weights):
    grid_cells = field_state[0]
    ncomp, len_x, len_y, len_z = grid_cells.shape
    domain = lax.axis_index("dom")
    column = lax.axis_index("gx")
    yz_index = lax.axis_index("yz")
    gx_count = lax.axis_size("gx")
    yz_count = lax.axis_size("yz")
    per_y = len_y // BLK
    per_z = len_z // BLK
    volume = BLK * BLK * BLK
    shell_cells = grid_cells[:, :, :, len_z - SR * BLK :]
    shell_cells = shell_cells.reshape(ncomp, len_x // BLK, BLK, per_y, BLK, SR, BLK)
    shell_cells = (
        shell_cells.transpose(1, 3, 5, 0, 2, 4, 6).reshape(-1, ncomp * volume).astype(jnp.bfloat16)
    )
    count_here = shell_cells.shape[0]
    owner_table = shell_owner[0]
    own_owner = lax.dynamic_index_in_dim(owner_table, yz_index, 0, keepdims=False)
    index_here = jnp.arange(count_here, dtype=jnp.int32)
    local_same = own_owner[None, :] == own_owner[:, None]
    rank_local = jnp.sum(
        (local_same & (index_here[None, :] < index_here[:, None])).astype(jnp.int32), axis=1
    )
    slot_of = own_owner * CAP + rank_local
    slot_count = yz_count * CAP
    select = jnp.arange(slot_count, dtype=jnp.int32)[:, None] == slot_of[None, :]
    send_cells = jnp.dot(
        select.astype(jnp.bfloat16), shell_cells, preferred_element_type=jnp.float32
    )
    send_cells = send_cells.astype(jnp.bfloat16).reshape(yz_count, CAP * ncomp, volume)
    got_cells = route_blocks(send_cells).reshape(slot_count, ncomp * volume)
    mine = (owner_table == yz_index).astype(jnp.int32)
    per_sender = jnp.sum(mine, axis=1)
    before = jnp.cumsum(per_sender) - per_sender
    rank_slot = jnp.arange(CAP, dtype=jnp.int32)
    got_tags = jnp.where(
        rank_slot[None, :] < per_sender[:, None], before[:, None] + rank_slot[None, :], -1
    ).reshape(slot_count)
    wanted = block_sources[0, 0].reshape(-1)
    match_table = (wanted[:, None] == got_tags[None, :]) & (wanted[:, None] >= 0)
    picked = jnp.dot(
        match_table.astype(jnp.bfloat16), got_cells, preferred_element_type=jnp.float32
    )
    slots_here = block_targets.shape[2]
    picked = picked.astype(jnp.bfloat16).reshape(slots_here, -1, ncomp, volume)
    interp_blocks = jnp.einsum(
        "jkcs,jkst->jct", picked, interp_weights[0, 0], preferred_element_type=jnp.float32
    )

    rows = lax.broadcasted_iota(jnp.int32, (len_x, len_y, len_z), 0) // BLK
    cols = lax.broadcasted_iota(jnp.int32, (len_x, len_y, len_z), 1) // BLK
    lanes = lax.broadcasted_iota(jnp.int32, (len_x, len_y, len_z), 2)
    spread_of = lax.broadcasted_iota(jnp.int32, (BLK, len_z), 1) % BLK
    offset_of = lax.broadcasted_iota(jnp.int32, (BLK, len_z), 0)
    spread = (spread_of == offset_of).astype(jnp.float32)
    stacked = interp_blocks.reshape(slots_here * ncomp * BLK * BLK, BLK)
    stacked = jnp.dot(stacked, spread, precision=lax.Precision.HIGHEST)
    stacked = stacked.reshape(slots_here, ncomp, BLK, BLK, len_z)
    targets = jnp.where(domain == 1, block_targets[0, 0], -1)
    spots = jnp.maximum(targets, 0)
    hit = (
        (rows[None] == (spots // (per_y * per_z))[:, None, None, None])
        & (cols[None] == (spots // per_z % per_y)[:, None, None, None])
        & (lanes[None] // BLK == (spots % per_z)[:, None, None, None])
        & (targets >= 0)[:, None, None, None]
    )
    for slot_number in range(slots_here):
        placed = jnp.tile(stacked[slot_number], (1, len_x // BLK, len_y // BLK, 1))
        grid_cells = jnp.where(hit[slot_number][None], placed, grid_cells)

    helio_side = domain == 1
    low_x = helio_side & (column == 0)
    high_x = helio_side & (column == gx_count - 1)
    low_y = yz_index == 0
    high_y = yz_index == yz_count - 1
    ghosts = exchange_faces(grid_cells)
    from_low_x, from_high_x, from_low_y, from_high_y = (
        lax.expand_dims(ghosts[0], (1,)),
        lax.expand_dims(ghosts[1], (1,)),
        lax.expand_dims(ghosts[2], (2,)),
        lax.expand_dims(ghosts[3], (2,)),
    )
    head_x, tail_x = grid_cells[:, :1], grid_cells[:, -1:]
    head_y, tail_y = grid_cells[:, :, :1], grid_cells[:, :, -1:]
    line_x = jnp.concatenate(
        [jnp.where(low_x, head_x, from_low_x), grid_cells, jnp.where(high_x, tail_x, from_high_x)],
        axis=1,
    )
    line_y = jnp.concatenate(
        [jnp.where(low_y, head_y, from_low_y), grid_cells, jnp.where(high_y, tail_y, from_high_y)],
        axis=2,
    )
    line_z = jnp.pad(grid_cells, ((0, 0), (0, 0), (0, 0), (1, 1)), mode="edge")
    step_ratio = jnp.where(domain == 0, CORONA_RATIO, HELIO_RATIO).astype(jnp.float32)
    updated = advance((line_x, line_y, line_z), grid_cells, step_ratio)
    return updated[None]


def solution(mesh):
    placed = (
        P("dom", None, "gx", "yz", None),
        P("gx", None, None),
        P("gx", "yz", None, None),
        P("gx", "yz", None),
        P("gx", "yz", None, None, None, None),
    )
    return jax.shard_map(
        local,
        mesh=mesh,
        in_specs=placed,
        out_specs=P("dom", None, "gx", "yz", None),
        check_vma=False,
    )
```

```python
import jax
import jax.numpy as jnp
from jax import lax
from jax.experimental import pallas as pl
from jax.experimental.pallas import tpu as pltpu
from jax.sharding import PartitionSpec as P

MESH = pl.DeviceIdType.MESH

BLK = 8
SR = 2
CAP = 2


HEAT_RATIO = 5.0 / 3.0
CORONA_RATIO = 0.04
HELIO_RATIO = 0.03


def direction_flux(grid_cells, direction):
    density = grid_cells[0]
    momentum = grid_cells[1:4]
    magnetic = grid_cells[4:7]
    energy = grid_cells[7]
    velocity = momentum / density
    field_sq = jnp.sum(magnetic * magnetic, axis=0)
    pressure = (HEAT_RATIO - 1.0) * (
        energy - 0.5 * jnp.sum(momentum * velocity, axis=0) - 0.5 * field_sq
    )
    total_pressure = pressure + 0.5 * field_sq
    normal_speed = velocity[direction]
    normal_field = magnetic[direction]
    velocity_dot = jnp.sum(velocity * magnetic, axis=0)
    flux_list = [momentum[direction]]
    for other in range(3):
        term = momentum[other] * normal_speed - magnetic[other] * normal_field
        if other == direction:
            term = term + total_pressure
        flux_list.append(term)
    for other in range(3):
        flux_list.append(normal_speed * magnetic[other] - normal_field * velocity[other])
    flux_list.append((energy + total_pressure) * normal_speed - normal_field * velocity_dot)
    wave_speed = jnp.abs(normal_speed) + jnp.sqrt((HEAT_RATIO * pressure + field_sq) / density)
    return (jnp.stack(flux_list), wave_speed)


def interface_change(padded_line, direction):
    phys_flux, wave_speed = direction_flux(padded_line, direction)
    array_dim = direction + 1
    cell_count = padded_line.shape[array_dim]
    low_cells = lax.slice_in_dim(padded_line, 0, cell_count - 1, axis=array_dim)
    high_cells = lax.slice_in_dim(padded_line, 1, cell_count, axis=array_dim)
    low_flux = lax.slice_in_dim(phys_flux, 0, cell_count - 1, axis=array_dim)
    high_flux = lax.slice_in_dim(phys_flux, 1, cell_count, axis=array_dim)
    low_speed = lax.slice_in_dim(wave_speed, 0, cell_count - 1, axis=direction)
    high_speed = lax.slice_in_dim(wave_speed, 1, cell_count, axis=direction)
    fastest = jnp.maximum(low_speed, high_speed)
    face_flux = 0.5 * (low_flux + high_flux) - 0.5 * fastest[None] * (high_cells - low_cells)
    upper_face = lax.slice_in_dim(face_flux, 1, cell_count - 1, axis=array_dim)
    lower_face = lax.slice_in_dim(face_flux, 0, cell_count - 2, axis=array_dim)
    return upper_face - lower_face


def advance(line_set, inner_cells, step_ratio):
    change = interface_change(line_set[0], 0) + interface_change(line_set[1], 1)
    change = change + interface_change(line_set[2], 2)
    return inner_cells - step_ratio * change


def route_kernel(send_ref, out_ref, landed, send_sem, recv_sem):
    domain = lax.axis_index("dom")
    here = lax.axis_index("yz")
    count = send_ref.shape[0]
    barrier = pltpu.get_barrier_semaphore()
    for partner in range(count):
        pl.semaphore_signal(
            barrier, inc=1, device_id={"dom": 1 - domain, "yz": partner}, device_id_type=MESH
        )
    pl.semaphore_wait(barrier, count)

    @pl.when(domain == 0)
    def _():
        copies = []
        for owner in range(count):
            copy = pltpu.make_async_remote_copy(
                src_ref=send_ref.at[owner],
                dst_ref=landed.at[here],
                send_sem=send_sem.at[owner],
                recv_sem=recv_sem.at[here],
                device_id={"dom": 1, "yz": owner},
                device_id_type=MESH,
            )
            copy.start()
            copies.append(copy)
        for copy in copies:
            copy.wait_send()
        out_ref[...] = jnp.zeros_like(out_ref)

    @pl.when(domain == 1)
    def _():
        for sender in range(count):
            pltpu.make_async_remote_copy(
                src_ref=send_ref.at[sender],
                dst_ref=landed.at[sender],
                send_sem=send_sem.at[sender],
                recv_sem=recv_sem.at[sender],
                device_id={"dom": 0, "yz": sender},
                device_id_type=MESH,
            ).wait_recv()
        out_ref[...] = landed[...]


def route_blocks(send_cells):
    count = send_cells.shape[0]
    return pl.pallas_call(
        route_kernel,
        out_shape=jax.ShapeDtypeStruct(send_cells.shape, send_cells.dtype),
        in_specs=[pl.BlockSpec(memory_space=pltpu.VMEM)],
        out_specs=pl.BlockSpec(memory_space=pltpu.VMEM),
        scratch_shapes=[
            pltpu.VMEM(send_cells.shape, send_cells.dtype),
            pltpu.SemaphoreType.DMA((count,)),
            pltpu.SemaphoreType.DMA((count,)),
        ],
        compiler_params=pltpu.CompilerParams(collective_id=0, has_side_effects=True),
    )(send_cells)


def ghost_pair(cells, axis, dim, wrap, fix_low, fix_high):
    count = lax.axis_size(axis)
    size = cells.shape[dim]
    head = lax.slice_in_dim(cells, 0, 1, axis=dim)
    tail = lax.slice_in_dim(cells, size - 1, size, axis=dim)
    up = [(i, i + 1) for i in range(count - 1)]
    down = [(i + 1, i) for i in range(count - 1)]
    if wrap:
        up.append((count - 1, 0))
        down.append((0, count - 1))
    from_low = lax.ppermute(tail, axis, up)
    from_high = lax.ppermute(head, axis, down)
    low = jnp.where(fix_low, head, from_low)
    high = jnp.where(fix_high, tail, from_high)
    return jnp.concatenate([low, cells, high], axis=dim)


def local(field_state, shell_owner, block_sources, block_targets, interp_weights):
    grid_cells = field_state[0]
    ncomp, len_x, len_y, len_z = grid_cells.shape
    domain = lax.axis_index("dom")
    column = lax.axis_index("gx")
    yz_index = lax.axis_index("yz")
    gx_count = lax.axis_size("gx")
    yz_count = lax.axis_size("yz")
    per_y = len_y // BLK
    per_z = len_z // BLK
    volume = BLK * BLK * BLK
    shell_cells = grid_cells[:, :, :, len_z - SR * BLK :]
    shell_cells = shell_cells.reshape(ncomp, len_x // BLK, BLK, per_y, BLK, SR, BLK)
    shell_cells = (
        shell_cells.transpose(1, 3, 5, 0, 2, 4, 6).reshape(-1, ncomp * volume).astype(jnp.bfloat16)
    )
    count_here = shell_cells.shape[0]
    owner_table = shell_owner[0]
    own_owner = lax.dynamic_index_in_dim(owner_table, yz_index, 0, keepdims=False)
    index_here = jnp.arange(count_here, dtype=jnp.int32)
    local_same = own_owner[None, :] == own_owner[:, None]
    rank_local = jnp.sum(
        (local_same & (index_here[None, :] < index_here[:, None])).astype(jnp.int32), axis=1
    )
    slot_of = own_owner * CAP + rank_local
    slot_count = yz_count * CAP
    select = jnp.arange(slot_count, dtype=jnp.int32)[:, None] == slot_of[None, :]
    send_cells = jnp.dot(
        select.astype(jnp.bfloat16), shell_cells, preferred_element_type=jnp.float32
    )
    send_cells = send_cells.astype(jnp.bfloat16).reshape(yz_count, CAP * ncomp, volume)
    got_cells = route_blocks(send_cells).reshape(slot_count, ncomp * volume)
    mine = (owner_table == yz_index).astype(jnp.int32)
    per_sender = jnp.sum(mine, axis=1)
    before = jnp.cumsum(per_sender) - per_sender
    rank_slot = jnp.arange(CAP, dtype=jnp.int32)
    got_tags = jnp.where(
        rank_slot[None, :] < per_sender[:, None], before[:, None] + rank_slot[None, :], -1
    ).reshape(slot_count)
    wanted = block_sources[0, 0].reshape(-1)
    match_table = (wanted[:, None] == got_tags[None, :]) & (wanted[:, None] >= 0)
    picked = jnp.dot(
        match_table.astype(jnp.bfloat16), got_cells, preferred_element_type=jnp.float32
    )
    slots_here = block_targets.shape[2]
    picked = picked.astype(jnp.bfloat16).reshape(slots_here, -1, ncomp, volume)
    interp_blocks = jnp.einsum(
        "jkcs,jkst->jct", picked, interp_weights[0, 0], preferred_element_type=jnp.float32
    )

    rows = lax.broadcasted_iota(jnp.int32, (len_x, len_y, len_z), 0) // BLK
    cols = lax.broadcasted_iota(jnp.int32, (len_x, len_y, len_z), 1) // BLK
    lanes = lax.broadcasted_iota(jnp.int32, (len_x, len_y, len_z), 2)
    spread_of = lax.broadcasted_iota(jnp.int32, (BLK, len_z), 1) % BLK
    offset_of = lax.broadcasted_iota(jnp.int32, (BLK, len_z), 0)
    spread = (spread_of == offset_of).astype(jnp.float32)
    stacked = interp_blocks.reshape(slots_here * ncomp * BLK * BLK, BLK)
    stacked = jnp.dot(stacked, spread, precision=lax.Precision.HIGHEST)
    stacked = stacked.reshape(slots_here, ncomp, BLK, BLK, len_z)
    targets = jnp.where(domain == 1, block_targets[0, 0], -1)
    spots = jnp.maximum(targets, 0)
    hit = (
        (rows[None] == (spots // (per_y * per_z))[:, None, None, None])
        & (cols[None] == (spots // per_z % per_y)[:, None, None, None])
        & (lanes[None] // BLK == (spots % per_z)[:, None, None, None])
        & (targets >= 0)[:, None, None, None]
    )
    for slot_number in range(slots_here):
        placed = jnp.tile(stacked[slot_number], (1, len_x // BLK, len_y // BLK, 1))
        grid_cells = jnp.where(hit[slot_number][None], placed, grid_cells)

    helio_side = domain == 1
    low_x = helio_side & (column == 0)
    high_x = helio_side & (column == gx_count - 1)
    low_y = yz_index == 0
    high_y = yz_index == yz_count - 1
    line_x = ghost_pair(grid_cells, "gx", 1, True, low_x, high_x)
    line_y = ghost_pair(grid_cells, "yz", 2, False, low_y, high_y)
    line_z = jnp.pad(grid_cells, ((0, 0), (0, 0), (0, 0), (1, 1)), mode="edge")
    step_ratio = jnp.where(domain == 0, CORONA_RATIO, HELIO_RATIO).astype(jnp.float32)
    updated = advance((line_x, line_y, line_z), grid_cells, step_ratio)
    return updated[None]


def solution(mesh):
    placed = (
        P("dom", None, "gx", "yz", None),
        P("gx", None, None),
        P("gx", "yz", None, None),
        P("gx", "yz", None),
        P("gx", "yz", None, None, None, None),
    )
    return jax.shard_map(
        local,
        mesh=mesh,
        in_specs=placed,
        out_specs=P("dom", None, "gx", "yz", None),
        check_vma=False,
    )
```

```python
import jax
import jax.numpy as jnp
from jax import lax
from jax.experimental import pallas as pl
from jax.experimental.pallas import tpu as pltpu
from jax.sharding import PartitionSpec as P

MESH = pl.DeviceIdType.MESH

BLK = 8
SR = 2
CAP = 2


HEAT_RATIO = 5.0 / 3.0
CORONA_RATIO = 0.04
HELIO_RATIO = 0.03


def direction_flux(grid_cells, direction):
    density = grid_cells[0]
    momentum = grid_cells[1:4]
    magnetic = grid_cells[4:7]
    energy = grid_cells[7]
    velocity = momentum / density
    field_sq = jnp.sum(magnetic * magnetic, axis=0)
    pressure = (HEAT_RATIO - 1.0) * (
        energy - 0.5 * jnp.sum(momentum * velocity, axis=0) - 0.5 * field_sq
    )
    total_pressure = pressure + 0.5 * field_sq
    normal_speed = velocity[direction]
    normal_field = magnetic[direction]
    velocity_dot = jnp.sum(velocity * magnetic, axis=0)
    flux_list = [momentum[direction]]
    for other in range(3):
        term = momentum[other] * normal_speed - magnetic[other] * normal_field
        if other == direction:
            term = term + total_pressure
        flux_list.append(term)
    for other in range(3):
        flux_list.append(normal_speed * magnetic[other] - normal_field * velocity[other])
    flux_list.append((energy + total_pressure) * normal_speed - normal_field * velocity_dot)
    wave_speed = jnp.abs(normal_speed) + jnp.sqrt((HEAT_RATIO * pressure + field_sq) / density)
    return (jnp.stack(flux_list), wave_speed)


def interface_change(padded_line, direction):
    phys_flux, wave_speed = direction_flux(padded_line, direction)
    array_dim = direction + 1
    cell_count = padded_line.shape[array_dim]
    low_cells = lax.slice_in_dim(padded_line, 0, cell_count - 1, axis=array_dim)
    high_cells = lax.slice_in_dim(padded_line, 1, cell_count, axis=array_dim)
    low_flux = lax.slice_in_dim(phys_flux, 0, cell_count - 1, axis=array_dim)
    high_flux = lax.slice_in_dim(phys_flux, 1, cell_count, axis=array_dim)
    low_speed = lax.slice_in_dim(wave_speed, 0, cell_count - 1, axis=direction)
    high_speed = lax.slice_in_dim(wave_speed, 1, cell_count, axis=direction)
    fastest = jnp.maximum(low_speed, high_speed)
    face_flux = 0.5 * (low_flux + high_flux) - 0.5 * fastest[None] * (high_cells - low_cells)
    upper_face = lax.slice_in_dim(face_flux, 1, cell_count - 1, axis=array_dim)
    lower_face = lax.slice_in_dim(face_flux, 0, cell_count - 2, axis=array_dim)
    return upper_face - lower_face


def advance(line_set, inner_cells, step_ratio):
    change = interface_change(line_set[0], 0) + interface_change(line_set[1], 1)
    change = change + interface_change(line_set[2], 2)
    return inner_cells - step_ratio * change


def route_kernel(send_ref, out_ref, landed, send_sem, recv_sem):
    domain = lax.axis_index("dom")
    here = lax.axis_index("yz")
    count = send_ref.shape[0]
    barrier = pltpu.get_barrier_semaphore()
    for partner in range(count):
        pl.semaphore_signal(
            barrier, inc=1, device_id={"dom": 1 - domain, "yz": partner}, device_id_type=MESH
        )
    pl.semaphore_wait(barrier, count)

    @pl.when(domain == 0)
    def _():
        copies = []
        for owner in range(count):
            copy = pltpu.make_async_remote_copy(
                src_ref=send_ref.at[owner],
                dst_ref=landed.at[here],
                send_sem=send_sem.at[owner],
                recv_sem=recv_sem.at[here],
                device_id={"dom": 1, "yz": owner},
                device_id_type=MESH,
            )
            copy.start()
            copies.append(copy)
        for copy in copies:
            copy.wait_send()
        out_ref[...] = jnp.zeros_like(out_ref)

    @pl.when(domain == 1)
    def _():
        for sender in range(count):
            pltpu.make_async_remote_copy(
                src_ref=send_ref.at[sender],
                dst_ref=landed.at[sender],
                send_sem=send_sem.at[sender],
                recv_sem=recv_sem.at[sender],
                device_id={"dom": 0, "yz": sender},
                device_id_type=MESH,
            ).wait_recv()
        out_ref[...] = landed[...]


def route_blocks(send_cells):
    count = send_cells.shape[0]
    return pl.pallas_call(
        route_kernel,
        out_shape=jax.ShapeDtypeStruct(send_cells.shape, send_cells.dtype),
        in_specs=[pl.BlockSpec(memory_space=pltpu.VMEM)],
        out_specs=pl.BlockSpec(memory_space=pltpu.VMEM),
        scratch_shapes=[
            pltpu.VMEM(send_cells.shape, send_cells.dtype),
            pltpu.SemaphoreType.DMA((count,)),
            pltpu.SemaphoreType.DMA((count,)),
        ],
        compiler_params=pltpu.CompilerParams(collective_id=0, has_side_effects=True),
    )(send_cells)


def ghost_pair(cells, axis, dim, wrap, fix_low, fix_high):
    count = lax.axis_size(axis)
    size = cells.shape[dim]
    head = lax.slice_in_dim(cells, 0, 1, axis=dim)
    tail = lax.slice_in_dim(cells, size - 1, size, axis=dim)
    up = [(i, i + 1) for i in range(count - 1)]
    down = [(i + 1, i) for i in range(count - 1)]
    if wrap:
        up.append((count - 1, 0))
        down.append((0, count - 1))
    from_low = lax.ppermute(tail, axis, up)
    from_high = lax.ppermute(head, axis, down)
    low = jnp.where(fix_low, head, from_low)
    high = jnp.where(fix_high, tail, from_high)
    return lax.squeeze(low, (dim,)), lax.squeeze(high, (dim,))


def cell_flux(parts, direction):
    density = parts[0]
    momentum = parts[1:4]
    magnetic = parts[4:7]
    energy = parts[7]
    velocity = [m / density for m in momentum]
    field_sq = magnetic[0] * magnetic[0] + magnetic[1] * magnetic[1] + magnetic[2] * magnetic[2]
    kinetic = momentum[0] * velocity[0] + momentum[1] * velocity[1] + momentum[2] * velocity[2]
    pressure = (HEAT_RATIO - 1.0) * (energy - 0.5 * kinetic - 0.5 * field_sq)
    total_pressure = pressure + 0.5 * field_sq
    normal_speed = velocity[direction]
    normal_field = magnetic[direction]
    velocity_dot = velocity[0] * magnetic[0] + velocity[1] * magnetic[1] + velocity[2] * magnetic[2]
    flux = [momentum[direction]]
    for other in range(3):
        term = momentum[other] * normal_speed - magnetic[other] * normal_field
        if other == direction:
            term = term + total_pressure
        flux.append(term)
    for other in range(3):
        flux.append(normal_speed * magnetic[other] - normal_field * velocity[other])
    flux.append((energy + total_pressure) * normal_speed - normal_field * velocity_dot)
    speed = jnp.abs(normal_speed) + jnp.sqrt((HEAT_RATIO * pressure + field_sq) / density)
    return flux, speed


def face_change(low, mid, high, low_flux, mid_flux, high_flux):
    (fl, sl), (fm, sm), (fh, sh) = low_flux, mid_flux, high_flux
    fast_low = jnp.maximum(sl, sm)
    fast_high = jnp.maximum(sm, sh)
    change = []
    for c in range(len(mid)):
        upper = 0.5 * (fm[c] + fh[c]) - 0.5 * fast_high * (high[c] - mid[c])
        lower = 0.5 * (fl[c] + fm[c]) - 0.5 * fast_low * (mid[c] - low[c])
        change.append(upper - lower)
    return change


def stencil_kernel(grid_ref, low_x_ref, high_x_ref, low_y_ref, high_y_ref, out_ref):
    ncomp, len_x, len_y, len_z = grid_ref.shape
    domain = lax.axis_index("dom")
    ratio = jnp.where(domain == 0, CORONA_RATIO, HELIO_RATIO).astype(jnp.float32)
    rows = lax.broadcasted_iota(jnp.int32, (len_y, len_z), 0)
    lanes = lax.broadcasted_iota(jnp.int32, (len_y, len_z), 1)

    def plane(x):
        if x < 0:
            return [low_x_ref[c] for c in range(ncomp)]
        if x >= len_x:
            return [high_x_ref[c] for c in range(ncomp)]
        return [grid_ref[c, x] for c in range(ncomp)]

    def shift(values, edge, step, axis, index, last):
        moved = pltpu.roll(values, step, axis)
        return jnp.where(index == last, edge, moved)

    low = plane(-1)
    mid = plane(0)
    low_flux = cell_flux(low, 0)
    mid_flux = cell_flux(mid, 0)
    for x in range(len_x):
        high = plane(x + 1)
        high_flux = cell_flux(high, 0)
        change = face_change(low, mid, high, low_flux, mid_flux, high_flux)
        y_low = [low_y_ref[c, pl.ds(x, 1), :] for c in range(ncomp)]
        y_high = [high_y_ref[c, pl.ds(x, 1), :] for c in range(ncomp)]
        y_flux = cell_flux(mid, 1)
        y_low_flux = cell_flux(y_low, 1)
        y_high_flux = cell_flux(y_high, 1)
        down = [shift(mid[c], y_low[c], 1, 0, rows, 0) for c in range(ncomp)]
        up = [shift(mid[c], y_high[c], len_y - 1, 0, rows, len_y - 1) for c in range(ncomp)]
        down_flux = (
            [shift(y_flux[0][c], y_low_flux[0][c], 1, 0, rows, 0) for c in range(ncomp)],
            shift(y_flux[1], y_low_flux[1], 1, 0, rows, 0),
        )
        up_flux = (
            [shift(y_flux[0][c], y_high_flux[0][c], len_y - 1, 0, rows, len_y - 1) for c in range(ncomp)],
            shift(y_flux[1], y_high_flux[1], len_y - 1, 0, rows, len_y - 1),
        )
        change_y = face_change(down, mid, up, down_flux, y_flux, up_flux)
        z_flux = cell_flux(mid, 2)
        back = [shift(mid[c], mid[c], 1, 1, lanes, 0) for c in range(ncomp)]
        front = [shift(mid[c], mid[c], len_z - 1, 1, lanes, len_z - 1) for c in range(ncomp)]
        back_flux = (
            [shift(z_flux[0][c], z_flux[0][c], 1, 1, lanes, 0) for c in range(ncomp)],
            shift(z_flux[1], z_flux[1], 1, 1, lanes, 0),
        )
        front_flux = (
            [shift(z_flux[0][c], z_flux[0][c], len_z - 1, 1, lanes, len_z - 1) for c in range(ncomp)],
            shift(z_flux[1], z_flux[1], len_z - 1, 1, lanes, len_z - 1),
        )
        change_z = face_change(back, mid, front, back_flux, z_flux, front_flux)
        for c in range(ncomp):
            total = change[c] + change_y[c]
            total = total + change_z[c]
            out_ref[c, x] = mid[c] - ratio * total
        low, mid = mid, high
        low_flux, mid_flux = mid_flux, high_flux


def stencil(grid_cells, low_x, high_x, low_y, high_y):
    vmem = pl.BlockSpec(memory_space=pltpu.VMEM)
    return pl.pallas_call(
        stencil_kernel,
        out_shape=jax.ShapeDtypeStruct(grid_cells.shape, grid_cells.dtype),
        in_specs=[vmem] * 5,
        out_specs=vmem,
    )(grid_cells, low_x, high_x, low_y, high_y)


def local(field_state, shell_owner, block_sources, block_targets, interp_weights):
    grid_cells = field_state[0]
    ncomp, len_x, len_y, len_z = grid_cells.shape
    domain = lax.axis_index("dom")
    column = lax.axis_index("gx")
    yz_index = lax.axis_index("yz")
    gx_count = lax.axis_size("gx")
    yz_count = lax.axis_size("yz")
    per_y = len_y // BLK
    per_z = len_z // BLK
    volume = BLK * BLK * BLK
    shell_cells = grid_cells[:, :, :, len_z - SR * BLK :]
    shell_cells = shell_cells.reshape(ncomp, len_x // BLK, BLK, per_y, BLK, SR, BLK)
    shell_cells = (
        shell_cells.transpose(1, 3, 5, 0, 2, 4, 6).reshape(-1, ncomp * volume).astype(jnp.bfloat16)
    )
    count_here = shell_cells.shape[0]
    owner_table = shell_owner[0]
    own_owner = lax.dynamic_index_in_dim(owner_table, yz_index, 0, keepdims=False)
    index_here = jnp.arange(count_here, dtype=jnp.int32)
    local_same = own_owner[None, :] == own_owner[:, None]
    rank_local = jnp.sum(
        (local_same & (index_here[None, :] < index_here[:, None])).astype(jnp.int32), axis=1
    )
    slot_of = own_owner * CAP + rank_local
    slot_count = yz_count * CAP
    select = jnp.arange(slot_count, dtype=jnp.int32)[:, None] == slot_of[None, :]
    send_cells = jnp.dot(
        select.astype(jnp.bfloat16), shell_cells, preferred_element_type=jnp.float32
    )
    send_cells = send_cells.astype(jnp.bfloat16).reshape(yz_count, CAP * ncomp, volume)
    got_cells = route_blocks(send_cells).reshape(slot_count, ncomp * volume)
    mine = (owner_table == yz_index).astype(jnp.int32)
    per_sender = jnp.sum(mine, axis=1)
    before = jnp.cumsum(per_sender) - per_sender
    rank_slot = jnp.arange(CAP, dtype=jnp.int32)
    got_tags = jnp.where(
        rank_slot[None, :] < per_sender[:, None], before[:, None] + rank_slot[None, :], -1
    ).reshape(slot_count)
    wanted = block_sources[0, 0].reshape(-1)
    match_table = (wanted[:, None] == got_tags[None, :]) & (wanted[:, None] >= 0)
    picked = jnp.dot(
        match_table.astype(jnp.bfloat16), got_cells, preferred_element_type=jnp.float32
    )
    slots_here = block_targets.shape[2]
    picked = picked.astype(jnp.bfloat16).reshape(slots_here, -1, ncomp, volume)
    interp_blocks = jnp.einsum(
        "jkcs,jkst->jct", picked, interp_weights[0, 0], preferred_element_type=jnp.float32
    )

    rows = lax.broadcasted_iota(jnp.int32, (len_x, len_y, len_z), 0) // BLK
    cols = lax.broadcasted_iota(jnp.int32, (len_x, len_y, len_z), 1) // BLK
    lanes = lax.broadcasted_iota(jnp.int32, (len_x, len_y, len_z), 2)
    spread_of = lax.broadcasted_iota(jnp.int32, (BLK, len_z), 1) % BLK
    offset_of = lax.broadcasted_iota(jnp.int32, (BLK, len_z), 0)
    spread = (spread_of == offset_of).astype(jnp.float32)
    stacked = interp_blocks.reshape(slots_here * ncomp * BLK * BLK, BLK)
    stacked = jnp.dot(stacked, spread, precision=lax.Precision.HIGHEST)
    stacked = stacked.reshape(slots_here, ncomp, BLK, BLK, len_z)
    targets = jnp.where(domain == 1, block_targets[0, 0], -1)
    spots = jnp.maximum(targets, 0)
    hit = (
        (rows[None] == (spots // (per_y * per_z))[:, None, None, None])
        & (cols[None] == (spots // per_z % per_y)[:, None, None, None])
        & (lanes[None] // BLK == (spots % per_z)[:, None, None, None])
        & (targets >= 0)[:, None, None, None]
    )
    for slot_number in range(slots_here):
        placed = jnp.tile(stacked[slot_number], (1, len_x // BLK, len_y // BLK, 1))
        grid_cells = jnp.where(hit[slot_number][None], placed, grid_cells)

    helio_side = domain == 1
    low_x = helio_side & (column == 0)
    high_x = helio_side & (column == gx_count - 1)
    low_y = yz_index == 0
    high_y = yz_index == yz_count - 1
    ghost_low_x, ghost_high_x = ghost_pair(grid_cells, "gx", 1, True, low_x, high_x)
    ghost_low_y, ghost_high_y = ghost_pair(grid_cells, "yz", 2, False, low_y, high_y)
    updated = stencil(grid_cells, ghost_low_x, ghost_high_x, ghost_low_y, ghost_high_y)
    return updated[None]


def solution(mesh):
    placed = (
        P("dom", None, "gx", "yz", None),
        P("gx", None, None),
        P("gx", "yz", None, None),
        P("gx", "yz", None),
        P("gx", "yz", None, None, None, None),
    )
    return jax.shard_map(
        local,
        mesh=mesh,
        in_specs=placed,
        out_specs=P("dom", None, "gx", "yz", None),
        check_vma=False,
    )
```

```python
import jax
import jax.numpy as jnp
from jax import lax
from jax.experimental import pallas as pl
from jax.experimental.pallas import tpu as pltpu
from jax.sharding import PartitionSpec as P

MESH = pl.DeviceIdType.MESH

BLK = 8
SR = 2
CAP = 2


HEAT_RATIO = 5.0 / 3.0
CORONA_RATIO = 0.04
HELIO_RATIO = 0.03


def direction_flux(grid_cells, direction):
    density = grid_cells[0]
    momentum = grid_cells[1:4]
    magnetic = grid_cells[4:7]
    energy = grid_cells[7]
    velocity = momentum / density
    field_sq = jnp.sum(magnetic * magnetic, axis=0)
    pressure = (HEAT_RATIO - 1.0) * (
        energy - 0.5 * jnp.sum(momentum * velocity, axis=0) - 0.5 * field_sq
    )
    total_pressure = pressure + 0.5 * field_sq
    normal_speed = velocity[direction]
    normal_field = magnetic[direction]
    velocity_dot = jnp.sum(velocity * magnetic, axis=0)
    flux_list = [momentum[direction]]
    for other in range(3):
        term = momentum[other] * normal_speed - magnetic[other] * normal_field
        if other == direction:
            term = term + total_pressure
        flux_list.append(term)
    for other in range(3):
        flux_list.append(normal_speed * magnetic[other] - normal_field * velocity[other])
    flux_list.append((energy + total_pressure) * normal_speed - normal_field * velocity_dot)
    wave_speed = jnp.abs(normal_speed) + jnp.sqrt((HEAT_RATIO * pressure + field_sq) / density)
    return (jnp.stack(flux_list), wave_speed)


def interface_change(padded_line, direction):
    phys_flux, wave_speed = direction_flux(padded_line, direction)
    array_dim = direction + 1
    cell_count = padded_line.shape[array_dim]
    low_cells = lax.slice_in_dim(padded_line, 0, cell_count - 1, axis=array_dim)
    high_cells = lax.slice_in_dim(padded_line, 1, cell_count, axis=array_dim)
    low_flux = lax.slice_in_dim(phys_flux, 0, cell_count - 1, axis=array_dim)
    high_flux = lax.slice_in_dim(phys_flux, 1, cell_count, axis=array_dim)
    low_speed = lax.slice_in_dim(wave_speed, 0, cell_count - 1, axis=direction)
    high_speed = lax.slice_in_dim(wave_speed, 1, cell_count, axis=direction)
    fastest = jnp.maximum(low_speed, high_speed)
    face_flux = 0.5 * (low_flux + high_flux) - 0.5 * fastest[None] * (high_cells - low_cells)
    upper_face = lax.slice_in_dim(face_flux, 1, cell_count - 1, axis=array_dim)
    lower_face = lax.slice_in_dim(face_flux, 0, cell_count - 2, axis=array_dim)
    return upper_face - lower_face


def advance(line_set, inner_cells, step_ratio):
    change = interface_change(line_set[0], 0) + interface_change(line_set[1], 1)
    change = change + interface_change(line_set[2], 2)
    return inner_cells - step_ratio * change


def route_kernel(send_ref, out_ref, landed, send_sem, recv_sem):
    domain = lax.axis_index("dom")
    here = lax.axis_index("yz")
    count = send_ref.shape[0]
    barrier = pltpu.get_barrier_semaphore()
    for partner in range(count):
        pl.semaphore_signal(
            barrier, inc=1, device_id={"dom": 1 - domain, "yz": partner}, device_id_type=MESH
        )
    pl.semaphore_wait(barrier, count)

    @pl.when(domain == 0)
    def _():
        copies = []
        for owner in range(count):
            copy = pltpu.make_async_remote_copy(
                src_ref=send_ref.at[owner],
                dst_ref=landed.at[here],
                send_sem=send_sem.at[owner],
                recv_sem=recv_sem.at[here],
                device_id={"dom": 1, "yz": owner},
                device_id_type=MESH,
            )
            copy.start()
            copies.append(copy)
        for copy in copies:
            copy.wait_send()
        out_ref[...] = jnp.zeros_like(out_ref)

    @pl.when(domain == 1)
    def _():
        for sender in range(count):
            pltpu.make_async_remote_copy(
                src_ref=send_ref.at[sender],
                dst_ref=landed.at[sender],
                send_sem=send_sem.at[sender],
                recv_sem=recv_sem.at[sender],
                device_id={"dom": 0, "yz": sender},
                device_id_type=MESH,
            ).wait_recv()
        out_ref[...] = landed[...]


def route_blocks(send_cells):
    count = send_cells.shape[0]
    return pl.pallas_call(
        route_kernel,
        out_shape=jax.ShapeDtypeStruct(send_cells.shape, send_cells.dtype),
        in_specs=[pl.BlockSpec(memory_space=pltpu.VMEM)],
        out_specs=pl.BlockSpec(memory_space=pltpu.VMEM),
        scratch_shapes=[
            pltpu.VMEM(send_cells.shape, send_cells.dtype),
            pltpu.SemaphoreType.DMA((count,)),
            pltpu.SemaphoreType.DMA((count,)),
        ],
        compiler_params=pltpu.CompilerParams(collective_id=0, has_side_effects=True),
    )(send_cells)


def ghost_pair(head, tail, axis, wrap):
    count = lax.axis_size(axis)
    up = [(i, i + 1) for i in range(count - 1)]
    down = [(i + 1, i) for i in range(count - 1)]
    if wrap:
        up.append((count - 1, 0))
        down.append((0, count - 1))
    return lax.ppermute(tail, axis, up), lax.ppermute(head, axis, down)

def cell_flux(parts, direction):
    density = parts[0]
    momentum = parts[1:4]
    magnetic = parts[4:7]
    energy = parts[7]
    velocity = [m / density for m in momentum]
    field_sq = magnetic[0] * magnetic[0] + magnetic[1] * magnetic[1] + magnetic[2] * magnetic[2]
    kinetic = momentum[0] * velocity[0] + momentum[1] * velocity[1] + momentum[2] * velocity[2]
    pressure = (HEAT_RATIO - 1.0) * (energy - 0.5 * kinetic - 0.5 * field_sq)
    total_pressure = pressure + 0.5 * field_sq
    normal_speed = velocity[direction]
    normal_field = magnetic[direction]
    velocity_dot = velocity[0] * magnetic[0] + velocity[1] * magnetic[1] + velocity[2] * magnetic[2]
    flux = [momentum[direction]]
    for other in range(3):
        term = momentum[other] * normal_speed - magnetic[other] * normal_field
        if other == direction:
            term = term + total_pressure
        flux.append(term)
    for other in range(3):
        flux.append(normal_speed * magnetic[other] - normal_field * velocity[other])
    flux.append((energy + total_pressure) * normal_speed - normal_field * velocity_dot)
    speed = jnp.abs(normal_speed) + jnp.sqrt((HEAT_RATIO * pressure + field_sq) / density)
    return flux, speed


def face_change(low, mid, high, low_flux, mid_flux, high_flux):
    (fl, sl), (fm, sm), (fh, sh) = low_flux, mid_flux, high_flux
    fast_low = jnp.maximum(sl, sm)
    fast_high = jnp.maximum(sm, sh)
    change = []
    for c in range(len(mid)):
        upper = 0.5 * (fm[c] + fh[c]) - 0.5 * fast_high * (high[c] - mid[c])
        lower = 0.5 * (fl[c] + fm[c]) - 0.5 * fast_low * (mid[c] - low[c])
        change.append(upper - lower)
    return change


def stencil_kernel(grid_ref, low_x_ref, high_x_ref, low_y_ref, high_y_ref, out_ref):
    ncomp, len_x, len_y, len_z = grid_ref.shape
    domain = lax.axis_index("dom")
    column = lax.axis_index("gx")
    row = lax.axis_index("yz")
    helio_side = domain == 1
    fix_low_x = helio_side & (column == 0)
    fix_high_x = helio_side & (column == lax.axis_size("gx") - 1)
    fix_low_y = row == 0
    fix_high_y = row == lax.axis_size("yz") - 1
    ratio = jnp.where(domain == 0, CORONA_RATIO, HELIO_RATIO).astype(jnp.float32)
    rows = lax.broadcasted_iota(jnp.int32, (len_y, len_z), 0)
    lanes = lax.broadcasted_iota(jnp.int32, (len_y, len_z), 1)

    def plane(x):
        if x < 0:
            return [jnp.where(fix_low_x, grid_ref[c, 0], low_x_ref[c]) for c in range(ncomp)]
        if x >= len_x:
            return [
                jnp.where(fix_high_x, grid_ref[c, len_x - 1], high_x_ref[c]) for c in range(ncomp)
            ]
        return [grid_ref[c, x] for c in range(ncomp)]

    def shift(values, edge, step, axis, index, last):
        moved = pltpu.roll(values, step, axis)
        return jnp.where(index == last, edge, moved)

    low = plane(-1)
    mid = plane(0)
    low_flux = cell_flux(low, 0)
    mid_flux = cell_flux(mid, 0)
    for x in range(len_x):
        high = plane(x + 1)
        high_flux = cell_flux(high, 0)
        change = face_change(low, mid, high, low_flux, mid_flux, high_flux)
        y_low = [
            jnp.where(fix_low_y, grid_ref[c, x, pl.ds(0, 1), :], low_y_ref[c, pl.ds(x, 1), :])
            for c in range(ncomp)
        ]
        y_high = [
            jnp.where(
                fix_high_y, grid_ref[c, x, pl.ds(len_y - 1, 1), :], high_y_ref[c, pl.ds(x, 1), :]
            )
            for c in range(ncomp)
        ]
        y_flux = cell_flux(mid, 1)
        y_low_flux = cell_flux(y_low, 1)
        y_high_flux = cell_flux(y_high, 1)
        down = [shift(mid[c], y_low[c], 1, 0, rows, 0) for c in range(ncomp)]
        up = [shift(mid[c], y_high[c], len_y - 1, 0, rows, len_y - 1) for c in range(ncomp)]
        down_flux = (
            [shift(y_flux[0][c], y_low_flux[0][c], 1, 0, rows, 0) for c in range(ncomp)],
            shift(y_flux[1], y_low_flux[1], 1, 0, rows, 0),
        )
        up_flux = (
            [shift(y_flux[0][c], y_high_flux[0][c], len_y - 1, 0, rows, len_y - 1) for c in range(ncomp)],
            shift(y_flux[1], y_high_flux[1], len_y - 1, 0, rows, len_y - 1),
        )
        change_y = face_change(down, mid, up, down_flux, y_flux, up_flux)
        z_flux = cell_flux(mid, 2)
        back = [shift(mid[c], mid[c], 1, 1, lanes, 0) for c in range(ncomp)]
        front = [shift(mid[c], mid[c], len_z - 1, 1, lanes, len_z - 1) for c in range(ncomp)]
        back_flux = (
            [shift(z_flux[0][c], z_flux[0][c], 1, 1, lanes, 0) for c in range(ncomp)],
            shift(z_flux[1], z_flux[1], 1, 1, lanes, 0),
        )
        front_flux = (
            [shift(z_flux[0][c], z_flux[0][c], len_z - 1, 1, lanes, len_z - 1) for c in range(ncomp)],
            shift(z_flux[1], z_flux[1], len_z - 1, 1, lanes, len_z - 1),
        )
        change_z = face_change(back, mid, front, back_flux, z_flux, front_flux)
        for c in range(ncomp):
            total = change[c] + change_y[c]
            total = total + change_z[c]
            out_ref[c, x] = mid[c] - ratio * total
        low, mid = mid, high
        low_flux, mid_flux = mid_flux, high_flux


def stencil(grid_cells, low_x, high_x, low_y, high_y):
    vmem = pl.BlockSpec(memory_space=pltpu.VMEM)
    return pl.pallas_call(
        stencil_kernel,
        out_shape=jax.ShapeDtypeStruct(grid_cells.shape, grid_cells.dtype),
        in_specs=[vmem] * 5,
        out_specs=vmem,
    )(grid_cells, low_x, high_x, low_y, high_y)

def local(field_state, shell_owner, block_sources, block_targets, interp_weights):
    grid_cells = field_state[0]
    ncomp, len_x, len_y, len_z = grid_cells.shape
    domain = lax.axis_index("dom")
    column = lax.axis_index("gx")
    yz_index = lax.axis_index("yz")
    gx_count = lax.axis_size("gx")
    yz_count = lax.axis_size("yz")
    per_y = len_y // BLK
    per_z = len_z // BLK
    volume = BLK * BLK * BLK
    shell_cells = grid_cells[:, :, :, len_z - SR * BLK :]
    shell_cells = shell_cells.reshape(ncomp, len_x // BLK, BLK, per_y, BLK, SR, BLK)
    shell_cells = (
        shell_cells.transpose(1, 3, 5, 0, 2, 4, 6).reshape(-1, ncomp * volume).astype(jnp.bfloat16)
    )
    count_here = shell_cells.shape[0]
    owner_table = shell_owner[0]
    own_owner = lax.dynamic_index_in_dim(owner_table, yz_index, 0, keepdims=False)
    index_here = jnp.arange(count_here, dtype=jnp.int32)
    local_same = own_owner[None, :] == own_owner[:, None]
    rank_local = jnp.sum(
        (local_same & (index_here[None, :] < index_here[:, None])).astype(jnp.int32), axis=1
    )
    slot_of = own_owner * CAP + rank_local
    slot_count = yz_count * CAP
    select = jnp.arange(slot_count, dtype=jnp.int32)[:, None] == slot_of[None, :]
    send_cells = jnp.dot(
        select.astype(jnp.bfloat16), shell_cells, preferred_element_type=jnp.float32
    )
    send_cells = send_cells.astype(jnp.bfloat16).reshape(yz_count, CAP * ncomp, volume)
    got_cells = route_blocks(send_cells).reshape(slot_count, ncomp * volume)
    mine = (owner_table == yz_index).astype(jnp.int32)
    per_sender = jnp.sum(mine, axis=1)
    before = jnp.cumsum(per_sender) - per_sender
    rank_slot = jnp.arange(CAP, dtype=jnp.int32)
    got_tags = jnp.where(
        rank_slot[None, :] < per_sender[:, None], before[:, None] + rank_slot[None, :], -1
    ).reshape(slot_count)
    wanted = block_sources[0, 0].reshape(-1)
    match_table = (wanted[:, None] == got_tags[None, :]) & (wanted[:, None] >= 0)
    picked = jnp.dot(
        match_table.astype(jnp.bfloat16), got_cells, preferred_element_type=jnp.float32
    )
    slots_here = block_targets.shape[2]
    picked = picked.astype(jnp.bfloat16).reshape(slots_here, -1, ncomp, volume)
    interp_blocks = jnp.einsum(
        "jkcs,jkst->jct", picked, interp_weights[0, 0], preferred_element_type=jnp.float32
    )

    rows = lax.broadcasted_iota(jnp.int32, (len_x, len_y, len_z), 0) // BLK
    cols = lax.broadcasted_iota(jnp.int32, (len_x, len_y, len_z), 1) // BLK
    lanes = lax.broadcasted_iota(jnp.int32, (len_x, len_y, len_z), 2)
    spread_of = lax.broadcasted_iota(jnp.int32, (BLK, len_z), 1) % BLK
    offset_of = lax.broadcasted_iota(jnp.int32, (BLK, len_z), 0)
    spread = (spread_of == offset_of).astype(jnp.float32)
    stacked = interp_blocks.reshape(slots_here * ncomp * BLK * BLK, BLK)
    stacked = jnp.dot(stacked, spread, precision=lax.Precision.HIGHEST)
    stacked = stacked.reshape(slots_here, ncomp, BLK, BLK, len_z)
    targets = jnp.where(domain == 1, block_targets[0, 0], -1)
    spots = jnp.maximum(targets, 0)
    hit = (
        (rows[None] == (spots // (per_y * per_z))[:, None, None, None])
        & (cols[None] == (spots // per_z % per_y)[:, None, None, None])
        & (lanes[None] // BLK == (spots % per_z)[:, None, None, None])
        & (targets >= 0)[:, None, None, None]
    )
    placed = [
        jnp.tile(stacked[slot_number], (1, len_x // BLK, len_y // BLK, 1))
        for slot_number in range(slots_here)
    ]

    def filled(view):
        cells = view(grid_cells)
        for slot_number in range(slots_here):
            cells = jnp.where(view(hit[slot_number][None]), view(placed[slot_number]), cells)
        return cells

    def at_x(index):
        return lambda cells: lax.index_in_dim(cells, index, axis=1, keepdims=False)

    def at_y(index):
        return lambda cells: lax.index_in_dim(cells, index, axis=2, keepdims=False)

    ghost_low_x, ghost_high_x = ghost_pair(filled(at_x(0)), filled(at_x(len_x - 1)), "gx", True)
    ghost_low_y, ghost_high_y = ghost_pair(filled(at_y(0)), filled(at_y(len_y - 1)), "yz", False)
    grid_cells = filled(lambda cells: cells)
    updated = stencil(grid_cells, ghost_low_x, ghost_high_x, ghost_low_y, ghost_high_y)
    return updated[None]


def solution(mesh):
    placed = (
        P("dom", None, "gx", "yz", None),
        P("gx", None, None),
        P("gx", "yz", None, None),
        P("gx", "yz", None),
        P("gx", "yz", None, None, None, None),
    )
    return jax.shard_map(
        local,
        mesh=mesh,
        in_specs=placed,
        out_specs=P("dom", None, "gx", "yz", None),
        check_vma=False,
    )
```

```python
import jax
import jax.numpy as jnp
from jax import lax
from jax.experimental import pallas as pl
from jax.experimental.pallas import tpu as pltpu
from jax.sharding import PartitionSpec as P

MESH = pl.DeviceIdType.MESH

BLK = 8
SR = 2
CAP = 2


HEAT_RATIO = 5.0 / 3.0
CORONA_RATIO = 0.04
HELIO_RATIO = 0.03


def direction_flux(grid_cells, direction):
    density = grid_cells[0]
    momentum = grid_cells[1:4]
    magnetic = grid_cells[4:7]
    energy = grid_cells[7]
    velocity = momentum / density
    field_sq = jnp.sum(magnetic * magnetic, axis=0)
    pressure = (HEAT_RATIO - 1.0) * (
        energy - 0.5 * jnp.sum(momentum * velocity, axis=0) - 0.5 * field_sq
    )
    total_pressure = pressure + 0.5 * field_sq
    normal_speed = velocity[direction]
    normal_field = magnetic[direction]
    velocity_dot = jnp.sum(velocity * magnetic, axis=0)
    flux_list = [momentum[direction]]
    for other in range(3):
        term = momentum[other] * normal_speed - magnetic[other] * normal_field
        if other == direction:
            term = term + total_pressure
        flux_list.append(term)
    for other in range(3):
        flux_list.append(normal_speed * magnetic[other] - normal_field * velocity[other])
    flux_list.append((energy + total_pressure) * normal_speed - normal_field * velocity_dot)
    wave_speed = jnp.abs(normal_speed) + jnp.sqrt((HEAT_RATIO * pressure + field_sq) / density)
    return (jnp.stack(flux_list), wave_speed)


def interface_change(padded_line, direction):
    phys_flux, wave_speed = direction_flux(padded_line, direction)
    array_dim = direction + 1
    cell_count = padded_line.shape[array_dim]
    low_cells = lax.slice_in_dim(padded_line, 0, cell_count - 1, axis=array_dim)
    high_cells = lax.slice_in_dim(padded_line, 1, cell_count, axis=array_dim)
    low_flux = lax.slice_in_dim(phys_flux, 0, cell_count - 1, axis=array_dim)
    high_flux = lax.slice_in_dim(phys_flux, 1, cell_count, axis=array_dim)
    low_speed = lax.slice_in_dim(wave_speed, 0, cell_count - 1, axis=direction)
    high_speed = lax.slice_in_dim(wave_speed, 1, cell_count, axis=direction)
    fastest = jnp.maximum(low_speed, high_speed)
    face_flux = 0.5 * (low_flux + high_flux) - 0.5 * fastest[None] * (high_cells - low_cells)
    upper_face = lax.slice_in_dim(face_flux, 1, cell_count - 1, axis=array_dim)
    lower_face = lax.slice_in_dim(face_flux, 0, cell_count - 2, axis=array_dim)
    return upper_face - lower_face


def advance(line_set, inner_cells, step_ratio):
    change = interface_change(line_set[0], 0) + interface_change(line_set[1], 1)
    change = change + interface_change(line_set[2], 2)
    return inner_cells - step_ratio * change


def route_kernel(send_ref, out_ref, landed, send_sem, recv_sem):
    domain = lax.axis_index("dom")
    here = lax.axis_index("yz")
    count = send_ref.shape[0]
    barrier = pltpu.get_barrier_semaphore()
    for partner in range(count):
        pl.semaphore_signal(
            barrier, inc=1, device_id={"dom": 1 - domain, "yz": partner}, device_id_type=MESH
        )
    pl.semaphore_wait(barrier, count)

    @pl.when(domain == 0)
    def _():
        copies = []
        for owner in range(count):
            copy = pltpu.make_async_remote_copy(
                src_ref=send_ref.at[owner],
                dst_ref=landed.at[here],
                send_sem=send_sem.at[owner],
                recv_sem=recv_sem.at[here],
                device_id={"dom": 1, "yz": owner},
                device_id_type=MESH,
            )
            copy.start()
            copies.append(copy)
        for copy in copies:
            copy.wait_send()
        out_ref[...] = jnp.zeros_like(out_ref)

    @pl.when(domain == 1)
    def _():
        for sender in range(count):
            pltpu.make_async_remote_copy(
                src_ref=send_ref.at[sender],
                dst_ref=landed.at[sender],
                send_sem=send_sem.at[sender],
                recv_sem=recv_sem.at[sender],
                device_id={"dom": 0, "yz": sender},
                device_id_type=MESH,
            ).wait_recv()
        out_ref[...] = landed[...]


def route_blocks(send_cells):
    count = send_cells.shape[0]
    return pl.pallas_call(
        route_kernel,
        out_shape=jax.ShapeDtypeStruct(send_cells.shape, send_cells.dtype),
        in_specs=[pl.BlockSpec(memory_space=pltpu.VMEM)],
        out_specs=pl.BlockSpec(memory_space=pltpu.VMEM),
        scratch_shapes=[
            pltpu.VMEM(send_cells.shape, send_cells.dtype),
            pltpu.SemaphoreType.DMA((count,)),
            pltpu.SemaphoreType.DMA((count,)),
        ],
        compiler_params=pltpu.CompilerParams(collective_id=0, has_side_effects=True),
    )(send_cells)


def ghost_pair(head, tail, axis, wrap):
    count = lax.axis_size(axis)
    up = [(i, i + 1) for i in range(count - 1)]
    down = [(i + 1, i) for i in range(count - 1)]
    if wrap:
        up.append((count - 1, 0))
        down.append((0, count - 1))
    return lax.ppermute(tail, axis, up), lax.ppermute(head, axis, down)

def cell_flux(parts, direction):
    density = parts[0]
    momentum = parts[1:4]
    magnetic = parts[4:7]
    energy = parts[7]
    velocity = [m / density for m in momentum]
    field_sq = magnetic[0] * magnetic[0] + magnetic[1] * magnetic[1] + magnetic[2] * magnetic[2]
    kinetic = momentum[0] * velocity[0] + momentum[1] * velocity[1] + momentum[2] * velocity[2]
    pressure = (HEAT_RATIO - 1.0) * (energy - 0.5 * kinetic - 0.5 * field_sq)
    total_pressure = pressure + 0.5 * field_sq
    normal_speed = velocity[direction]
    normal_field = magnetic[direction]
    velocity_dot = velocity[0] * magnetic[0] + velocity[1] * magnetic[1] + velocity[2] * magnetic[2]
    flux = [momentum[direction]]
    for other in range(3):
        term = momentum[other] * normal_speed - magnetic[other] * normal_field
        if other == direction:
            term = term + total_pressure
        flux.append(term)
    for other in range(3):
        flux.append(normal_speed * magnetic[other] - normal_field * velocity[other])
    flux.append((energy + total_pressure) * normal_speed - normal_field * velocity_dot)
    speed = jnp.abs(normal_speed) + jnp.sqrt((HEAT_RATIO * pressure + field_sq) / density)
    return flux, speed


def face_change(low, mid, high, low_flux, mid_flux, high_flux):
    (fl, sl), (fm, sm), (fh, sh) = low_flux, mid_flux, high_flux
    fast_low = jnp.maximum(sl, sm)
    fast_high = jnp.maximum(sm, sh)
    change = []
    for c in range(len(mid)):
        upper = 0.5 * (fm[c] + fh[c]) - 0.5 * fast_high * (high[c] - mid[c])
        lower = 0.5 * (fl[c] + fm[c]) - 0.5 * fast_low * (mid[c] - low[c])
        change.append(upper - lower)
    return change


def stencil_kernel(grid_ref, low_x_ref, high_x_ref, low_y_ref, high_y_ref, out_ref):
    ncomp, len_x, len_y, len_z = grid_ref.shape
    domain = lax.axis_index("dom")
    column = lax.axis_index("gx")
    row = lax.axis_index("yz")
    helio_side = domain == 1
    fix_low_x = helio_side & (column == 0)
    fix_high_x = helio_side & (column == lax.axis_size("gx") - 1)
    fix_low_y = row == 0
    fix_high_y = row == lax.axis_size("yz") - 1
    ratio = jnp.where(domain == 0, CORONA_RATIO, HELIO_RATIO).astype(jnp.float32)
    rows = lax.broadcasted_iota(jnp.int32, (len_y, len_z), 0)
    lanes = lax.broadcasted_iota(jnp.int32, (len_y, len_z), 1)

    def plane(x):
        if x < 0:
            return [jnp.where(fix_low_x, grid_ref[c, 0], low_x_ref[c]) for c in range(ncomp)]
        if x >= len_x:
            return [
                jnp.where(fix_high_x, grid_ref[c, len_x - 1], high_x_ref[c]) for c in range(ncomp)
            ]
        return [grid_ref[c, x] for c in range(ncomp)]

    def shift(values, edge, step, axis, index, last):
        moved = pltpu.roll(values, step, axis)
        return jnp.where(index == last, edge, moved)

    low = plane(-1)
    mid = plane(0)
    low_flux = cell_flux(low, 0)
    mid_flux = cell_flux(mid, 0)
    for x in range(len_x):
        high = plane(x + 1)
        high_flux = cell_flux(high, 0)
        change = face_change(low, mid, high, low_flux, mid_flux, high_flux)
        y_low = [
            jnp.where(fix_low_y, grid_ref[c, x, pl.ds(0, 1), :], low_y_ref[c, pl.ds(x, 1), :])
            for c in range(ncomp)
        ]
        y_high = [
            jnp.where(
                fix_high_y, grid_ref[c, x, pl.ds(len_y - 1, 1), :], high_y_ref[c, pl.ds(x, 1), :]
            )
            for c in range(ncomp)
        ]
        y_flux = cell_flux(mid, 1)
        y_low_flux = cell_flux(y_low, 1)
        y_high_flux = cell_flux(y_high, 1)
        down = [shift(mid[c], y_low[c], 1, 0, rows, 0) for c in range(ncomp)]
        up = [shift(mid[c], y_high[c], len_y - 1, 0, rows, len_y - 1) for c in range(ncomp)]
        down_flux = (
            [shift(y_flux[0][c], y_low_flux[0][c], 1, 0, rows, 0) for c in range(ncomp)],
            shift(y_flux[1], y_low_flux[1], 1, 0, rows, 0),
        )
        up_flux = (
            [shift(y_flux[0][c], y_high_flux[0][c], len_y - 1, 0, rows, len_y - 1) for c in range(ncomp)],
            shift(y_flux[1], y_high_flux[1], len_y - 1, 0, rows, len_y - 1),
        )
        change_y = face_change(down, mid, up, down_flux, y_flux, up_flux)
        z_flux = cell_flux(mid, 2)
        back = [shift(mid[c], mid[c], 1, 1, lanes, 0) for c in range(ncomp)]
        front = [shift(mid[c], mid[c], len_z - 1, 1, lanes, len_z - 1) for c in range(ncomp)]
        back_flux = (
            [shift(z_flux[0][c], z_flux[0][c], 1, 1, lanes, 0) for c in range(ncomp)],
            shift(z_flux[1], z_flux[1], 1, 1, lanes, 0),
        )
        front_flux = (
            [shift(z_flux[0][c], z_flux[0][c], len_z - 1, 1, lanes, len_z - 1) for c in range(ncomp)],
            shift(z_flux[1], z_flux[1], len_z - 1, 1, lanes, len_z - 1),
        )
        change_z = face_change(back, mid, front, back_flux, z_flux, front_flux)
        for c in range(ncomp):
            total = change[c] + change_y[c]
            total = total + change_z[c]
            out_ref[c, x] = mid[c] - ratio * total
        low, mid = mid, high
        low_flux, mid_flux = mid_flux, high_flux


def stencil(grid_cells, low_x, high_x, low_y, high_y):
    vmem = pl.BlockSpec(memory_space=pltpu.VMEM)
    return pl.pallas_call(
        stencil_kernel,
        out_shape=jax.ShapeDtypeStruct(grid_cells.shape, grid_cells.dtype),
        in_specs=[vmem] * 5,
        out_specs=vmem,
    )(grid_cells, low_x, high_x, low_y, high_y)

def fill_kernel(targets_ref, grid_ref, stacked_ref, out_ref, low_x_ref, high_x_ref, low_y_ref, high_y_ref):
    ncomp, len_x, len_y, len_z = grid_ref.shape
    per_y = len_y // BLK
    per_z = len_z // BLK
    out_ref[...] = grid_ref[...]
    helio_side = lax.axis_index("dom") == 1
    lanes = lax.broadcasted_iota(jnp.int32, (BLK, len_z), 1) // BLK
    for slot in range(stacked_ref.shape[0]):
        target = targets_ref[slot]

        @pl.when(helio_side & (target >= 0))
        def _():
            corner_x = target // (per_y * per_z) * BLK
            corner_y = pl.multiple_of(target // per_z % per_y * BLK, BLK)
            lane_hit = lanes == target % per_z
            for c in range(ncomp):
                for a in range(BLK):
                    window = (c, corner_x + a, pl.ds(corner_y, BLK), slice(None))
                    out_ref[window] = jnp.where(lane_hit, stacked_ref[slot, c, a], out_ref[window])

    low_x_ref[...] = out_ref[:, 0]
    high_x_ref[...] = out_ref[:, len_x - 1]
    for c in range(ncomp):
        for x in range(len_x):
            low_y_ref[c, pl.ds(x, 1), :] = out_ref[c, x, pl.ds(0, 1), :]
            high_y_ref[c, pl.ds(x, 1), :] = out_ref[c, x, pl.ds(len_y - 1, 1), :]


def fill_blocks(targets, grid_cells, stacked):
    ncomp, len_x, len_y, len_z = grid_cells.shape
    vmem = pl.BlockSpec(memory_space=pltpu.VMEM)
    face = jax.ShapeDtypeStruct((ncomp, len_x, len_z), grid_cells.dtype)
    return pl.pallas_call(
        fill_kernel,
        out_shape=(jax.ShapeDtypeStruct(grid_cells.shape, grid_cells.dtype),) + (face,) * 4,
        in_specs=[pl.BlockSpec(memory_space=pltpu.SMEM), vmem, vmem],
        out_specs=(vmem,) * 5,
    )(targets, grid_cells, stacked)


def local(field_state, shell_owner, block_sources, block_targets, interp_weights):
    grid_cells = field_state[0]
    ncomp, len_x, len_y, len_z = grid_cells.shape
    domain = lax.axis_index("dom")
    column = lax.axis_index("gx")
    yz_index = lax.axis_index("yz")
    gx_count = lax.axis_size("gx")
    yz_count = lax.axis_size("yz")
    per_y = len_y // BLK
    per_z = len_z // BLK
    volume = BLK * BLK * BLK
    shell_cells = grid_cells[:, :, :, len_z - SR * BLK :]
    shell_cells = shell_cells.reshape(ncomp, len_x // BLK, BLK, per_y, BLK, SR, BLK)
    shell_cells = (
        shell_cells.transpose(1, 3, 5, 0, 2, 4, 6).reshape(-1, ncomp * volume).astype(jnp.bfloat16)
    )
    count_here = shell_cells.shape[0]
    owner_table = shell_owner[0]
    own_owner = lax.dynamic_index_in_dim(owner_table, yz_index, 0, keepdims=False)
    index_here = jnp.arange(count_here, dtype=jnp.int32)
    local_same = own_owner[None, :] == own_owner[:, None]
    rank_local = jnp.sum(
        (local_same & (index_here[None, :] < index_here[:, None])).astype(jnp.int32), axis=1
    )
    slot_of = own_owner * CAP + rank_local
    slot_count = yz_count * CAP
    select = jnp.arange(slot_count, dtype=jnp.int32)[:, None] == slot_of[None, :]
    send_cells = jnp.dot(
        select.astype(jnp.bfloat16), shell_cells, preferred_element_type=jnp.float32
    )
    send_cells = send_cells.astype(jnp.bfloat16).reshape(yz_count, CAP * ncomp, volume)
    got_cells = route_blocks(send_cells).reshape(slot_count, ncomp * volume)
    mine = (owner_table == yz_index).astype(jnp.int32)
    per_sender = jnp.sum(mine, axis=1)
    before = jnp.cumsum(per_sender) - per_sender
    rank_slot = jnp.arange(CAP, dtype=jnp.int32)
    got_tags = jnp.where(
        rank_slot[None, :] < per_sender[:, None], before[:, None] + rank_slot[None, :], -1
    ).reshape(slot_count)
    wanted = block_sources[0, 0].reshape(-1)
    match_table = (wanted[:, None] == got_tags[None, :]) & (wanted[:, None] >= 0)
    picked = jnp.dot(
        match_table.astype(jnp.bfloat16), got_cells, preferred_element_type=jnp.float32
    )
    slots_here = block_targets.shape[2]
    picked = picked.astype(jnp.bfloat16).reshape(slots_here, -1, ncomp, volume)
    interp_blocks = jnp.einsum(
        "jkcs,jkst->jct", picked, interp_weights[0, 0], preferred_element_type=jnp.float32
    )

    spread_of = lax.broadcasted_iota(jnp.int32, (BLK, len_z), 1) % BLK
    offset_of = lax.broadcasted_iota(jnp.int32, (BLK, len_z), 0)
    spread = (spread_of == offset_of).astype(jnp.float32)
    stacked = interp_blocks.reshape(slots_here * ncomp * BLK * BLK, BLK)
    stacked = jnp.dot(stacked, spread, precision=lax.Precision.HIGHEST)
    stacked = stacked.reshape(slots_here, ncomp, BLK, BLK, len_z)
    grid_cells, head_x, tail_x, head_y, tail_y = fill_blocks(block_targets[0, 0], grid_cells, stacked)
    ghost_low_x, ghost_high_x = ghost_pair(head_x, tail_x, "gx", True)
    ghost_low_y, ghost_high_y = ghost_pair(head_y, tail_y, "yz", False)
    updated = stencil(grid_cells, ghost_low_x, ghost_high_x, ghost_low_y, ghost_high_y)
    return updated[None]


def solution(mesh):
    placed = (
        P("dom", None, "gx", "yz", None),
        P("gx", None, None),
        P("gx", "yz", None, None),
        P("gx", "yz", None),
        P("gx", "yz", None, None, None, None),
    )
    return jax.shard_map(
        local,
        mesh=mesh,
        in_specs=placed,
        out_specs=P("dom", None, "gx", "yz", None),
        check_vma=False,
    )
```

```python
import jax
import jax.numpy as jnp
from jax import lax
from jax.experimental import pallas as pl
from jax.experimental.pallas import tpu as pltpu
from jax.sharding import PartitionSpec as P

MESH = pl.DeviceIdType.MESH

BLK = 8
SR = 2
CAP = 2


HEAT_RATIO = 5.0 / 3.0
CORONA_RATIO = 0.04
HELIO_RATIO = 0.03


def direction_flux(grid_cells, direction):
    density = grid_cells[0]
    momentum = grid_cells[1:4]
    magnetic = grid_cells[4:7]
    energy = grid_cells[7]
    velocity = momentum / density
    field_sq = jnp.sum(magnetic * magnetic, axis=0)
    pressure = (HEAT_RATIO - 1.0) * (
        energy - 0.5 * jnp.sum(momentum * velocity, axis=0) - 0.5 * field_sq
    )
    total_pressure = pressure + 0.5 * field_sq
    normal_speed = velocity[direction]
    normal_field = magnetic[direction]
    velocity_dot = jnp.sum(velocity * magnetic, axis=0)
    flux_list = [momentum[direction]]
    for other in range(3):
        term = momentum[other] * normal_speed - magnetic[other] * normal_field
        if other == direction:
            term = term + total_pressure
        flux_list.append(term)
    for other in range(3):
        flux_list.append(normal_speed * magnetic[other] - normal_field * velocity[other])
    flux_list.append((energy + total_pressure) * normal_speed - normal_field * velocity_dot)
    wave_speed = jnp.abs(normal_speed) + jnp.sqrt((HEAT_RATIO * pressure + field_sq) / density)
    return (jnp.stack(flux_list), wave_speed)


def interface_change(padded_line, direction):
    phys_flux, wave_speed = direction_flux(padded_line, direction)
    array_dim = direction + 1
    cell_count = padded_line.shape[array_dim]
    low_cells = lax.slice_in_dim(padded_line, 0, cell_count - 1, axis=array_dim)
    high_cells = lax.slice_in_dim(padded_line, 1, cell_count, axis=array_dim)
    low_flux = lax.slice_in_dim(phys_flux, 0, cell_count - 1, axis=array_dim)
    high_flux = lax.slice_in_dim(phys_flux, 1, cell_count, axis=array_dim)
    low_speed = lax.slice_in_dim(wave_speed, 0, cell_count - 1, axis=direction)
    high_speed = lax.slice_in_dim(wave_speed, 1, cell_count, axis=direction)
    fastest = jnp.maximum(low_speed, high_speed)
    face_flux = 0.5 * (low_flux + high_flux) - 0.5 * fastest[None] * (high_cells - low_cells)
    upper_face = lax.slice_in_dim(face_flux, 1, cell_count - 1, axis=array_dim)
    lower_face = lax.slice_in_dim(face_flux, 0, cell_count - 2, axis=array_dim)
    return upper_face - lower_face


def advance(line_set, inner_cells, step_ratio):
    change = interface_change(line_set[0], 0) + interface_change(line_set[1], 1)
    change = change + interface_change(line_set[2], 2)
    return inner_cells - step_ratio * change


def route_kernel(send_ref, out_ref, landed, send_sem, recv_sem):
    domain = lax.axis_index("dom")
    here = lax.axis_index("yz")
    count = send_ref.shape[0]
    barrier = pltpu.get_barrier_semaphore()
    for partner in range(count):
        pl.semaphore_signal(
            barrier, inc=1, device_id={"dom": 1 - domain, "yz": partner}, device_id_type=MESH
        )
    pl.semaphore_wait(barrier, count)

    @pl.when(domain == 0)
    def _():
        copies = []
        for owner in range(count):
            copy = pltpu.make_async_remote_copy(
                src_ref=send_ref.at[owner],
                dst_ref=landed.at[here],
                send_sem=send_sem.at[owner],
                recv_sem=recv_sem.at[here],
                device_id={"dom": 1, "yz": owner},
                device_id_type=MESH,
            )
            copy.start()
            copies.append(copy)
        for copy in copies:
            copy.wait_send()
        out_ref[...] = jnp.zeros_like(out_ref)

    @pl.when(domain == 1)
    def _():
        for sender in range(count):
            pltpu.make_async_remote_copy(
                src_ref=send_ref.at[sender],
                dst_ref=landed.at[sender],
                send_sem=send_sem.at[sender],
                recv_sem=recv_sem.at[sender],
                device_id={"dom": 0, "yz": sender},
                device_id_type=MESH,
            ).wait_recv()
        out_ref[...] = landed[...]


def route_blocks(send_cells):
    count = send_cells.shape[0]
    return pl.pallas_call(
        route_kernel,
        out_shape=jax.ShapeDtypeStruct(send_cells.shape, send_cells.dtype),
        in_specs=[pl.BlockSpec(memory_space=pltpu.VMEM)],
        out_specs=pl.BlockSpec(memory_space=pltpu.VMEM),
        scratch_shapes=[
            pltpu.VMEM(send_cells.shape, send_cells.dtype),
            pltpu.SemaphoreType.DMA((count,)),
            pltpu.SemaphoreType.DMA((count,)),
        ],
        compiler_params=pltpu.CompilerParams(collective_id=0, has_side_effects=True),
    )(send_cells)


def ghost_pair(head, tail, axis, wrap):
    count = lax.axis_size(axis)
    up = [(i, i + 1) for i in range(count - 1)]
    down = [(i + 1, i) for i in range(count - 1)]
    if wrap:
        up.append((count - 1, 0))
        down.append((0, count - 1))
    return lax.ppermute(tail, axis, up), lax.ppermute(head, axis, down)

def cell_flux(parts, direction):
    density = parts[0]
    momentum = parts[1:4]
    magnetic = parts[4:7]
    energy = parts[7]
    velocity = [m / density for m in momentum]
    field_sq = magnetic[0] * magnetic[0] + magnetic[1] * magnetic[1] + magnetic[2] * magnetic[2]
    kinetic = momentum[0] * velocity[0] + momentum[1] * velocity[1] + momentum[2] * velocity[2]
    pressure = (HEAT_RATIO - 1.0) * (energy - 0.5 * kinetic - 0.5 * field_sq)
    total_pressure = pressure + 0.5 * field_sq
    normal_speed = velocity[direction]
    normal_field = magnetic[direction]
    velocity_dot = velocity[0] * magnetic[0] + velocity[1] * magnetic[1] + velocity[2] * magnetic[2]
    flux = [momentum[direction]]
    for other in range(3):
        term = momentum[other] * normal_speed - magnetic[other] * normal_field
        if other == direction:
            term = term + total_pressure
        flux.append(term)
    for other in range(3):
        flux.append(normal_speed * magnetic[other] - normal_field * velocity[other])
    flux.append((energy + total_pressure) * normal_speed - normal_field * velocity_dot)
    speed = jnp.abs(normal_speed) + jnp.sqrt((HEAT_RATIO * pressure + field_sq) / density)
    return flux, speed


def face_change(low, mid, high, low_flux, mid_flux, high_flux):
    (fl, sl), (fm, sm), (fh, sh) = low_flux, mid_flux, high_flux
    fast_low = jnp.maximum(sl, sm)
    fast_high = jnp.maximum(sm, sh)
    change = []
    for c in range(len(mid)):
        upper = 0.5 * (fm[c] + fh[c]) - 0.5 * fast_high * (high[c] - mid[c])
        lower = 0.5 * (fl[c] + fm[c]) - 0.5 * fast_low * (mid[c] - low[c])
        change.append(upper - lower)
    return change


def stencil_kernel(grid_ref, low_x_ref, high_x_ref, low_y_ref, high_y_ref, out_ref):
    ncomp, len_x, len_y, len_z = grid_ref.shape
    domain = lax.axis_index("dom")
    column = lax.axis_index("gx")
    row = lax.axis_index("yz")
    helio_side = domain == 1
    fix_low_x = helio_side & (column == 0)
    fix_high_x = helio_side & (column == lax.axis_size("gx") - 1)
    fix_low_y = row == 0
    fix_high_y = row == lax.axis_size("yz") - 1
    ratio = jnp.where(domain == 0, CORONA_RATIO, HELIO_RATIO).astype(jnp.float32)
    rows = lax.broadcasted_iota(jnp.int32, (len_y, len_z), 0)
    lanes = lax.broadcasted_iota(jnp.int32, (len_y, len_z), 1)

    def plane(x):
        if x < 0:
            return [jnp.where(fix_low_x, grid_ref[c, 0], low_x_ref[c]) for c in range(ncomp)]
        if x >= len_x:
            return [
                jnp.where(fix_high_x, grid_ref[c, len_x - 1], high_x_ref[c]) for c in range(ncomp)
            ]
        return [grid_ref[c, x] for c in range(ncomp)]

    def shift(values, edge, step, axis, index, last):
        moved = pltpu.roll(values, step, axis)
        return jnp.where(index == last, edge, moved)

    low = plane(-1)
    mid = plane(0)
    low_flux = cell_flux(low, 0)
    mid_flux = cell_flux(mid, 0)
    for x in range(len_x):
        high = plane(x + 1)
        high_flux = cell_flux(high, 0)
        change = face_change(low, mid, high, low_flux, mid_flux, high_flux)
        y_low = [
            jnp.where(fix_low_y, grid_ref[c, x, pl.ds(0, 1), :], low_y_ref[c, pl.ds(x, 1), :])
            for c in range(ncomp)
        ]
        y_high = [
            jnp.where(
                fix_high_y, grid_ref[c, x, pl.ds(len_y - 1, 1), :], high_y_ref[c, pl.ds(x, 1), :]
            )
            for c in range(ncomp)
        ]
        y_flux = cell_flux(mid, 1)
        y_low_flux = cell_flux(y_low, 1)
        y_high_flux = cell_flux(y_high, 1)
        down = [shift(mid[c], y_low[c], 1, 0, rows, 0) for c in range(ncomp)]
        up = [shift(mid[c], y_high[c], len_y - 1, 0, rows, len_y - 1) for c in range(ncomp)]
        down_flux = (
            [shift(y_flux[0][c], y_low_flux[0][c], 1, 0, rows, 0) for c in range(ncomp)],
            shift(y_flux[1], y_low_flux[1], 1, 0, rows, 0),
        )
        up_flux = (
            [shift(y_flux[0][c], y_high_flux[0][c], len_y - 1, 0, rows, len_y - 1) for c in range(ncomp)],
            shift(y_flux[1], y_high_flux[1], len_y - 1, 0, rows, len_y - 1),
        )
        change_y = face_change(down, mid, up, down_flux, y_flux, up_flux)
        z_flux = cell_flux(mid, 2)
        back = [shift(mid[c], mid[c], 1, 1, lanes, 0) for c in range(ncomp)]
        front = [shift(mid[c], mid[c], len_z - 1, 1, lanes, len_z - 1) for c in range(ncomp)]
        back_flux = (
            [shift(z_flux[0][c], z_flux[0][c], 1, 1, lanes, 0) for c in range(ncomp)],
            shift(z_flux[1], z_flux[1], 1, 1, lanes, 0),
        )
        front_flux = (
            [shift(z_flux[0][c], z_flux[0][c], len_z - 1, 1, lanes, len_z - 1) for c in range(ncomp)],
            shift(z_flux[1], z_flux[1], len_z - 1, 1, lanes, len_z - 1),
        )
        change_z = face_change(back, mid, front, back_flux, z_flux, front_flux)
        for c in range(ncomp):
            total = change[c] + change_y[c]
            total = total + change_z[c]
            out_ref[c, x] = mid[c] - ratio * total
        low, mid = mid, high
        low_flux, mid_flux = mid_flux, high_flux


def stencil(grid_cells, low_x, high_x, low_y, high_y):
    vmem = pl.BlockSpec(memory_space=pltpu.VMEM)
    return pl.pallas_call(
        stencil_kernel,
        out_shape=jax.ShapeDtypeStruct(grid_cells.shape, grid_cells.dtype),
        in_specs=[vmem] * 5,
        out_specs=vmem,
    )(grid_cells, low_x, high_x, low_y, high_y)

def fill_kernel(targets_ref, grid_ref, stacked_ref, out_ref, low_x_ref, high_x_ref, low_y_ref, high_y_ref):
    ncomp, len_x, len_y, len_z = grid_ref.shape
    per_y = len_y // BLK
    per_z = len_z // BLK
    out_ref[...] = grid_ref[...]
    helio_side = lax.axis_index("dom") == 1
    lanes = lax.broadcasted_iota(jnp.int32, (BLK, len_z), 1) // BLK
    for slot in range(stacked_ref.shape[0]):
        target = targets_ref[slot]

        @pl.when(helio_side & (target >= 0))
        def _():
            corner_x = target // (per_y * per_z) * BLK
            corner_y = pl.multiple_of(target // per_z % per_y * BLK, BLK)
            lane_hit = lanes == target % per_z
            for c in range(ncomp):
                for a in range(BLK):
                    window = (c, corner_x + a, pl.ds(corner_y, BLK), slice(None))
                    out_ref[window] = jnp.where(lane_hit, stacked_ref[slot, c, a], out_ref[window])

    low_x_ref[...] = out_ref[:, 0]
    high_x_ref[...] = out_ref[:, len_x - 1]
    for c in range(ncomp):
        for x in range(len_x):
            low_y_ref[c, pl.ds(x, 1), :] = out_ref[c, x, pl.ds(0, 1), :]
            high_y_ref[c, pl.ds(x, 1), :] = out_ref[c, x, pl.ds(len_y - 1, 1), :]


def fill_blocks(targets, grid_cells, stacked):
    ncomp, len_x, len_y, len_z = grid_cells.shape
    vmem = pl.BlockSpec(memory_space=pltpu.VMEM)
    face = jax.ShapeDtypeStruct((ncomp, len_x, len_z), grid_cells.dtype)
    return pl.pallas_call(
        fill_kernel,
        out_shape=(jax.ShapeDtypeStruct(grid_cells.shape, grid_cells.dtype),) + (face,) * 4,
        in_specs=[pl.BlockSpec(memory_space=pltpu.SMEM), vmem, vmem],
        out_specs=(vmem,) * 5,
    )(targets, grid_cells, stacked)


def halo_kernel(low_x_ref, high_x_ref, low_y_ref, high_y_ref, out_ref, landed, send_sem, recv_sem):
    column = lax.axis_index("gx")
    row = lax.axis_index("yz")
    gx_count = lax.axis_size("gx")
    yz_count = lax.axis_size("yz")
    up_x = {"gx": lax.rem(column + 1, gx_count)}
    down_x = {"gx": lax.rem(column + gx_count - 1, gx_count)}
    up_y = {"yz": lax.rem(row + 1, yz_count)}
    down_y = {"yz": lax.rem(row + yz_count - 1, yz_count)}
    barrier = pltpu.get_barrier_semaphore()
    for partner in (up_x, down_x, up_y, down_y):
        pl.semaphore_signal(barrier, inc=1, device_id=partner, device_id_type=MESH)
    pl.semaphore_wait(barrier, 4)
    sends = ((high_x_ref, up_x), (low_x_ref, down_x), (high_y_ref, up_y), (low_y_ref, down_y))
    copies = []
    for slot, (source, partner) in enumerate(sends):
        copy = pltpu.make_async_remote_copy(
            src_ref=source,
            dst_ref=landed.at[slot],
            send_sem=send_sem.at[slot],
            recv_sem=recv_sem.at[slot],
            device_id=partner,
            device_id_type=MESH,
        )
        copy.start()
        copies.append(copy)
    for copy in copies:
        copy.wait()
    out_ref[...] = landed[...]


def exchange_faces(low_x, high_x, low_y, high_y):
    face = (4,) + low_x.shape
    vmem = pl.BlockSpec(memory_space=pltpu.VMEM)
    return pl.pallas_call(
        halo_kernel,
        out_shape=jax.ShapeDtypeStruct(face, low_x.dtype),
        in_specs=[vmem] * 4,
        out_specs=vmem,
        scratch_shapes=[
            pltpu.VMEM(face, low_x.dtype),
            pltpu.SemaphoreType.DMA((4,)),
            pltpu.SemaphoreType.DMA((4,)),
        ],
        compiler_params=pltpu.CompilerParams(collective_id=1, has_side_effects=True),
    )(low_x, high_x, low_y, high_y)


def local(field_state, shell_owner, block_sources, block_targets, interp_weights):
    grid_cells = field_state[0]
    ncomp, len_x, len_y, len_z = grid_cells.shape
    domain = lax.axis_index("dom")
    column = lax.axis_index("gx")
    yz_index = lax.axis_index("yz")
    gx_count = lax.axis_size("gx")
    yz_count = lax.axis_size("yz")
    per_y = len_y // BLK
    per_z = len_z // BLK
    volume = BLK * BLK * BLK
    shell_cells = grid_cells[:, :, :, len_z - SR * BLK :]
    shell_cells = shell_cells.reshape(ncomp, len_x // BLK, BLK, per_y, BLK, SR, BLK)
    shell_cells = (
        shell_cells.transpose(1, 3, 5, 0, 2, 4, 6).reshape(-1, ncomp * volume).astype(jnp.bfloat16)
    )
    count_here = shell_cells.shape[0]
    owner_table = shell_owner[0]
    own_owner = lax.dynamic_index_in_dim(owner_table, yz_index, 0, keepdims=False)
    index_here = jnp.arange(count_here, dtype=jnp.int32)
    local_same = own_owner[None, :] == own_owner[:, None]
    rank_local = jnp.sum(
        (local_same & (index_here[None, :] < index_here[:, None])).astype(jnp.int32), axis=1
    )
    slot_of = own_owner * CAP + rank_local
    slot_count = yz_count * CAP
    select = jnp.arange(slot_count, dtype=jnp.int32)[:, None] == slot_of[None, :]
    send_cells = jnp.dot(
        select.astype(jnp.bfloat16), shell_cells, preferred_element_type=jnp.float32
    )
    send_cells = send_cells.astype(jnp.bfloat16).reshape(yz_count, CAP * ncomp, volume)
    got_cells = route_blocks(send_cells).reshape(slot_count, ncomp * volume)
    mine = (owner_table == yz_index).astype(jnp.int32)
    per_sender = jnp.sum(mine, axis=1)
    before = jnp.cumsum(per_sender) - per_sender
    rank_slot = jnp.arange(CAP, dtype=jnp.int32)
    got_tags = jnp.where(
        rank_slot[None, :] < per_sender[:, None], before[:, None] + rank_slot[None, :], -1
    ).reshape(slot_count)
    wanted = block_sources[0, 0].reshape(-1)
    match_table = (wanted[:, None] == got_tags[None, :]) & (wanted[:, None] >= 0)
    picked = jnp.dot(
        match_table.astype(jnp.bfloat16), got_cells, preferred_element_type=jnp.float32
    )
    slots_here = block_targets.shape[2]
    picked = picked.astype(jnp.bfloat16).reshape(slots_here, -1, ncomp, volume)
    interp_blocks = jnp.einsum(
        "jkcs,jkst->jct", picked, interp_weights[0, 0], preferred_element_type=jnp.float32
    )

    spread_of = lax.broadcasted_iota(jnp.int32, (BLK, len_z), 1) % BLK
    offset_of = lax.broadcasted_iota(jnp.int32, (BLK, len_z), 0)
    spread = (spread_of == offset_of).astype(jnp.float32)
    stacked = interp_blocks.reshape(slots_here * ncomp * BLK * BLK, BLK)
    stacked = jnp.dot(stacked, spread, precision=lax.Precision.HIGHEST)
    stacked = stacked.reshape(slots_here, ncomp, BLK, BLK, len_z)
    grid_cells, head_x, tail_x, head_y, tail_y = fill_blocks(block_targets[0, 0], grid_cells, stacked)
    ghosts = exchange_faces(head_x, tail_x, head_y, tail_y)
    ghost_low_x, ghost_high_x, ghost_low_y, ghost_high_y = (ghosts[n] for n in range(4))
    updated = stencil(grid_cells, ghost_low_x, ghost_high_x, ghost_low_y, ghost_high_y)
    return updated[None]


def solution(mesh):
    placed = (
        P("dom", None, "gx", "yz", None),
        P("gx", None, None),
        P("gx", "yz", None, None),
        P("gx", "yz", None),
        P("gx", "yz", None, None, None, None),
    )
    return jax.shard_map(
        local,
        mesh=mesh,
        in_specs=placed,
        out_specs=P("dom", None, "gx", "yz", None),
        check_vma=False,
    )
```

```python
import jax
import jax.numpy as jnp
from jax import lax
from jax.experimental import pallas as pl
from jax.experimental.pallas import tpu as pltpu
from jax.sharding import PartitionSpec as P

MESH = pl.DeviceIdType.MESH

BLK = 8
SR = 2
CAP = 2


HEAT_RATIO = 5.0 / 3.0
CORONA_RATIO = 0.04
HELIO_RATIO = 0.03


def direction_flux(grid_cells, direction):
    density = grid_cells[0]
    momentum = grid_cells[1:4]
    magnetic = grid_cells[4:7]
    energy = grid_cells[7]
    velocity = momentum / density
    field_sq = jnp.sum(magnetic * magnetic, axis=0)
    pressure = (HEAT_RATIO - 1.0) * (
        energy - 0.5 * jnp.sum(momentum * velocity, axis=0) - 0.5 * field_sq
    )
    total_pressure = pressure + 0.5 * field_sq
    normal_speed = velocity[direction]
    normal_field = magnetic[direction]
    velocity_dot = jnp.sum(velocity * magnetic, axis=0)
    flux_list = [momentum[direction]]
    for other in range(3):
        term = momentum[other] * normal_speed - magnetic[other] * normal_field
        if other == direction:
            term = term + total_pressure
        flux_list.append(term)
    for other in range(3):
        flux_list.append(normal_speed * magnetic[other] - normal_field * velocity[other])
    flux_list.append((energy + total_pressure) * normal_speed - normal_field * velocity_dot)
    wave_speed = jnp.abs(normal_speed) + jnp.sqrt((HEAT_RATIO * pressure + field_sq) / density)
    return (jnp.stack(flux_list), wave_speed)


def interface_change(padded_line, direction):
    phys_flux, wave_speed = direction_flux(padded_line, direction)
    array_dim = direction + 1
    cell_count = padded_line.shape[array_dim]
    low_cells = lax.slice_in_dim(padded_line, 0, cell_count - 1, axis=array_dim)
    high_cells = lax.slice_in_dim(padded_line, 1, cell_count, axis=array_dim)
    low_flux = lax.slice_in_dim(phys_flux, 0, cell_count - 1, axis=array_dim)
    high_flux = lax.slice_in_dim(phys_flux, 1, cell_count, axis=array_dim)
    low_speed = lax.slice_in_dim(wave_speed, 0, cell_count - 1, axis=direction)
    high_speed = lax.slice_in_dim(wave_speed, 1, cell_count, axis=direction)
    fastest = jnp.maximum(low_speed, high_speed)
    face_flux = 0.5 * (low_flux + high_flux) - 0.5 * fastest[None] * (high_cells - low_cells)
    upper_face = lax.slice_in_dim(face_flux, 1, cell_count - 1, axis=array_dim)
    lower_face = lax.slice_in_dim(face_flux, 0, cell_count - 2, axis=array_dim)
    return upper_face - lower_face


def advance(line_set, inner_cells, step_ratio):
    change = interface_change(line_set[0], 0) + interface_change(line_set[1], 1)
    change = change + interface_change(line_set[2], 2)
    return inner_cells - step_ratio * change


def route_kernel(send_ref, out_ref, landed, send_sem, recv_sem):
    domain = lax.axis_index("dom")
    here = lax.axis_index("yz")
    count = send_ref.shape[0]
    barrier = pltpu.get_barrier_semaphore()
    for partner in range(count):
        pl.semaphore_signal(
            barrier, inc=1, device_id={"dom": 1 - domain, "yz": partner}, device_id_type=MESH
        )
    pl.semaphore_wait(barrier, count)

    @pl.when(domain == 0)
    def _():
        copies = []
        for owner in range(count):
            copy = pltpu.make_async_remote_copy(
                src_ref=send_ref.at[owner],
                dst_ref=landed.at[here],
                send_sem=send_sem.at[owner],
                recv_sem=recv_sem.at[here],
                device_id={"dom": 1, "yz": owner},
                device_id_type=MESH,
            )
            copy.start()
            copies.append(copy)
        for copy in copies:
            copy.wait_send()
        out_ref[...] = jnp.zeros_like(out_ref)

    @pl.when(domain == 1)
    def _():
        for sender in range(count):
            pltpu.make_async_remote_copy(
                src_ref=send_ref.at[sender],
                dst_ref=landed.at[sender],
                send_sem=send_sem.at[sender],
                recv_sem=recv_sem.at[sender],
                device_id={"dom": 0, "yz": sender},
                device_id_type=MESH,
            ).wait_recv()
        out_ref[...] = landed[...]


def route_blocks(send_cells):
    count = send_cells.shape[0]
    return pl.pallas_call(
        route_kernel,
        out_shape=jax.ShapeDtypeStruct(send_cells.shape, send_cells.dtype),
        in_specs=[pl.BlockSpec(memory_space=pltpu.VMEM)],
        out_specs=pl.BlockSpec(memory_space=pltpu.VMEM),
        scratch_shapes=[
            pltpu.VMEM(send_cells.shape, send_cells.dtype),
            pltpu.SemaphoreType.DMA((count,)),
            pltpu.SemaphoreType.DMA((count,)),
        ],
        compiler_params=pltpu.CompilerParams(collective_id=0, has_side_effects=True),
    )(send_cells)


def ghost_pair(head, tail, axis, wrap):
    count = lax.axis_size(axis)
    up = [(i, i + 1) for i in range(count - 1)]
    down = [(i + 1, i) for i in range(count - 1)]
    if wrap:
        up.append((count - 1, 0))
        down.append((0, count - 1))
    return lax.ppermute(tail, axis, up), lax.ppermute(head, axis, down)

def cell_flux(parts, direction):
    density = parts[0]
    momentum = parts[1:4]
    magnetic = parts[4:7]
    energy = parts[7]
    velocity = [m / density for m in momentum]
    field_sq = magnetic[0] * magnetic[0] + magnetic[1] * magnetic[1] + magnetic[2] * magnetic[2]
    kinetic = momentum[0] * velocity[0] + momentum[1] * velocity[1] + momentum[2] * velocity[2]
    pressure = (HEAT_RATIO - 1.0) * (energy - 0.5 * kinetic - 0.5 * field_sq)
    total_pressure = pressure + 0.5 * field_sq
    normal_speed = velocity[direction]
    normal_field = magnetic[direction]
    velocity_dot = velocity[0] * magnetic[0] + velocity[1] * magnetic[1] + velocity[2] * magnetic[2]
    flux = [momentum[direction]]
    for other in range(3):
        term = momentum[other] * normal_speed - magnetic[other] * normal_field
        if other == direction:
            term = term + total_pressure
        flux.append(term)
    for other in range(3):
        flux.append(normal_speed * magnetic[other] - normal_field * velocity[other])
    flux.append((energy + total_pressure) * normal_speed - normal_field * velocity_dot)
    speed = jnp.abs(normal_speed) + jnp.sqrt((HEAT_RATIO * pressure + field_sq) / density)
    return flux, speed


def face_change(low, mid, high, low_flux, mid_flux, high_flux):
    (fl, sl), (fm, sm), (fh, sh) = low_flux, mid_flux, high_flux
    fast_low = jnp.maximum(sl, sm)
    fast_high = jnp.maximum(sm, sh)
    change = []
    for c in range(len(mid)):
        upper = 0.5 * (fm[c] + fh[c]) - 0.5 * fast_high * (high[c] - mid[c])
        lower = 0.5 * (fl[c] + fm[c]) - 0.5 * fast_low * (mid[c] - low[c])
        change.append(upper - lower)
    return change


def stencil_kernel(grid_ref, low_x_ref, high_x_ref, low_y_ref, high_y_ref, out_ref):
    ncomp, len_x, len_y, len_z = grid_ref.shape
    domain = lax.axis_index("dom")
    column = lax.axis_index("gx")
    row = lax.axis_index("yz")
    helio_side = domain == 1
    fix_low_x = helio_side & (column == 0)
    fix_high_x = helio_side & (column == lax.axis_size("gx") - 1)
    fix_low_y = row == 0
    fix_high_y = row == lax.axis_size("yz") - 1
    ratio = jnp.where(domain == 0, CORONA_RATIO, HELIO_RATIO).astype(jnp.float32)
    rows = lax.broadcasted_iota(jnp.int32, (len_y, len_z), 0)
    lanes = lax.broadcasted_iota(jnp.int32, (len_y, len_z), 1)

    def plane(x):
        if x < 0:
            return [jnp.where(fix_low_x, grid_ref[c, 0], low_x_ref[c]) for c in range(ncomp)]
        if x >= len_x:
            return [
                jnp.where(fix_high_x, grid_ref[c, len_x - 1], high_x_ref[c]) for c in range(ncomp)
            ]
        return [grid_ref[c, x] for c in range(ncomp)]

    def shift(values, edge, step, axis, index, last):
        moved = pltpu.roll(values, step, axis)
        return jnp.where(index == last, edge, moved)

    low = plane(-1)
    mid = plane(0)
    low_flux = cell_flux(low, 0)
    mid_flux = cell_flux(mid, 0)
    for x in range(len_x):
        high = plane(x + 1)
        high_flux = cell_flux(high, 0)
        change = face_change(low, mid, high, low_flux, mid_flux, high_flux)
        y_low = [
            jnp.where(fix_low_y, grid_ref[c, x, pl.ds(0, 1), :], low_y_ref[c, pl.ds(x, 1), :])
            for c in range(ncomp)
        ]
        y_high = [
            jnp.where(
                fix_high_y, grid_ref[c, x, pl.ds(len_y - 1, 1), :], high_y_ref[c, pl.ds(x, 1), :]
            )
            for c in range(ncomp)
        ]
        y_flux = cell_flux(mid, 1)
        y_low_flux = cell_flux(y_low, 1)
        y_high_flux = cell_flux(y_high, 1)
        down = [shift(mid[c], y_low[c], 1, 0, rows, 0) for c in range(ncomp)]
        up = [shift(mid[c], y_high[c], len_y - 1, 0, rows, len_y - 1) for c in range(ncomp)]
        down_flux = (
            [shift(y_flux[0][c], y_low_flux[0][c], 1, 0, rows, 0) for c in range(ncomp)],
            shift(y_flux[1], y_low_flux[1], 1, 0, rows, 0),
        )
        up_flux = (
            [shift(y_flux[0][c], y_high_flux[0][c], len_y - 1, 0, rows, len_y - 1) for c in range(ncomp)],
            shift(y_flux[1], y_high_flux[1], len_y - 1, 0, rows, len_y - 1),
        )
        change_y = face_change(down, mid, up, down_flux, y_flux, up_flux)
        z_flux = cell_flux(mid, 2)
        back = [shift(mid[c], mid[c], 1, 1, lanes, 0) for c in range(ncomp)]
        front = [shift(mid[c], mid[c], len_z - 1, 1, lanes, len_z - 1) for c in range(ncomp)]
        back_flux = (
            [shift(z_flux[0][c], z_flux[0][c], 1, 1, lanes, 0) for c in range(ncomp)],
            shift(z_flux[1], z_flux[1], 1, 1, lanes, 0),
        )
        front_flux = (
            [shift(z_flux[0][c], z_flux[0][c], len_z - 1, 1, lanes, len_z - 1) for c in range(ncomp)],
            shift(z_flux[1], z_flux[1], len_z - 1, 1, lanes, len_z - 1),
        )
        change_z = face_change(back, mid, front, back_flux, z_flux, front_flux)
        for c in range(ncomp):
            total = change[c] + change_y[c]
            total = total + change_z[c]
            out_ref[c, x] = mid[c] - ratio * total
        low, mid = mid, high
        low_flux, mid_flux = mid_flux, high_flux


def stencil(grid_cells, low_x, high_x, low_y, high_y):
    vmem = pl.BlockSpec(memory_space=pltpu.VMEM)
    return pl.pallas_call(
        stencil_kernel,
        out_shape=jax.ShapeDtypeStruct(grid_cells.shape, grid_cells.dtype),
        in_specs=[vmem] * 5,
        out_specs=vmem,
    )(grid_cells, low_x, high_x, low_y, high_y)

def fill_kernel(targets_ref, grid_ref, stacked_ref, out_ref, low_x_ref, high_x_ref, low_y_ref, high_y_ref):
    ncomp, len_x, len_y, len_z = grid_ref.shape
    per_y = len_y // BLK
    per_z = len_z // BLK
    out_ref[...] = grid_ref[...]
    helio_side = lax.axis_index("dom") == 1
    lanes = lax.broadcasted_iota(jnp.int32, (BLK, len_z), 1) // BLK
    for slot in range(stacked_ref.shape[0]):
        target = targets_ref[slot]

        @pl.when(helio_side & (target >= 0))
        def _():
            corner_x = target // (per_y * per_z) * BLK
            corner_y = pl.multiple_of(target // per_z % per_y * BLK, BLK)
            lane_hit = lanes == target % per_z
            for c in range(ncomp):
                for a in range(BLK):
                    window = (c, corner_x + a, pl.ds(corner_y, BLK), slice(None))
                    out_ref[window] = jnp.where(lane_hit, stacked_ref[slot, c, a], out_ref[window])

    low_x_ref[...] = out_ref[:, 0]
    high_x_ref[...] = out_ref[:, len_x - 1]
    for c in range(ncomp):
        for x in range(len_x):
            low_y_ref[c, pl.ds(x, 1), :] = out_ref[c, x, pl.ds(0, 1), :]
            high_y_ref[c, pl.ds(x, 1), :] = out_ref[c, x, pl.ds(len_y - 1, 1), :]


def fill_blocks(targets, grid_cells, stacked):
    ncomp, len_x, len_y, len_z = grid_cells.shape
    vmem = pl.BlockSpec(memory_space=pltpu.VMEM)
    face = jax.ShapeDtypeStruct((ncomp, len_x, len_z), grid_cells.dtype)
    return pl.pallas_call(
        fill_kernel,
        out_shape=(jax.ShapeDtypeStruct(grid_cells.shape, grid_cells.dtype),) + (face,) * 4,
        in_specs=[pl.BlockSpec(memory_space=pltpu.SMEM), vmem, vmem],
        out_specs=(vmem,) * 5,
    )(targets, grid_cells, stacked)


def halo_kernel(low_x_ref, high_x_ref, low_y_ref, high_y_ref, out_ref, landed, send_sem, recv_sem):
    column = lax.axis_index("gx")
    row = lax.axis_index("yz")
    gx_count = lax.axis_size("gx")
    yz_count = lax.axis_size("yz")
    up_x = {"gx": lax.rem(column + 1, gx_count)}
    down_x = {"gx": lax.rem(column + gx_count - 1, gx_count)}
    up_y = {"yz": lax.rem(row + 1, yz_count)}
    down_y = {"yz": lax.rem(row + yz_count - 1, yz_count)}
    barrier = pltpu.get_barrier_semaphore()
    for partner in (up_x, down_x, up_y, down_y):
        pl.semaphore_signal(barrier, inc=1, device_id=partner, device_id_type=MESH)
    pl.semaphore_wait(barrier, 4)
    sends = ((high_x_ref, up_x), (low_x_ref, down_x), (high_y_ref, up_y), (low_y_ref, down_y))
    copies = []
    for slot, (source, partner) in enumerate(sends):
        copy = pltpu.make_async_remote_copy(
            src_ref=source,
            dst_ref=landed.at[slot],
            send_sem=send_sem.at[slot],
            recv_sem=recv_sem.at[slot],
            device_id=partner,
            device_id_type=MESH,
        )
        copy.start()
        copies.append(copy)
    for copy in copies:
        copy.wait()
    out_ref[...] = landed[...]


def exchange_faces(low_x, high_x, low_y, high_y):
    face = (4,) + low_x.shape
    vmem = pl.BlockSpec(memory_space=pltpu.VMEM)
    return pl.pallas_call(
        halo_kernel,
        out_shape=jax.ShapeDtypeStruct(face, low_x.dtype),
        in_specs=[vmem] * 4,
        out_specs=vmem,
        scratch_shapes=[
            pltpu.VMEM(face, low_x.dtype),
            pltpu.SemaphoreType.DMA((4,)),
            pltpu.SemaphoreType.DMA((4,)),
        ],
        compiler_params=pltpu.CompilerParams(collective_id=1, has_side_effects=True),
    )(low_x, high_x, low_y, high_y)


def local(field_state, shell_owner, block_sources, block_targets, interp_weights):
    grid_cells = field_state[0]
    ncomp, len_x, len_y, len_z = grid_cells.shape
    domain = lax.axis_index("dom")
    column = lax.axis_index("gx")
    yz_index = lax.axis_index("yz")
    gx_count = lax.axis_size("gx")
    yz_count = lax.axis_size("yz")
    per_y = len_y // BLK
    per_z = len_z // BLK
    volume = BLK * BLK * BLK
    shell_cells = grid_cells[:, :, :, len_z - SR * BLK :]
    shell_cells = shell_cells.reshape(ncomp, len_x // BLK, BLK, per_y, BLK, SR, BLK)
    shell_cells = (
        shell_cells.transpose(1, 3, 5, 0, 2, 4, 6).reshape(-1, ncomp * volume).astype(jnp.bfloat16)
    )
    count_here = shell_cells.shape[0]
    shell_cells, owner_table = lax.optimization_barrier((shell_cells, shell_owner[0]))
    own_owner = lax.dynamic_index_in_dim(owner_table, yz_index, 0, keepdims=False)
    index_here = jnp.arange(count_here, dtype=jnp.int32)
    local_same = own_owner[None, :] == own_owner[:, None]
    rank_local = jnp.sum(
        (local_same & (index_here[None, :] < index_here[:, None])).astype(jnp.int32), axis=1
    )
    slot_of = own_owner * CAP + rank_local
    slot_count = yz_count * CAP
    select = jnp.arange(slot_count, dtype=jnp.int32)[:, None] == slot_of[None, :]
    send_cells = jnp.dot(
        select.astype(jnp.bfloat16), shell_cells, preferred_element_type=jnp.float32
    )
    send_cells = send_cells.astype(jnp.bfloat16).reshape(yz_count, CAP * ncomp, volume)
    got_cells = route_blocks(send_cells).reshape(slot_count, ncomp * volume)
    got_cells, owner_table, block_sources = lax.optimization_barrier(
        (got_cells, shell_owner[0], block_sources)
    )
    mine = (owner_table == yz_index).astype(jnp.int32)
    per_sender = jnp.sum(mine, axis=1)
    before = jnp.cumsum(per_sender) - per_sender
    rank_slot = jnp.arange(CAP, dtype=jnp.int32)
    got_tags = jnp.where(
        rank_slot[None, :] < per_sender[:, None], before[:, None] + rank_slot[None, :], -1
    ).reshape(slot_count)
    wanted = block_sources[0, 0].reshape(-1)
    match_table = (wanted[:, None] == got_tags[None, :]) & (wanted[:, None] >= 0)
    picked = jnp.dot(
        match_table.astype(jnp.bfloat16), got_cells, preferred_element_type=jnp.float32
    )
    slots_here = block_targets.shape[2]
    picked = picked.astype(jnp.bfloat16).reshape(slots_here, -1, ncomp, volume)
    interp_blocks = jnp.einsum(
        "jkcs,jkst->jct", picked, interp_weights[0, 0], preferred_element_type=jnp.float32
    )

    spread_of = lax.broadcasted_iota(jnp.int32, (BLK, len_z), 1) % BLK
    offset_of = lax.broadcasted_iota(jnp.int32, (BLK, len_z), 0)
    spread = (spread_of == offset_of).astype(jnp.float32)
    stacked = interp_blocks.reshape(slots_here * ncomp * BLK * BLK, BLK)
    stacked = jnp.dot(stacked, spread, precision=lax.Precision.HIGHEST)
    stacked = stacked.reshape(slots_here, ncomp, BLK, BLK, len_z)
    grid_cells, head_x, tail_x, head_y, tail_y = fill_blocks(block_targets[0, 0], grid_cells, stacked)
    ghosts = exchange_faces(head_x, tail_x, head_y, tail_y)
    ghost_low_x, ghost_high_x, ghost_low_y, ghost_high_y = (ghosts[n] for n in range(4))
    updated = stencil(grid_cells, ghost_low_x, ghost_high_x, ghost_low_y, ghost_high_y)
    return updated[None]


def solution(mesh):
    placed = (
        P("dom", None, "gx", "yz", None),
        P("gx", None, None),
        P("gx", "yz", None, None),
        P("gx", "yz", None),
        P("gx", "yz", None, None, None, None),
    )
    return jax.shard_map(
        local,
        mesh=mesh,
        in_specs=placed,
        out_specs=P("dom", None, "gx", "yz", None),
        check_vma=False,
    )
```

```python
import jax
import jax.numpy as jnp
from jax import lax
from jax.experimental import pallas as pl
from jax.experimental.pallas import tpu as pltpu
from jax.sharding import PartitionSpec as P

MESH = pl.DeviceIdType.MESH

BLK = 8
SR = 2
CAP = 2


HEAT_RATIO = 5.0 / 3.0
CORONA_RATIO = 0.04
HELIO_RATIO = 0.03


def direction_flux(grid_cells, direction):
    density = grid_cells[0]
    momentum = grid_cells[1:4]
    magnetic = grid_cells[4:7]
    energy = grid_cells[7]
    velocity = momentum / density
    field_sq = jnp.sum(magnetic * magnetic, axis=0)
    pressure = (HEAT_RATIO - 1.0) * (
        energy - 0.5 * jnp.sum(momentum * velocity, axis=0) - 0.5 * field_sq
    )
    total_pressure = pressure + 0.5 * field_sq
    normal_speed = velocity[direction]
    normal_field = magnetic[direction]
    velocity_dot = jnp.sum(velocity * magnetic, axis=0)
    flux_list = [momentum[direction]]
    for other in range(3):
        term = momentum[other] * normal_speed - magnetic[other] * normal_field
        if other == direction:
            term = term + total_pressure
        flux_list.append(term)
    for other in range(3):
        flux_list.append(normal_speed * magnetic[other] - normal_field * velocity[other])
    flux_list.append((energy + total_pressure) * normal_speed - normal_field * velocity_dot)
    wave_speed = jnp.abs(normal_speed) + jnp.sqrt((HEAT_RATIO * pressure + field_sq) / density)
    return (jnp.stack(flux_list), wave_speed)


def interface_change(padded_line, direction):
    phys_flux, wave_speed = direction_flux(padded_line, direction)
    array_dim = direction + 1
    cell_count = padded_line.shape[array_dim]
    low_cells = lax.slice_in_dim(padded_line, 0, cell_count - 1, axis=array_dim)
    high_cells = lax.slice_in_dim(padded_line, 1, cell_count, axis=array_dim)
    low_flux = lax.slice_in_dim(phys_flux, 0, cell_count - 1, axis=array_dim)
    high_flux = lax.slice_in_dim(phys_flux, 1, cell_count, axis=array_dim)
    low_speed = lax.slice_in_dim(wave_speed, 0, cell_count - 1, axis=direction)
    high_speed = lax.slice_in_dim(wave_speed, 1, cell_count, axis=direction)
    fastest = jnp.maximum(low_speed, high_speed)
    face_flux = 0.5 * (low_flux + high_flux) - 0.5 * fastest[None] * (high_cells - low_cells)
    upper_face = lax.slice_in_dim(face_flux, 1, cell_count - 1, axis=array_dim)
    lower_face = lax.slice_in_dim(face_flux, 0, cell_count - 2, axis=array_dim)
    return upper_face - lower_face


def advance(line_set, inner_cells, step_ratio):
    change = interface_change(line_set[0], 0) + interface_change(line_set[1], 1)
    change = change + interface_change(line_set[2], 2)
    return inner_cells - step_ratio * change


def route_kernel(send_ref, out_ref, landed, send_sem, recv_sem):
    domain = lax.axis_index("dom")
    here = lax.axis_index("yz")
    count = send_ref.shape[0]
    barrier = pltpu.get_barrier_semaphore()
    for partner in range(count):
        pl.semaphore_signal(
            barrier, inc=1, device_id={"dom": 1 - domain, "yz": partner}, device_id_type=MESH
        )
    pl.semaphore_wait(barrier, count)

    @pl.when(domain == 0)
    def _():
        copies = []
        for owner in range(count):
            copy = pltpu.make_async_remote_copy(
                src_ref=send_ref.at[owner],
                dst_ref=landed.at[here],
                send_sem=send_sem.at[owner],
                recv_sem=recv_sem.at[here],
                device_id={"dom": 1, "yz": owner},
                device_id_type=MESH,
            )
            copy.start()
            copies.append(copy)
        for copy in copies:
            copy.wait_send()
        out_ref[...] = jnp.zeros_like(out_ref)

    @pl.when(domain == 1)
    def _():
        for sender in range(count):
            pltpu.make_async_remote_copy(
                src_ref=send_ref.at[sender],
                dst_ref=landed.at[sender],
                send_sem=send_sem.at[sender],
                recv_sem=recv_sem.at[sender],
                device_id={"dom": 0, "yz": sender},
                device_id_type=MESH,
            ).wait_recv()
        out_ref[...] = landed[...]


def route_blocks(send_cells):
    count = send_cells.shape[0]
    return pl.pallas_call(
        route_kernel,
        out_shape=jax.ShapeDtypeStruct(send_cells.shape, send_cells.dtype),
        in_specs=[pl.BlockSpec(memory_space=pltpu.VMEM)],
        out_specs=pl.BlockSpec(memory_space=pltpu.VMEM),
        scratch_shapes=[
            pltpu.VMEM(send_cells.shape, send_cells.dtype),
            pltpu.SemaphoreType.DMA((count,)),
            pltpu.SemaphoreType.DMA((count,)),
        ],
        compiler_params=pltpu.CompilerParams(collective_id=0, has_side_effects=True),
    )(send_cells)


def ghost_pair(head, tail, axis, wrap):
    count = lax.axis_size(axis)
    up = [(i, i + 1) for i in range(count - 1)]
    down = [(i + 1, i) for i in range(count - 1)]
    if wrap:
        up.append((count - 1, 0))
        down.append((0, count - 1))
    return lax.ppermute(tail, axis, up), lax.ppermute(head, axis, down)

def cell_flux(parts, direction):
    density = parts[0]
    momentum = parts[1:4]
    magnetic = parts[4:7]
    energy = parts[7]
    velocity = [m / density for m in momentum]
    field_sq = magnetic[0] * magnetic[0] + magnetic[1] * magnetic[1] + magnetic[2] * magnetic[2]
    kinetic = momentum[0] * velocity[0] + momentum[1] * velocity[1] + momentum[2] * velocity[2]
    pressure = (HEAT_RATIO - 1.0) * (energy - 0.5 * kinetic - 0.5 * field_sq)
    total_pressure = pressure + 0.5 * field_sq
    normal_speed = velocity[direction]
    normal_field = magnetic[direction]
    velocity_dot = velocity[0] * magnetic[0] + velocity[1] * magnetic[1] + velocity[2] * magnetic[2]
    flux = [momentum[direction]]
    for other in range(3):
        term = momentum[other] * normal_speed - magnetic[other] * normal_field
        if other == direction:
            term = term + total_pressure
        flux.append(term)
    for other in range(3):
        flux.append(normal_speed * magnetic[other] - normal_field * velocity[other])
    flux.append((energy + total_pressure) * normal_speed - normal_field * velocity_dot)
    speed = jnp.abs(normal_speed) + jnp.sqrt((HEAT_RATIO * pressure + field_sq) / density)
    return flux, speed


def face_change(low, mid, high, low_flux, mid_flux, high_flux):
    (fl, sl), (fm, sm), (fh, sh) = low_flux, mid_flux, high_flux
    fast_low = jnp.maximum(sl, sm)
    fast_high = jnp.maximum(sm, sh)
    change = []
    for c in range(len(mid)):
        upper = 0.5 * (fm[c] + fh[c]) - 0.5 * fast_high * (high[c] - mid[c])
        lower = 0.5 * (fl[c] + fm[c]) - 0.5 * fast_low * (mid[c] - low[c])
        change.append(upper - lower)
    return change


def stencil_kernel(grid_ref, low_x_ref, high_x_ref, low_y_ref, high_y_ref, out_ref):
    ncomp, len_x, len_y, len_z = grid_ref.shape
    domain = lax.axis_index("dom")
    column = lax.axis_index("gx")
    row = lax.axis_index("yz")
    helio_side = domain == 1
    fix_low_x = helio_side & (column == 0)
    fix_high_x = helio_side & (column == lax.axis_size("gx") - 1)
    fix_low_y = row == 0
    fix_high_y = row == lax.axis_size("yz") - 1
    ratio = jnp.where(domain == 0, CORONA_RATIO, HELIO_RATIO).astype(jnp.float32)
    rows = lax.broadcasted_iota(jnp.int32, (len_y, len_z), 0)
    lanes = lax.broadcasted_iota(jnp.int32, (len_y, len_z), 1)

    def plane(x):
        if x < 0:
            return [jnp.where(fix_low_x, grid_ref[c, 0], low_x_ref[c]) for c in range(ncomp)]
        if x >= len_x:
            return [
                jnp.where(fix_high_x, grid_ref[c, len_x - 1], high_x_ref[c]) for c in range(ncomp)
            ]
        return [grid_ref[c, x] for c in range(ncomp)]

    def shift(values, edge, step, axis, index, last):
        moved = pltpu.roll(values, step, axis)
        return jnp.where(index == last, edge, moved)

    low = plane(-1)
    mid = plane(0)
    low_flux = cell_flux(low, 0)
    mid_flux = cell_flux(mid, 0)
    for x in range(len_x):
        high = plane(x + 1)
        high_flux = cell_flux(high, 0)
        change = face_change(low, mid, high, low_flux, mid_flux, high_flux)
        y_low = [
            jnp.where(fix_low_y, grid_ref[c, x, pl.ds(0, 1), :], low_y_ref[c, pl.ds(x, 1), :])
            for c in range(ncomp)
        ]
        y_high = [
            jnp.where(
                fix_high_y, grid_ref[c, x, pl.ds(len_y - 1, 1), :], high_y_ref[c, pl.ds(x, 1), :]
            )
            for c in range(ncomp)
        ]
        y_flux = cell_flux(mid, 1)
        y_low_flux = cell_flux(y_low, 1)
        y_high_flux = cell_flux(y_high, 1)
        down = [shift(mid[c], y_low[c], 1, 0, rows, 0) for c in range(ncomp)]
        up = [shift(mid[c], y_high[c], len_y - 1, 0, rows, len_y - 1) for c in range(ncomp)]
        down_flux = (
            [shift(y_flux[0][c], y_low_flux[0][c], 1, 0, rows, 0) for c in range(ncomp)],
            shift(y_flux[1], y_low_flux[1], 1, 0, rows, 0),
        )
        up_flux = (
            [shift(y_flux[0][c], y_high_flux[0][c], len_y - 1, 0, rows, len_y - 1) for c in range(ncomp)],
            shift(y_flux[1], y_high_flux[1], len_y - 1, 0, rows, len_y - 1),
        )
        change_y = face_change(down, mid, up, down_flux, y_flux, up_flux)
        z_flux = cell_flux(mid, 2)
        back = [shift(mid[c], mid[c], 1, 1, lanes, 0) for c in range(ncomp)]
        front = [shift(mid[c], mid[c], len_z - 1, 1, lanes, len_z - 1) for c in range(ncomp)]
        back_flux = (
            [shift(z_flux[0][c], z_flux[0][c], 1, 1, lanes, 0) for c in range(ncomp)],
            shift(z_flux[1], z_flux[1], 1, 1, lanes, 0),
        )
        front_flux = (
            [shift(z_flux[0][c], z_flux[0][c], len_z - 1, 1, lanes, len_z - 1) for c in range(ncomp)],
            shift(z_flux[1], z_flux[1], len_z - 1, 1, lanes, len_z - 1),
        )
        change_z = face_change(back, mid, front, back_flux, z_flux, front_flux)
        for c in range(ncomp):
            total = change[c] + change_y[c]
            total = total + change_z[c]
            out_ref[c, x] = mid[c] - ratio * total
        low, mid = mid, high
        low_flux, mid_flux = mid_flux, high_flux


def stencil(grid_cells, low_x, high_x, low_y, high_y):
    vmem = pl.BlockSpec(memory_space=pltpu.VMEM)
    return pl.pallas_call(
        stencil_kernel,
        out_shape=jax.ShapeDtypeStruct(grid_cells.shape, grid_cells.dtype),
        in_specs=[vmem] * 5,
        out_specs=vmem,
    )(grid_cells, low_x, high_x, low_y, high_y)

def fill_kernel(targets_ref, grid_ref, stacked_ref, out_ref, low_x_ref, high_x_ref, low_y_ref, high_y_ref):
    ncomp, len_x, len_y, len_z = grid_ref.shape
    per_y = len_y // BLK
    per_z = len_z // BLK
    out_ref[...] = grid_ref[...]
    helio_side = lax.axis_index("dom") == 1
    lanes = lax.broadcasted_iota(jnp.int32, (BLK, len_z), 1) // BLK
    for slot in range(stacked_ref.shape[0]):
        target = targets_ref[slot]

        @pl.when(helio_side & (target >= 0))
        def _():
            corner_x = target // (per_y * per_z) * BLK
            corner_y = pl.multiple_of(target // per_z % per_y * BLK, BLK)
            lane_hit = lanes == target % per_z
            for c in range(ncomp):
                for a in range(BLK):
                    window = (c, corner_x + a, pl.ds(corner_y, BLK), slice(None))
                    out_ref[window] = jnp.where(lane_hit, stacked_ref[slot, c, a], out_ref[window])

    low_x_ref[...] = out_ref[:, 0]
    high_x_ref[...] = out_ref[:, len_x - 1]
    for c in range(ncomp):
        for x in range(len_x):
            low_y_ref[c, pl.ds(x, 1), :] = out_ref[c, x, pl.ds(0, 1), :]
            high_y_ref[c, pl.ds(x, 1), :] = out_ref[c, x, pl.ds(len_y - 1, 1), :]


def fill_blocks(targets, grid_cells, stacked):
    ncomp, len_x, len_y, len_z = grid_cells.shape
    vmem = pl.BlockSpec(memory_space=pltpu.VMEM)
    face = jax.ShapeDtypeStruct((ncomp, len_x, len_z), grid_cells.dtype)
    return pl.pallas_call(
        fill_kernel,
        out_shape=(jax.ShapeDtypeStruct(grid_cells.shape, grid_cells.dtype),) + (face,) * 4,
        in_specs=[pl.BlockSpec(memory_space=pltpu.SMEM), vmem, vmem],
        out_specs=(vmem,) * 5,
    )(targets, grid_cells, stacked)


def local(field_state, shell_owner, block_sources, block_targets, interp_weights):
    grid_cells = field_state[0]
    ncomp, len_x, len_y, len_z = grid_cells.shape
    domain = lax.axis_index("dom")
    column = lax.axis_index("gx")
    yz_index = lax.axis_index("yz")
    gx_count = lax.axis_size("gx")
    yz_count = lax.axis_size("yz")
    per_y = len_y // BLK
    per_z = len_z // BLK
    volume = BLK * BLK * BLK
    shell_cells = grid_cells[:, :, :, len_z - SR * BLK :]
    shell_cells = shell_cells.reshape(ncomp, len_x // BLK, BLK, per_y, BLK, SR, BLK)
    shell_cells = (
        shell_cells.transpose(1, 3, 5, 0, 2, 4, 6).reshape(-1, ncomp * volume).astype(jnp.bfloat16)
    )
    count_here = shell_cells.shape[0]
    shell_cells, owner_table = lax.optimization_barrier((shell_cells, shell_owner[0]))
    own_owner = lax.dynamic_index_in_dim(owner_table, yz_index, 0, keepdims=False)
    index_here = jnp.arange(count_here, dtype=jnp.int32)
    local_same = own_owner[None, :] == own_owner[:, None]
    rank_local = jnp.sum(
        (local_same & (index_here[None, :] < index_here[:, None])).astype(jnp.int32), axis=1
    )
    slot_of = own_owner * CAP + rank_local
    slot_count = yz_count * CAP
    select = jnp.arange(slot_count, dtype=jnp.int32)[:, None] == slot_of[None, :]
    send_cells = jnp.dot(
        select.astype(jnp.bfloat16), shell_cells, preferred_element_type=jnp.float32
    )
    send_cells = send_cells.astype(jnp.bfloat16).reshape(yz_count, CAP * ncomp, volume)
    got_cells = route_blocks(send_cells).reshape(slot_count, ncomp * volume)
    got_cells, owner_table, block_sources = lax.optimization_barrier(
        (got_cells, shell_owner[0], block_sources)
    )
    mine = (owner_table == yz_index).astype(jnp.int32)
    per_sender = jnp.sum(mine, axis=1)
    before = jnp.cumsum(per_sender) - per_sender
    rank_slot = jnp.arange(CAP, dtype=jnp.int32)
    got_tags = jnp.where(
        rank_slot[None, :] < per_sender[:, None], before[:, None] + rank_slot[None, :], -1
    ).reshape(slot_count)
    wanted = block_sources[0, 0].reshape(-1)
    match_table = (wanted[:, None] == got_tags[None, :]) & (wanted[:, None] >= 0)
    picked = jnp.dot(
        match_table.astype(jnp.bfloat16), got_cells, preferred_element_type=jnp.float32
    )
    slots_here = block_targets.shape[2]
    picked = picked.astype(jnp.bfloat16).reshape(slots_here, -1, ncomp, volume)
    interp_blocks = jnp.einsum(
        "jkcs,jkst->jct", picked, interp_weights[0, 0], preferred_element_type=jnp.float32
    )

    spread_of = lax.broadcasted_iota(jnp.int32, (BLK, len_z), 1) % BLK
    offset_of = lax.broadcasted_iota(jnp.int32, (BLK, len_z), 0)
    spread = (spread_of == offset_of).astype(jnp.float32)
    stacked = interp_blocks.reshape(slots_here * ncomp * BLK * BLK, BLK)
    stacked = jnp.dot(stacked, spread, precision=lax.Precision.HIGHEST)
    stacked = stacked.reshape(slots_here, ncomp, BLK, BLK, len_z)
    grid_cells, head_x, tail_x, head_y, tail_y = fill_blocks(block_targets[0, 0], grid_cells, stacked)
    ghost_low_x, ghost_high_x = ghost_pair(head_x, tail_x, "gx", True)
    ghost_low_y, ghost_high_y = ghost_pair(head_y, tail_y, "yz", False)
    updated = stencil(grid_cells, ghost_low_x, ghost_high_x, ghost_low_y, ghost_high_y)
    return updated[None]


def solution(mesh):
    placed = (
        P("dom", None, "gx", "yz", None),
        P("gx", None, None),
        P("gx", "yz", None, None),
        P("gx", "yz", None),
        P("gx", "yz", None, None, None, None),
    )
    return jax.shard_map(
        local,
        mesh=mesh,
        in_specs=placed,
        out_specs=P("dom", None, "gx", "yz", None),
        check_vma=False,
    )
```

```python
import jax
import jax.numpy as jnp
from jax import lax
from jax.experimental import pallas as pl
from jax.experimental.pallas import tpu as pltpu
from jax.sharding import PartitionSpec as P

MESH = pl.DeviceIdType.MESH

BLK = 8
SR = 2
CAP = 2


HEAT_RATIO = 5.0 / 3.0
CORONA_RATIO = 0.04
HELIO_RATIO = 0.03


def direction_flux(grid_cells, direction):
    density = grid_cells[0]
    momentum = grid_cells[1:4]
    magnetic = grid_cells[4:7]
    energy = grid_cells[7]
    velocity = momentum / density
    field_sq = jnp.sum(magnetic * magnetic, axis=0)
    pressure = (HEAT_RATIO - 1.0) * (
        energy - 0.5 * jnp.sum(momentum * velocity, axis=0) - 0.5 * field_sq
    )
    total_pressure = pressure + 0.5 * field_sq
    normal_speed = velocity[direction]
    normal_field = magnetic[direction]
    velocity_dot = jnp.sum(velocity * magnetic, axis=0)
    flux_list = [momentum[direction]]
    for other in range(3):
        term = momentum[other] * normal_speed - magnetic[other] * normal_field
        if other == direction:
            term = term + total_pressure
        flux_list.append(term)
    for other in range(3):
        flux_list.append(normal_speed * magnetic[other] - normal_field * velocity[other])
    flux_list.append((energy + total_pressure) * normal_speed - normal_field * velocity_dot)
    wave_speed = jnp.abs(normal_speed) + jnp.sqrt((HEAT_RATIO * pressure + field_sq) / density)
    return (jnp.stack(flux_list), wave_speed)


def interface_change(padded_line, direction):
    phys_flux, wave_speed = direction_flux(padded_line, direction)
    array_dim = direction + 1
    cell_count = padded_line.shape[array_dim]
    low_cells = lax.slice_in_dim(padded_line, 0, cell_count - 1, axis=array_dim)
    high_cells = lax.slice_in_dim(padded_line, 1, cell_count, axis=array_dim)
    low_flux = lax.slice_in_dim(phys_flux, 0, cell_count - 1, axis=array_dim)
    high_flux = lax.slice_in_dim(phys_flux, 1, cell_count, axis=array_dim)
    low_speed = lax.slice_in_dim(wave_speed, 0, cell_count - 1, axis=direction)
    high_speed = lax.slice_in_dim(wave_speed, 1, cell_count, axis=direction)
    fastest = jnp.maximum(low_speed, high_speed)
    face_flux = 0.5 * (low_flux + high_flux) - 0.5 * fastest[None] * (high_cells - low_cells)
    upper_face = lax.slice_in_dim(face_flux, 1, cell_count - 1, axis=array_dim)
    lower_face = lax.slice_in_dim(face_flux, 0, cell_count - 2, axis=array_dim)
    return upper_face - lower_face


def advance(line_set, inner_cells, step_ratio):
    change = interface_change(line_set[0], 0) + interface_change(line_set[1], 1)
    change = change + interface_change(line_set[2], 2)
    return inner_cells - step_ratio * change


def route_kernel(send_ref, out_ref, landed, send_sem, recv_sem):
    domain = lax.axis_index("dom")
    here = lax.axis_index("yz")
    count = send_ref.shape[0]
    barrier = pltpu.get_barrier_semaphore()
    for partner in range(count):
        pl.semaphore_signal(
            barrier, inc=1, device_id={"dom": 1 - domain, "yz": partner}, device_id_type=MESH
        )
    pl.semaphore_wait(barrier, count)

    @pl.when(domain == 0)
    def _():
        copies = []
        for owner in range(count):
            copy = pltpu.make_async_remote_copy(
                src_ref=send_ref.at[owner],
                dst_ref=landed.at[here],
                send_sem=send_sem.at[owner],
                recv_sem=recv_sem.at[here],
                device_id={"dom": 1, "yz": owner},
                device_id_type=MESH,
            )
            copy.start()
            copies.append(copy)
        for copy in copies:
            copy.wait_send()
        out_ref[...] = jnp.zeros_like(out_ref)

    @pl.when(domain == 1)
    def _():
        for sender in range(count):
            pltpu.make_async_remote_copy(
                src_ref=send_ref.at[sender],
                dst_ref=landed.at[sender],
                send_sem=send_sem.at[sender],
                recv_sem=recv_sem.at[sender],
                device_id={"dom": 0, "yz": sender},
                device_id_type=MESH,
            ).wait_recv()
        out_ref[...] = landed[...]


def route_blocks(send_cells):
    count = send_cells.shape[0]
    return pl.pallas_call(
        route_kernel,
        out_shape=jax.ShapeDtypeStruct(send_cells.shape, send_cells.dtype),
        in_specs=[pl.BlockSpec(memory_space=pltpu.VMEM)],
        out_specs=pl.BlockSpec(memory_space=pltpu.VMEM),
        scratch_shapes=[
            pltpu.VMEM(send_cells.shape, send_cells.dtype),
            pltpu.SemaphoreType.DMA((count,)),
            pltpu.SemaphoreType.DMA((count,)),
        ],
        compiler_params=pltpu.CompilerParams(collective_id=0, has_side_effects=True),
    )(send_cells)


def ghost_pair(cells, axis, dim, wrap, fix_low, fix_high):
    count = lax.axis_size(axis)
    size = cells.shape[dim]
    head = lax.slice_in_dim(cells, 0, 1, axis=dim)
    tail = lax.slice_in_dim(cells, size - 1, size, axis=dim)
    up = [(i, i + 1) for i in range(count - 1)]
    down = [(i + 1, i) for i in range(count - 1)]
    if wrap:
        up.append((count - 1, 0))
        down.append((0, count - 1))
    from_low = lax.ppermute(tail, axis, up)
    from_high = lax.ppermute(head, axis, down)
    low = jnp.where(fix_low, head, from_low)
    high = jnp.where(fix_high, tail, from_high)
    return jnp.concatenate([low, cells, high], axis=dim)


def interp_kernel(picked_ref, weights_ref, out_ref):
    slots, sources = picked_ref.shape[0], picked_ref.shape[1]
    for slot in range(slots):
        total = jnp.dot(
            picked_ref[slot, 0], weights_ref[slot, 0], preferred_element_type=jnp.float32
        )
        for source in range(1, sources):
            total = total + jnp.dot(
                picked_ref[slot, source], weights_ref[slot, source],
                preferred_element_type=jnp.float32,
            )
        out_ref[slot] = total


def interpolate(picked, weights):
    slots, sources, ncomp, cells = picked.shape
    vmem = pl.BlockSpec(memory_space=pltpu.VMEM)
    return pl.pallas_call(
        interp_kernel,
        out_shape=jax.ShapeDtypeStruct((slots, ncomp, weights.shape[-1]), jnp.float32),
        in_specs=[vmem, vmem],
        out_specs=vmem,
    )(picked, weights)


def local(field_state, shell_owner, block_sources, block_targets, interp_weights):
    grid_cells = field_state[0]
    ncomp, len_x, len_y, len_z = grid_cells.shape
    domain = lax.axis_index("dom")
    column = lax.axis_index("gx")
    yz_index = lax.axis_index("yz")
    gx_count = lax.axis_size("gx")
    yz_count = lax.axis_size("yz")
    per_y = len_y // BLK
    per_z = len_z // BLK
    volume = BLK * BLK * BLK
    shell_cells = grid_cells[:, :, :, len_z - SR * BLK :]
    shell_cells = shell_cells.reshape(ncomp, len_x // BLK, BLK, per_y, BLK, SR, BLK)
    shell_cells = (
        shell_cells.transpose(1, 3, 5, 0, 2, 4, 6).reshape(-1, ncomp * volume).astype(jnp.bfloat16)
    )
    count_here = shell_cells.shape[0]
    owner_table = shell_owner[0]
    own_owner = lax.dynamic_index_in_dim(owner_table, yz_index, 0, keepdims=False)
    index_here = jnp.arange(count_here, dtype=jnp.int32)
    local_same = own_owner[None, :] == own_owner[:, None]
    rank_local = jnp.sum(
        (local_same & (index_here[None, :] < index_here[:, None])).astype(jnp.int32), axis=1
    )
    slot_of = own_owner * CAP + rank_local
    slot_count = yz_count * CAP
    select = jnp.arange(slot_count, dtype=jnp.int32)[:, None] == slot_of[None, :]
    send_cells = jnp.dot(
        select.astype(jnp.bfloat16), shell_cells, preferred_element_type=jnp.float32
    )
    send_cells = send_cells.astype(jnp.bfloat16).reshape(yz_count, CAP * ncomp, volume)
    got_cells = route_blocks(send_cells).reshape(slot_count, ncomp * volume)
    mine = (owner_table == yz_index).astype(jnp.int32)
    per_sender = jnp.sum(mine, axis=1)
    before = jnp.cumsum(per_sender) - per_sender
    rank_slot = jnp.arange(CAP, dtype=jnp.int32)
    got_tags = jnp.where(
        rank_slot[None, :] < per_sender[:, None], before[:, None] + rank_slot[None, :], -1
    ).reshape(slot_count)
    wanted = block_sources[0, 0].reshape(-1)
    match_table = (wanted[:, None] == got_tags[None, :]) & (wanted[:, None] >= 0)
    picked = jnp.dot(
        match_table.astype(jnp.bfloat16), got_cells, preferred_element_type=jnp.float32
    )
    slots_here = block_targets.shape[2]
    picked = picked.astype(jnp.bfloat16).reshape(slots_here, -1, ncomp, volume)
    interp_blocks = interpolate(picked, interp_weights[0, 0])

    rows = lax.broadcasted_iota(jnp.int32, (len_x, len_y, len_z), 0) // BLK
    cols = lax.broadcasted_iota(jnp.int32, (len_x, len_y, len_z), 1) // BLK
    lanes = lax.broadcasted_iota(jnp.int32, (len_x, len_y, len_z), 2)
    spread_of = lax.broadcasted_iota(jnp.int32, (BLK, len_z), 1) % BLK
    offset_of = lax.broadcasted_iota(jnp.int32, (BLK, len_z), 0)
    spread = (spread_of == offset_of).astype(jnp.float32)
    stacked = interp_blocks.reshape(slots_here * ncomp * BLK * BLK, BLK)
    stacked = jnp.dot(stacked, spread, precision=lax.Precision.HIGHEST)
    stacked = stacked.reshape(slots_here, ncomp, BLK, BLK, len_z)
    targets = jnp.where(domain == 1, block_targets[0, 0], -1)
    spots = jnp.maximum(targets, 0)
    hit = (
        (rows[None] == (spots // (per_y * per_z))[:, None, None, None])
        & (cols[None] == (spots // per_z % per_y)[:, None, None, None])
        & (lanes[None] // BLK == (spots % per_z)[:, None, None, None])
        & (targets >= 0)[:, None, None, None]
    )
    for slot_number in range(slots_here):
        placed = jnp.tile(stacked[slot_number], (1, len_x // BLK, len_y // BLK, 1))
        grid_cells = jnp.where(hit[slot_number][None], placed, grid_cells)

    helio_side = domain == 1
    low_x = helio_side & (column == 0)
    high_x = helio_side & (column == gx_count - 1)
    low_y = yz_index == 0
    high_y = yz_index == yz_count - 1
    line_x = ghost_pair(grid_cells, "gx", 1, True, low_x, high_x)
    line_y = ghost_pair(grid_cells, "yz", 2, False, low_y, high_y)
    line_z = jnp.pad(grid_cells, ((0, 0), (0, 0), (0, 0), (1, 1)), mode="edge")
    step_ratio = jnp.where(domain == 0, CORONA_RATIO, HELIO_RATIO).astype(jnp.float32)
    updated = advance((line_x, line_y, line_z), grid_cells, step_ratio)
    return updated[None]


def solution(mesh):
    placed = (
        P("dom", None, "gx", "yz", None),
        P("gx", None, None),
        P("gx", "yz", None, None),
        P("gx", "yz", None),
        P("gx", "yz", None, None, None, None),
    )
    return jax.shard_map(
        local,
        mesh=mesh,
        in_specs=placed,
        out_specs=P("dom", None, "gx", "yz", None),
        check_vma=False,
    )
```

```python
import jax
import jax.numpy as jnp
from jax import lax
from jax.experimental import pallas as pl
from jax.experimental.pallas import tpu as pltpu
from jax.sharding import PartitionSpec as P

MESH = pl.DeviceIdType.MESH

BLK = 8
SR = 2
CAP = 2


HEAT_RATIO = 5.0 / 3.0
CORONA_RATIO = 0.04
HELIO_RATIO = 0.03


def direction_flux(grid_cells, direction):
    density = grid_cells[0]
    momentum = grid_cells[1:4]
    magnetic = grid_cells[4:7]
    energy = grid_cells[7]
    velocity = momentum / density
    field_sq = jnp.sum(magnetic * magnetic, axis=0)
    pressure = (HEAT_RATIO - 1.0) * (
        energy - 0.5 * jnp.sum(momentum * velocity, axis=0) - 0.5 * field_sq
    )
    total_pressure = pressure + 0.5 * field_sq
    normal_speed = velocity[direction]
    normal_field = magnetic[direction]
    velocity_dot = jnp.sum(velocity * magnetic, axis=0)
    flux_list = [momentum[direction]]
    for other in range(3):
        term = momentum[other] * normal_speed - magnetic[other] * normal_field
        if other == direction:
            term = term + total_pressure
        flux_list.append(term)
    for other in range(3):
        flux_list.append(normal_speed * magnetic[other] - normal_field * velocity[other])
    flux_list.append((energy + total_pressure) * normal_speed - normal_field * velocity_dot)
    wave_speed = jnp.abs(normal_speed) + jnp.sqrt((HEAT_RATIO * pressure + field_sq) / density)
    return (jnp.stack(flux_list), wave_speed)


def interface_change(padded_line, direction):
    phys_flux, wave_speed = direction_flux(padded_line, direction)
    array_dim = direction + 1
    cell_count = padded_line.shape[array_dim]
    low_cells = lax.slice_in_dim(padded_line, 0, cell_count - 1, axis=array_dim)
    high_cells = lax.slice_in_dim(padded_line, 1, cell_count, axis=array_dim)
    low_flux = lax.slice_in_dim(phys_flux, 0, cell_count - 1, axis=array_dim)
    high_flux = lax.slice_in_dim(phys_flux, 1, cell_count, axis=array_dim)
    low_speed = lax.slice_in_dim(wave_speed, 0, cell_count - 1, axis=direction)
    high_speed = lax.slice_in_dim(wave_speed, 1, cell_count, axis=direction)
    fastest = jnp.maximum(low_speed, high_speed)
    face_flux = 0.5 * (low_flux + high_flux) - 0.5 * fastest[None] * (high_cells - low_cells)
    upper_face = lax.slice_in_dim(face_flux, 1, cell_count - 1, axis=array_dim)
    lower_face = lax.slice_in_dim(face_flux, 0, cell_count - 2, axis=array_dim)
    return upper_face - lower_face


def advance(line_set, inner_cells, step_ratio):
    change = interface_change(line_set[0], 0) + interface_change(line_set[1], 1)
    change = change + interface_change(line_set[2], 2)
    return inner_cells - step_ratio * change


def route_kernel(send_ref, out_ref, landed, send_sem, recv_sem):
    domain = lax.axis_index("dom")
    here = lax.axis_index("yz")
    count = send_ref.shape[0]
    barrier = pltpu.get_barrier_semaphore()
    for partner in range(count):
        pl.semaphore_signal(
            barrier, inc=1, device_id={"dom": 1 - domain, "yz": partner}, device_id_type=MESH
        )
    pl.semaphore_wait(barrier, count)

    @pl.when(domain == 0)
    def _():
        copies = []
        for owner in range(count):
            copy = pltpu.make_async_remote_copy(
                src_ref=send_ref.at[owner],
                dst_ref=landed.at[here],
                send_sem=send_sem.at[owner],
                recv_sem=recv_sem.at[here],
                device_id={"dom": 1, "yz": owner},
                device_id_type=MESH,
            )
            copy.start()
            copies.append(copy)
        for copy in copies:
            copy.wait_send()
        out_ref[...] = jnp.zeros_like(out_ref)

    @pl.when(domain == 1)
    def _():
        for sender in range(count):
            pltpu.make_async_remote_copy(
                src_ref=send_ref.at[sender],
                dst_ref=landed.at[sender],
                send_sem=send_sem.at[sender],
                recv_sem=recv_sem.at[sender],
                device_id={"dom": 0, "yz": sender},
                device_id_type=MESH,
            ).wait_recv()
        out_ref[...] = landed[...]


def route_blocks(send_cells):
    count = send_cells.shape[0]
    return pl.pallas_call(
        route_kernel,
        out_shape=jax.ShapeDtypeStruct(send_cells.shape, send_cells.dtype),
        in_specs=[pl.BlockSpec(memory_space=pltpu.VMEM)],
        out_specs=pl.BlockSpec(memory_space=pltpu.VMEM),
        scratch_shapes=[
            pltpu.VMEM(send_cells.shape, send_cells.dtype),
            pltpu.SemaphoreType.DMA((count,)),
            pltpu.SemaphoreType.DMA((count,)),
        ],
        compiler_params=pltpu.CompilerParams(collective_id=0, has_side_effects=True),
    )(send_cells)


def ghost_pair(cells, axis, dim, wrap, fix_low, fix_high):
    count = lax.axis_size(axis)
    size = cells.shape[dim]
    head = lax.slice_in_dim(cells, 0, 1, axis=dim)
    tail = lax.slice_in_dim(cells, size - 1, size, axis=dim)
    up = [(i, i + 1) for i in range(count - 1)]
    down = [(i + 1, i) for i in range(count - 1)]
    if wrap:
        up.append((count - 1, 0))
        down.append((0, count - 1))
    from_low = lax.ppermute(tail, axis, up)
    from_high = lax.ppermute(head, axis, down)
    low = jnp.where(fix_low, head, from_low)
    high = jnp.where(fix_high, tail, from_high)
    return jnp.concatenate([low, cells, high], axis=dim)


def local(field_state, shell_owner, block_sources, block_targets, interp_weights):
    grid_cells = field_state[0]
    ncomp, len_x, len_y, len_z = grid_cells.shape
    domain = lax.axis_index("dom")
    column = lax.axis_index("gx")
    yz_index = lax.axis_index("yz")
    gx_count = lax.axis_size("gx")
    yz_count = lax.axis_size("yz")
    per_y = len_y // BLK
    per_z = len_z // BLK
    volume = BLK * BLK * BLK
    shell_cells = grid_cells[:, :, :, len_z - SR * BLK :]
    shell_cells = shell_cells.reshape(ncomp, len_x // BLK, BLK, per_y, BLK, SR, BLK)
    shell_cells = (
        shell_cells.transpose(1, 3, 5, 0, 2, 4, 6).reshape(-1, ncomp * volume).astype(jnp.bfloat16)
    )
    count_here = shell_cells.shape[0]
    owner_table = shell_owner[0]
    own_owner = lax.dynamic_index_in_dim(owner_table, yz_index, 0, keepdims=False)
    index_here = jnp.arange(count_here, dtype=jnp.int32)
    local_same = own_owner[None, :] == own_owner[:, None]
    rank_local = jnp.sum(
        (local_same & (index_here[None, :] < index_here[:, None])).astype(jnp.int32), axis=1
    )
    slot_of = own_owner * CAP + rank_local
    slot_count = yz_count * CAP
    select = jnp.arange(slot_count, dtype=jnp.int32)[:, None] == slot_of[None, :]
    send_cells = jnp.dot(
        select.astype(jnp.bfloat16), shell_cells, preferred_element_type=jnp.float32
    )
    send_cells = send_cells.astype(jnp.bfloat16).reshape(yz_count, CAP * ncomp, volume)
    got_cells = route_blocks(send_cells).reshape(slot_count, ncomp, volume)
    mine = (owner_table == yz_index).astype(jnp.int32)
    per_sender = jnp.sum(mine, axis=1)
    before = jnp.cumsum(per_sender) - per_sender
    rank_slot = jnp.arange(CAP, dtype=jnp.int32)
    got_tags = jnp.where(
        rank_slot[None, :] < per_sender[:, None], before[:, None] + rank_slot[None, :], -1
    ).reshape(slot_count)
    wanted = block_sources[0, 0].reshape(-1)
    match_table = (wanted[:, None] == got_tags[None, :]) & (wanted[:, None] >= 0)
    picked = jnp.einsum(
        "ws,scv->wcv", match_table.astype(jnp.bfloat16), got_cells,
        preferred_element_type=jnp.float32,
    )
    slots_here = block_targets.shape[2]
    picked = picked.astype(jnp.bfloat16).reshape(slots_here, -1, ncomp, volume)
    interp_blocks = jnp.einsum(
        "jkcs,jkst->jct", picked, interp_weights[0, 0], preferred_element_type=jnp.float32
    )

    rows = lax.broadcasted_iota(jnp.int32, (len_x, len_y, len_z), 0) // BLK
    cols = lax.broadcasted_iota(jnp.int32, (len_x, len_y, len_z), 1) // BLK
    lanes = lax.broadcasted_iota(jnp.int32, (len_x, len_y, len_z), 2)
    spread_of = lax.broadcasted_iota(jnp.int32, (BLK, len_z), 1) % BLK
    offset_of = lax.broadcasted_iota(jnp.int32, (BLK, len_z), 0)
    spread = (spread_of == offset_of).astype(jnp.float32)
    stacked = interp_blocks.reshape(slots_here * ncomp * BLK * BLK, BLK)
    stacked = jnp.dot(stacked, spread, precision=lax.Precision.HIGHEST)
    stacked = stacked.reshape(slots_here, ncomp, BLK, BLK, len_z)
    targets = jnp.where(domain == 1, block_targets[0, 0], -1)
    spots = jnp.maximum(targets, 0)
    hit = (
        (rows[None] == (spots // (per_y * per_z))[:, None, None, None])
        & (cols[None] == (spots // per_z % per_y)[:, None, None, None])
        & (lanes[None] // BLK == (spots % per_z)[:, None, None, None])
        & (targets >= 0)[:, None, None, None]
    )
    for slot_number in range(slots_here):
        placed = jnp.tile(stacked[slot_number], (1, len_x // BLK, len_y // BLK, 1))
        grid_cells = jnp.where(hit[slot_number][None], placed, grid_cells)

    helio_side = domain == 1
    low_x = helio_side & (column == 0)
    high_x = helio_side & (column == gx_count - 1)
    low_y = yz_index == 0
    high_y = yz_index == yz_count - 1
    line_x = ghost_pair(grid_cells, "gx", 1, True, low_x, high_x)
    line_y = ghost_pair(grid_cells, "yz", 2, False, low_y, high_y)
    line_z = jnp.pad(grid_cells, ((0, 0), (0, 0), (0, 0), (1, 1)), mode="edge")
    step_ratio = jnp.where(domain == 0, CORONA_RATIO, HELIO_RATIO).astype(jnp.float32)
    updated = advance((line_x, line_y, line_z), grid_cells, step_ratio)
    return updated[None]


def solution(mesh):
    placed = (
        P("dom", None, "gx", "yz", None),
        P("gx", None, None),
        P("gx", "yz", None, None),
        P("gx", "yz", None),
        P("gx", "yz", None, None, None, None),
    )
    return jax.shard_map(
        local,
        mesh=mesh,
        in_specs=placed,
        out_specs=P("dom", None, "gx", "yz", None),
        check_vma=False,
    )
```

```python
import jax
import jax.numpy as jnp
from jax import lax
from jax.experimental import pallas as pl
from jax.experimental.pallas import tpu as pltpu
from jax.sharding import PartitionSpec as P

MESH = pl.DeviceIdType.MESH

BLK = 8
SR = 2
CAP = 2


HEAT_RATIO = 5.0 / 3.0
CORONA_RATIO = 0.04
HELIO_RATIO = 0.03


def direction_flux(grid_cells, direction):
    density = grid_cells[0]
    momentum = grid_cells[1:4]
    magnetic = grid_cells[4:7]
    energy = grid_cells[7]
    velocity = momentum / density
    field_sq = jnp.sum(magnetic * magnetic, axis=0)
    pressure = (HEAT_RATIO - 1.0) * (
        energy - 0.5 * jnp.sum(momentum * velocity, axis=0) - 0.5 * field_sq
    )
    total_pressure = pressure + 0.5 * field_sq
    normal_speed = velocity[direction]
    normal_field = magnetic[direction]
    velocity_dot = jnp.sum(velocity * magnetic, axis=0)
    flux_list = [momentum[direction]]
    for other in range(3):
        term = momentum[other] * normal_speed - magnetic[other] * normal_field
        if other == direction:
            term = term + total_pressure
        flux_list.append(term)
    for other in range(3):
        flux_list.append(normal_speed * magnetic[other] - normal_field * velocity[other])
    flux_list.append((energy + total_pressure) * normal_speed - normal_field * velocity_dot)
    wave_speed = jnp.abs(normal_speed) + jnp.sqrt((HEAT_RATIO * pressure + field_sq) / density)
    return (jnp.stack(flux_list), wave_speed)


def interface_change(padded_line, direction):
    phys_flux, wave_speed = direction_flux(padded_line, direction)
    array_dim = direction + 1
    cell_count = padded_line.shape[array_dim]
    low_cells = lax.slice_in_dim(padded_line, 0, cell_count - 1, axis=array_dim)
    high_cells = lax.slice_in_dim(padded_line, 1, cell_count, axis=array_dim)
    low_flux = lax.slice_in_dim(phys_flux, 0, cell_count - 1, axis=array_dim)
    high_flux = lax.slice_in_dim(phys_flux, 1, cell_count, axis=array_dim)
    low_speed = lax.slice_in_dim(wave_speed, 0, cell_count - 1, axis=direction)
    high_speed = lax.slice_in_dim(wave_speed, 1, cell_count, axis=direction)
    fastest = jnp.maximum(low_speed, high_speed)
    face_flux = 0.5 * (low_flux + high_flux) - 0.5 * fastest[None] * (high_cells - low_cells)
    upper_face = lax.slice_in_dim(face_flux, 1, cell_count - 1, axis=array_dim)
    lower_face = lax.slice_in_dim(face_flux, 0, cell_count - 2, axis=array_dim)
    return upper_face - lower_face


def advance(line_set, inner_cells, step_ratio):
    change = interface_change(line_set[0], 0) + interface_change(line_set[1], 1)
    change = change + interface_change(line_set[2], 2)
    return inner_cells - step_ratio * change


def route_kernel(send_ref, out_ref, landed, send_sem, recv_sem):
    domain = lax.axis_index("dom")
    here = lax.axis_index("yz")
    count = send_ref.shape[0]
    barrier = pltpu.get_barrier_semaphore()
    for partner in range(count):
        pl.semaphore_signal(
            barrier, inc=1, device_id={"dom": 1 - domain, "yz": partner}, device_id_type=MESH
        )
    pl.semaphore_wait(barrier, count)

    @pl.when(domain == 0)
    def _():
        copies = []
        for owner in range(count):
            copy = pltpu.make_async_remote_copy(
                src_ref=send_ref.at[owner],
                dst_ref=landed.at[here],
                send_sem=send_sem.at[owner],
                recv_sem=recv_sem.at[here],
                device_id={"dom": 1, "yz": owner},
                device_id_type=MESH,
            )
            copy.start()
            copies.append(copy)
        for copy in copies:
            copy.wait_send()
        out_ref[...] = jnp.zeros_like(out_ref)

    @pl.when(domain == 1)
    def _():
        for sender in range(count):
            pltpu.make_async_remote_copy(
                src_ref=send_ref.at[sender],
                dst_ref=landed.at[sender],
                send_sem=send_sem.at[sender],
                recv_sem=recv_sem.at[sender],
                device_id={"dom": 0, "yz": sender},
                device_id_type=MESH,
            ).wait_recv()
        out_ref[...] = landed[...]


def route_blocks(send_cells):
    count = send_cells.shape[0]
    return pl.pallas_call(
        route_kernel,
        out_shape=jax.ShapeDtypeStruct(send_cells.shape, send_cells.dtype),
        in_specs=[pl.BlockSpec(memory_space=pltpu.VMEM)],
        out_specs=pl.BlockSpec(memory_space=pltpu.VMEM),
        scratch_shapes=[
            pltpu.VMEM(send_cells.shape, send_cells.dtype),
            pltpu.SemaphoreType.DMA((count,)),
            pltpu.SemaphoreType.DMA((count,)),
        ],
        compiler_params=pltpu.CompilerParams(collective_id=0, has_side_effects=True),
    )(send_cells)


def ghost_pair(cells, axis, dim, wrap, fix_low, fix_high):
    count = lax.axis_size(axis)
    size = cells.shape[dim]
    head = lax.slice_in_dim(cells, 0, 1, axis=dim)
    tail = lax.slice_in_dim(cells, size - 1, size, axis=dim)
    up = [(i, i + 1) for i in range(count - 1)]
    down = [(i + 1, i) for i in range(count - 1)]
    if wrap:
        up.append((count - 1, 0))
        down.append((0, count - 1))
    from_low = lax.ppermute(tail.astype(jnp.bfloat16), axis, up).astype(cells.dtype)
    from_high = lax.ppermute(head.astype(jnp.bfloat16), axis, down).astype(cells.dtype)
    low = jnp.where(fix_low, head, from_low)
    high = jnp.where(fix_high, tail, from_high)
    return jnp.concatenate([low, cells, high], axis=dim)


def local(field_state, shell_owner, block_sources, block_targets, interp_weights):
    grid_cells = field_state[0]
    ncomp, len_x, len_y, len_z = grid_cells.shape
    domain = lax.axis_index("dom")
    column = lax.axis_index("gx")
    yz_index = lax.axis_index("yz")
    gx_count = lax.axis_size("gx")
    yz_count = lax.axis_size("yz")
    per_y = len_y // BLK
    per_z = len_z // BLK
    volume = BLK * BLK * BLK
    shell_cells = grid_cells[:, :, :, len_z - SR * BLK :]
    shell_cells = shell_cells.reshape(ncomp, len_x // BLK, BLK, per_y, BLK, SR, BLK)
    shell_cells = (
        shell_cells.transpose(1, 3, 5, 0, 2, 4, 6).reshape(-1, ncomp * volume).astype(jnp.bfloat16)
    )
    count_here = shell_cells.shape[0]
    owner_table = shell_owner[0]
    own_owner = lax.dynamic_index_in_dim(owner_table, yz_index, 0, keepdims=False)
    index_here = jnp.arange(count_here, dtype=jnp.int32)
    local_same = own_owner[None, :] == own_owner[:, None]
    rank_local = jnp.sum(
        (local_same & (index_here[None, :] < index_here[:, None])).astype(jnp.int32), axis=1
    )
    slot_of = own_owner * CAP + rank_local
    slot_count = yz_count * CAP
    select = jnp.arange(slot_count, dtype=jnp.int32)[:, None] == slot_of[None, :]
    send_cells = jnp.dot(
        select.astype(jnp.bfloat16), shell_cells, preferred_element_type=jnp.float32
    )
    send_cells = send_cells.astype(jnp.bfloat16).reshape(yz_count, CAP * ncomp, volume)
    got_cells = route_blocks(send_cells).reshape(slot_count, ncomp * volume)
    mine = (owner_table == yz_index).astype(jnp.int32)
    per_sender = jnp.sum(mine, axis=1)
    before = jnp.cumsum(per_sender) - per_sender
    rank_slot = jnp.arange(CAP, dtype=jnp.int32)
    got_tags = jnp.where(
        rank_slot[None, :] < per_sender[:, None], before[:, None] + rank_slot[None, :], -1
    ).reshape(slot_count)
    wanted = block_sources[0, 0].reshape(-1)
    match_table = (wanted[:, None] == got_tags[None, :]) & (wanted[:, None] >= 0)
    picked = jnp.dot(
        match_table.astype(jnp.bfloat16), got_cells, preferred_element_type=jnp.float32
    )
    slots_here = block_targets.shape[2]
    picked = picked.astype(jnp.bfloat16).reshape(slots_here, -1, ncomp, volume)
    interp_blocks = jnp.einsum(
        "jkcs,jkst->jct", picked, interp_weights[0, 0], preferred_element_type=jnp.float32
    )

    rows = lax.broadcasted_iota(jnp.int32, (len_x, len_y, len_z), 0) // BLK
    cols = lax.broadcasted_iota(jnp.int32, (len_x, len_y, len_z), 1) // BLK
    lanes = lax.broadcasted_iota(jnp.int32, (len_x, len_y, len_z), 2)
    spread_of = lax.broadcasted_iota(jnp.int32, (BLK, len_z), 1) % BLK
    offset_of = lax.broadcasted_iota(jnp.int32, (BLK, len_z), 0)
    spread = (spread_of == offset_of).astype(jnp.float32)
    stacked = interp_blocks.reshape(slots_here * ncomp * BLK * BLK, BLK)
    stacked = jnp.dot(stacked, spread, precision=lax.Precision.HIGHEST)
    stacked = stacked.reshape(slots_here, ncomp, BLK, BLK, len_z)
    targets = jnp.where(domain == 1, block_targets[0, 0], -1)
    spots = jnp.maximum(targets, 0)
    hit = (
        (rows[None] == (spots // (per_y * per_z))[:, None, None, None])
        & (cols[None] == (spots // per_z % per_y)[:, None, None, None])
        & (lanes[None] // BLK == (spots % per_z)[:, None, None, None])
        & (targets >= 0)[:, None, None, None]
    )
    for slot_number in range(slots_here):
        placed = jnp.tile(stacked[slot_number], (1, len_x // BLK, len_y // BLK, 1))
        grid_cells = jnp.where(hit[slot_number][None], placed, grid_cells)

    helio_side = domain == 1
    low_x = helio_side & (column == 0)
    high_x = helio_side & (column == gx_count - 1)
    low_y = yz_index == 0
    high_y = yz_index == yz_count - 1
    line_x = ghost_pair(grid_cells, "gx", 1, True, low_x, high_x)
    line_y = ghost_pair(grid_cells, "yz", 2, False, low_y, high_y)
    line_z = jnp.pad(grid_cells, ((0, 0), (0, 0), (0, 0), (1, 1)), mode="edge")
    step_ratio = jnp.where(domain == 0, CORONA_RATIO, HELIO_RATIO).astype(jnp.float32)
    updated = advance((line_x, line_y, line_z), grid_cells, step_ratio)
    return updated[None]


def solution(mesh):
    placed = (
        P("dom", None, "gx", "yz", None),
        P("gx", None, None),
        P("gx", "yz", None, None),
        P("gx", "yz", None),
        P("gx", "yz", None, None, None, None),
    )
    return jax.shard_map(
        local,
        mesh=mesh,
        in_specs=placed,
        out_specs=P("dom", None, "gx", "yz", None),
        check_vma=False,
    )
```
